512 devices in a mesh: magnet: 16 (over y, x), slab: 32 (over z, core).
Axes of the slice: x: 4, y: 4, z: 16, core: 2. Of those that a mesh axis runs over, the one named last changes fastest.
Arguments:
- foil_warmth: float32 [4096, 512], P(('magnet', 'slab')), may hold values from 0.5 to 4
- terminal_voltage_input: float32 [4096, 512], P(('magnet', 'slab')), may hold values from -6 to 6
- foil_segment_pattern: int32 [4096, 512], P(('magnet', 'slab')), may hold values from 0 to 2
- underlying_block_map: int32 [4096, 512], P('magnet'), may hold values from 3840 to 4095
- prior_block_warmth: float32 [32, 4096, 128], P('slab', 'magnet'), may hold values from 0 to 2
- substance_kind: int32 [32, 4096, 128], P('slab', 'magnet'), may hold values from 0 to 3
Outputs:
- sheet_potential: float32 [4096, 512], P(('magnet', 'slab'))
- brick_heated: float32 [32, 4096, 128], P('slab', 'magnet')
The draws below stay inside these ranges and needn't reach their ends.
Inputs may be any that keep to these rules, and one draw needn't show every extreme that they name: `foil_segment_pattern`: 0 marks plain heater steel, 1 copper-plated stations, 2 current-lead contacts. `underlying_block_map`: the value is radial layer times 128 plus azimuthal cell. `substance_kind`: 0 insulation, 1 Nb3Sn coil, 2 copper wedge, 3 steel collar.
All inputs are finite; a program needn't handle non-finite values.
Results may differ from the reference program's by a relative error of at most 0.0001.
Values sent between devices are 32-bit elements; how exact they have to be, the bound alone decides.
No kernel may reach another device: no remote copies, remote signals or barrier semaphores. Data moves between devices by JAX's collectives and lax.ppermute only.
A program may use at most 64 MiB of HBM per device.

```python
import math
import jax
import jax.numpy as jnp

SW = 512
BRD = 1
SPOKE_COUNT = 128
ITERS = 3
SUBSTEPS = 4
AXIAL_COUNT = 4096
SHELL_COUNT = 32


def with_ends(array, key, smallest, high):
    dims = array.shape
    index_at = [jax.random.randint(jax.random.fold_in(key, axis), (), 0, dims[axis]) for axis in range(len(dims))]
    array = array.at[tuple(index_at)].set(smallest)
    longest = dims.index(max(dims))
    index_at[longest] = (index_at[longest] + 1) % dims[longest]
    return array.at[tuple(index_at)].set(high)


def shard_levels(rng, shape, split, least, high):
    loudness = 1.0
    for axis_at, shards_of in split:
        draws = jax.random.uniform(jax.random.fold_in(jax.random.fold_in(rng, 6), axis_at), (shards_of,), jnp.float32, least / len(split), high / len(split))
        loudness = loudness * jnp.repeat(jnp.exp(draws), shape[axis_at] // shards_of).reshape((-1,) + (1,) * (len(shape) - 1 - axis_at))
    return loudness


def noise(key, extent, width, most, pieces=(), held_as=jnp.bfloat16):
    values = jax.random.normal(key, extent, jnp.float32) * width
    if len(pieces) > 0:
        values = shard_levels(key, extent, pieces, -0.22, 0.18) * values
    return jnp.clip(values, min=-most, max=most).astype(held_as)


def setup_inputs(seed: int = 0) -> dict:
    streams_of = jax.random.split(jax.random.key(seed), 7)
    return {
        "foil_warmth": jnp.clip(jnp.exp(math.log(4.0) - 2.0794415 * jax.random.uniform(streams_of[0], (AXIAL_COUNT, SW), jnp.float32) ** shard_levels(streams_of[0], (AXIAL_COUNT, SW), ((0, 512),), -0.2, 0.2)), 0.5, 4.0),
        "terminal_voltage_input": noise(streams_of[1], (AXIAL_COUNT, SW), 1.0, 6.0, ((0, 512),), jnp.float32),
        "foil_segment_pattern": with_ends(jax.random.randint(streams_of[2], (AXIAL_COUNT, SW), 0, 3), jax.random.fold_in(streams_of[2], 1), 0, 2).astype(jnp.int32),
        "underlying_block_map": with_ends(jax.random.randint(streams_of[3], (AXIAL_COUNT, SW), (SHELL_COUNT - 2 * BRD) * SPOKE_COUNT, SHELL_COUNT * SPOKE_COUNT), jax.random.fold_in(streams_of[3], 1), (SHELL_COUNT - 2 * BRD) * SPOKE_COUNT, (SHELL_COUNT * SPOKE_COUNT) - 1).astype(jnp.int32),
        "prior_block_warmth": jnp.clip(2.0 * jax.random.uniform(streams_of[4], (SHELL_COUNT, AXIAL_COUNT, SPOKE_COUNT), jnp.float32) ** shard_levels(streams_of[4], (SHELL_COUNT, AXIAL_COUNT, SPOKE_COUNT), ((0, 32), (1, 16)), -0.2, 0.2), 0.0, 2.0),
        "substance_kind": with_ends(jax.random.randint(streams_of[5], (SHELL_COUNT, AXIAL_COUNT, SPOKE_COUNT), 0, 4), jax.random.fold_in(streams_of[5], 1), 0, 3).astype(jnp.int32),
    }


leak_diag = 0.25
contact_gain = 4.0
copper_factor = 3.0
sheet_slope = 0.5
heat_factor = 1.5
time_step = 0.03
conduct_table = (0.3, 1.0, 2.0, 0.6)
capacity_table = (1.0, 1.5, 2.0, 1.2)
diffusivity_derivative = 0.4


def lookup_table(substance_kind, table):
    running_total = jnp.zeros(substance_kind.shape, jnp.float32)
    for material_index in range(4):
        running_total = running_total + jnp.where(substance_kind == material_index, table[material_index], 0.0).astype(jnp.float32)
    return running_total


def face_coeffs(sigma_padded):
    centre = sigma_padded[1:-1, 1:-1]
    return (0.5 * (centre + sigma_padded[:-2, 1:-1]), 0.5 * (centre + sigma_padded[2:, 1:-1]),
            0.5 * (centre + sigma_padded[1:-1, :-2]), 0.5 * (centre + sigma_padded[1:-1, 2:]))


def neighbour_values(padded):
    return (padded[:-2, 1:-1], padded[2:, 1:-1], padded[1:-1, :-2], padded[1:-1, 2:])


def apply_sheet(values_grid, coeffs, diagonal):
    neighbours = neighbour_values(jnp.pad(values_grid, 1))
    result = diagonal * values_grid
    for coeff_face, neighbour in zip(coeffs, neighbours):
        result = result - coeff_face * neighbour
    return result


def diffusivity_update(temp_pad, cond_pad, resistive_power_density, specific_storage_grid):
    centre_t = temp_pad[1:-1, 1:-1]
    centre_k = cond_pad[1:-1, 1:-1]
    flux_total = jnp.zeros(centre_t.shape, jnp.float32)
    pairs = ((temp_pad[:-2, 1:-1], cond_pad[:-2, 1:-1]), (temp_pad[2:, 1:-1], cond_pad[2:, 1:-1]),
             (temp_pad[1:-1, :-2], cond_pad[1:-1, :-2]), (temp_pad[1:-1, 2:], cond_pad[1:-1, 2:]))
    for other_t, other_k in pairs:
        flux_total = flux_total + 0.5 * (centre_k + other_k) * (other_t - centre_t)
    for offset in (1, -1):
        other_t = jnp.roll(centre_t, offset, axis=2)
        other_k = jnp.roll(centre_k, offset, axis=2)
        flux_total = flux_total + 0.5 * (centre_k + other_k) * (other_t - centre_t)
    return centre_t + time_step * (flux_total + resistive_power_density) / specific_storage_grid


def reference(foil_warmth, terminal_voltage_input, foil_segment_pattern, underlying_block_map, prior_block_warmth, substance_kind):
    copper = jnp.where(foil_segment_pattern == 1, copper_factor, 1.0).astype(jnp.float32)
    sigma_cells = copper / (1.0 + sheet_slope * foil_warmth)
    coeffs = face_coeffs(jnp.pad(sigma_cells, 1))
    contact = jnp.where(foil_segment_pattern == 2, contact_gain, 0.0).astype(jnp.float32)
    diagonal = leak_diag + contact + coeffs[0] + coeffs[1] + coeffs[2] + coeffs[3]
    rhs_field = contact * terminal_voltage_input
    voltage_solution = jnp.zeros_like(rhs_field)
    residual = rhs_field
    direction = rhs_field
    norm_now = jnp.sum(residual * residual)
    for iteration in range(ITERS):
        image_field = apply_sheet(direction, coeffs, diagonal)
        step_length = norm_now / jnp.sum(direction * image_field)
        voltage_solution = voltage_solution + step_length * direction
        residual = residual - step_length * image_field
        if iteration + 1 < ITERS:
            norm_next = jnp.sum(residual * residual)
            direction = residual + (norm_next / norm_now) * direction
            norm_now = norm_next
    neighbours = neighbour_values(jnp.pad(voltage_solution, 1))
    joule = jnp.zeros_like(voltage_solution)
    for coeff_face, neighbour in zip(coeffs, neighbours):
        joule = joule + coeff_face * (voltage_solution - neighbour) ** 2
    joule = heat_factor * joule
    row_index = jnp.broadcast_to(jnp.arange(AXIAL_COUNT, dtype=jnp.int32)[:, None], underlying_block_map.shape)
    resistive_power_density = jnp.zeros((SHELL_COUNT, AXIAL_COUNT, SPOKE_COUNT), jnp.float32).at[underlying_block_map // SPOKE_COUNT, row_index, underlying_block_map % SPOKE_COUNT].add(joule)
    reference_diffusivity = lookup_table(substance_kind, conduct_table)
    specific_storage_grid = lookup_table(substance_kind, capacity_table)
    warmth_distribution = prior_block_warmth
    for substep in range(SUBSTEPS):
        diffusivity_coefficient = reference_diffusivity * (1.0 + diffusivity_derivative * warmth_distribution)
        margin_count = ((1, 1), (1, 1), (0, 0))
        warmth_distribution = diffusivity_update(jnp.pad(warmth_distribution, margin_count), jnp.pad(diffusivity_coefficient, margin_count), resistive_power_density, specific_storage_grid)
    return voltage_solution, warmth_distribution
```

```python
import functools

import jax
import jax.numpy as jnp
from jax import lax
from jax.experimental import pallas as pl
from jax.experimental.pallas import tpu as pltpu
from jax.sharding import PartitionSpec as P

SUBSTEPS = 4
HALO = SUBSTEPS
ROWS = 8

leak_diag = 0.25
contact_gain = 4.0
copper_factor = 3.0
sheet_slope = 0.5
heat_factor = 1.5
time_step = 0.03
conduct_table = (0.3, 1.0, 2.0, 0.6)
capacity_table = (1.0, 1.5, 2.0, 1.2)
diffusivity_derivative = 0.4

SHIFT = 9.85
SCALE = 9.6
BOTH = ("magnet", "slab")


def place():
    size = lax.axis_size("slab")
    return lax.axis_index("magnet") * size + lax.axis_index("slab"), lax.axis_size("magnet") * size


def above(v):
    return pltpu.roll(v, 1, 0)


def below(v):
    return pltpu.roll(v, v.shape[0] - 1, 0)


def left(v):
    return pltpu.roll(v, 1, 1)


def right(v):
    return pltpu.roll(v, v.shape[1] - 1, 1)


def rows_inside(shape, margin):
    index, count = place()
    row = lax.broadcasted_iota(jnp.int32, shape, 0)
    low = jnp.where(index > 0, 0, margin)
    high = jnp.where(index < count - 1, shape[0], shape[0] - margin)
    return jnp.where((row >= low) & (row < high), 1.0, 0.0).astype(jnp.float32)


def basis_kernel(own, before, after, moments, w0_out, w1_out, w2_out, down_out, right_out, left_out, cells_out):
    def window(i):
        part = slice(ROWS * i, ROWS * (i + 1))
        return jnp.concatenate([before[part, :], own[part, :], after[part, :]], axis=0)

    warmth, voltage, pattern = window(0), window(1), window(2)
    cells_out[...] = window(3)
    shape = warmth.shape
    inside = rows_inside(shape, ROWS)
    col = lax.broadcasted_iota(jnp.int32, shape, 1)
    last = col == shape[1] - 1
    sigma = inside * jnp.where(pattern == 1.0, copper_factor, 1.0) / (1.0 + sheet_slope * warmth)
    contact = jnp.where(pattern == 2.0, contact_gain, 0.0)
    c_down = 0.5 * (sigma + below(sigma))
    c_right = 0.5 * (sigma + jnp.where(last, 0.0, right(sigma)))
    c_left = jnp.where(col == 0, 0.5 * sigma, left(c_right))
    diagonal = leak_diag + contact + above(c_down) + c_down + c_left + c_right
    diagonal = (diagonal - SHIFT) * (1.0 / SCALE)
    o_down = c_down * inside * below(inside) * (1.0 / SCALE)
    o_up = above(o_down)
    o_right = jnp.where(last, 0.0, c_right) * (1.0 / SCALE)
    o_left = left(o_right)

    def apply(v):
        return diagonal * v - (o_up * above(v) + o_down * below(v)) - (o_left * left(v) + o_right * right(v))

    w0 = contact * voltage
    w1 = apply(w0)
    w2 = 2.0 * apply(w1) - w0
    w3 = apply(w2)
    w0_out[...] = w0
    w1_out[...] = w1
    w2_out[...] = w2
    down_out[...] = c_down
    right_out[...] = c_right
    left_out[...] = c_left
    a, b, c, d = (v[ROWS : 2 * ROWS] for v in (w0, w1, w2, w3))
    lane = lax.broadcasted_iota(jnp.int32, (1, 128), 1)
    line = jnp.zeros((1, 128), jnp.float32)
    for i, (u, v) in enumerate(((a, a), (a, b), (a, c), (b, b), (b, c), (c, c), (c, d))):
        line = jnp.where(lane == i, jnp.sum(u * v, keepdims=True), line)
    moments[...] = jnp.broadcast_to(line, moments.shape)


def sum_kernel(lines, out):
    out[...] = jnp.broadcast_to(jnp.sum(lines[...], axis=0, keepdims=True), out.shape)


def solve_small(lines):
    total = jnp.sum(lines, axis=0, keepdims=True)
    g00, g01, g02, g11, g12, g22, k22 = (total[:, i : i + 1] for i in range(7))
    gram = ((g00, g01, g02), (g01, g11, g12), (g02, g12, g22))
    k11, k12 = 0.5 * (g12 + g01), 0.5 * (g22 + g02)
    shifted = ((g01, g11, g12), (g11, k11, k12), (g12, k12, k22))
    energy = [[SCALE * shifted[i][j] + SHIFT * gram[i][j] for j in range(3)] for i in range(3)]

    def form(m, v):
        return sum(v[i] * (v[i] * m[i][i] + 2.0 * sum((v[j] * m[i][j] for j in range(i + 1, len(v))), 0.0)) for i in range(len(v)))

    def ratio(num, den, low, high):
        return jnp.clip(num / jnp.maximum(den, 1e-37), low, high)

    alpha0 = g00 / energy[0][0]
    r = [1.0 - alpha0 * SHIFT, -alpha0 * SCALE]
    rr1 = jnp.maximum(form(gram, r), 0.0)
    beta = ratio(rr1, g00, 0.0, 1e4)
    p = [r[0] + beta, r[1]]
    alpha1 = ratio(rr1, form(energy, p), 0.05, 4.1)
    half = 0.5 * SCALE * p[1]
    image = [half + SHIFT * p[0], SCALE * p[0] + SHIFT * p[1], half]
    x = [alpha0 + alpha1 * p[0], alpha1 * p[1]]
    r = [r[0] - alpha1 * image[0], r[1] - alpha1 * image[1], -alpha1 * image[2]]
    rr2 = jnp.maximum(form(gram, r), 0.0)
    beta = ratio(rr2, rr1, 0.0, 1e4)
    p = [r[0] + beta * p[0], r[1] + beta * p[1], r[2]]
    alpha2 = ratio(rr2, form(energy, p), 0.05, 4.1)
    return x[0] + alpha2 * p[0], x[1] + alpha2 * p[1], alpha2 * p[2]


def heat_kernel(
    layers, lines, w0, w1, w2, c_down, c_right, c_left, cells, own, before, after, potential, heated, warm, base, store, heat
):
    span = ROWS + 2 * HALO
    f0, f1, f2 = solve_small(lines[...])
    shape = w0.shape
    inside = rows_inside(shape, ROWS)
    x = (f0 * w0[...] + f1 * w1[...] + f2 * w2[...]) * inside
    potential[...] = x[ROWS : 2 * ROWS]
    col = lax.broadcasted_iota(jnp.int32, shape, 1)
    step = x - below(x)
    q_down = c_down[...] * (step * step)
    step = x - jnp.where(col == shape[1] - 1, 0.0, right(x))
    q_right = c_right[...] * (step * step)
    q_left = jnp.where(col == 0, c_left[...] * (x * x), left(q_right))
    joule = heat_factor * ((q_down + above(q_down)) + (q_right + q_left))
    joule = joule[ROWS - HALO : ROWS - HALO + span]
    cell = cells[ROWS - HALO : ROWS - HALO + span, :].astype(jnp.int32)
    spokes = heated.shape[-1]
    azimuth = cell & (spokes - 1)
    outer = cell >= (layers - 1) * spokes
    pieces = []
    for part in (jnp.where(outer, 0.0, joule), jnp.where(outer, joule, 0.0)):
        for _ in range(3):
            piece = part.astype(jnp.bfloat16)
            pieces.append(piece.astype(jnp.float32))
            part = part - piece.astype(jnp.float32)
    stacked = jnp.concatenate(pieces, axis=0)
    row_of = lax.rem(lax.broadcasted_iota(jnp.int32, stacked.shape, 0), span)
    spoke = lax.broadcasted_iota(jnp.int32, (spokes, shape[1]), 0)
    total = jnp.zeros((stacked.shape[0], spokes), jnp.float32)
    for row in range(1, span - 1):
        pick = jnp.where(azimuth[row : row + 1, :] == spoke, 1.0, 0.0).astype(jnp.bfloat16)
        some = jnp.where(row_of == row, stacked, 0.0).astype(jnp.bfloat16)
        total = total + lax.dot_general(some, pick, (((1,), (1,)), ((), ())), preferred_element_type=jnp.float32)
    heat[0] = total[0:span] + (total[span : 2 * span] + total[2 * span : 3 * span])
    heat[1] = total[3 * span : 4 * span] + (total[4 * span : 5 * span] + total[5 * span : 6 * span])

    cut = (span, spokes)
    there = rows_inside(cut, HALO)
    for layer in range(layers):

        def assemble(i):
            part = slice(ROWS * i, ROWS * (i + 1))
            return jnp.concatenate(
                [before[layer, part][ROWS - HALO :], own[layer, part], after[layer, part][:HALO]], axis=0
            )

        kind = assemble(1)
        conduct = jnp.where(kind == 0.0, conduct_table[0], jnp.where(kind == 1.0, conduct_table[1], jnp.where(kind == 2.0, conduct_table[2], conduct_table[3])))
        gain = [0.5 * time_step / c for c in capacity_table]
        gains = jnp.where(kind == 0.0, gain[0], jnp.where(kind == 1.0, gain[1], jnp.where(kind == 2.0, gain[2], gain[3])))
        warm[0, layer] = assemble(0) * there
        base[layer] = conduct * there
        store[layer] = gains * there

    for substep in range(SUBSTEPS):
        now, then = substep % 2, 1 - substep % 2

        def conductivity(layer):
            t = warm[now, layer]
            return t, base[layer] * (1.0 + diffusivity_derivative * t)

        t, k = conductivity(0)
        inner = k * t
        for layer in range(layers):
            if layer + 1 < layers:
                t_next, k_next = conductivity(layer + 1)
                outer_face = (k + k_next) * (t_next - t)
            else:
                t_next, k_next = None, None
                outer_face = -(k * t)
            flux = outer_face - inner
            face = (k + below(k)) * (below(t) - t)
            flux = flux + (face - above(face))
            face = (k + right(k)) * (right(t) - t)
            flux = flux + (face - left(face))
            if layer >= layers - 2:
                flux = flux + 2.0 * heat[layer - (layers - 2)]
            fresh = t + store[layer] * flux
            if substep + 1 < SUBSTEPS:
                warm[then, layer] = fresh
            else:
                heated[layer] = fresh[HALO : HALO + ROWS]
            t, k, inner = t_next, k_next, outer_face


def vmem(count):
    return [pl.BlockSpec(memory_space=pltpu.VMEM)] * count


def local(foil_warmth, terminal_voltage_input, foil_segment_pattern, underlying_block_map, prior_block_warmth, substance_kind):
    f32 = jnp.float32
    magnets, layers = lax.axis_size("magnet"), lax.axis_size("slab")
    count = magnets * layers
    width, spokes = foil_warmth.shape[1], prior_block_warmth.shape[2]
    onward = [(i, i + 1) for i in range(count - 1)]
    backward = [(i + 1, i) for i in range(count - 1)]

    def around(block):
        return lax.ppermute(block, BOTH, onward), lax.ppermute(block, BOTH, backward)

    bricks = jnp.concatenate(
        [
            prior_block_warmth.reshape(layers, ROWS, spokes),
            substance_kind.astype(f32).reshape(layers, ROWS, spokes),
        ],
        axis=1,
    )
    bricks = lax.all_to_all(bricks, "slab", 0, 0)

    cells = lax.dynamic_slice_in_dim(underlying_block_map, lax.axis_index("slab") * ROWS, ROWS, axis=0)
    sheet = jnp.concatenate(
        [foil_warmth, terminal_voltage_input, foil_segment_pattern.astype(f32), cells.astype(f32)], axis=0
    )
    field = jax.ShapeDtypeStruct((3 * ROWS, width), f32)
    moments, *fields = pl.pallas_call(
        basis_kernel,
        out_shape=(jax.ShapeDtypeStruct((layers, 128), f32),) + (field,) * 7,
        in_specs=vmem(3),
        out_specs=vmem(8),
        name="basis",
    )(sheet, *around(sheet))

    lines = lax.all_to_all(moments.reshape(layers, 1, 128), "slab", 0, 0).reshape(layers, 128)
    lines = pl.pallas_call(
        sum_kernel,
        out_shape=jax.ShapeDtypeStruct((magnets, 128), f32),
        in_specs=vmem(1),
        out_specs=vmem(1)[0],
        name="total",
    )(lines)
    lines = lax.all_to_all(lines.reshape(magnets, 1, 128), "magnet", 0, 0).reshape(magnets, 128)

    span = ROWS + 2 * HALO
    potential, heated = pl.pallas_call(
        functools.partial(heat_kernel, layers),
        out_shape=(jax.ShapeDtypeStruct((ROWS, width), f32), jax.ShapeDtypeStruct((layers, ROWS, spokes), f32)),
        in_specs=vmem(11),
        out_specs=vmem(2),
        scratch_shapes=[
            pltpu.VMEM((2, layers, span, spokes), f32),
            pltpu.VMEM((layers, span, spokes), f32),
            pltpu.VMEM((layers, span, spokes), f32),
            pltpu.VMEM((2, span, spokes), f32),
        ],
        name="heat",
    )(lines, *fields, bricks, *around(bricks))
    heated = lax.all_to_all(heated, "slab", 0, 0)
    return potential, heated.reshape(prior_block_warmth.shape)


def solution(mesh):
    placed = (
        P(("magnet", "slab"), None),
        P(("magnet", "slab"), None),
        P(("magnet", "slab"), None),
        P("magnet", None),
        P("slab", "magnet", None),
        P("slab", "magnet", None),
    )
    return jax.shard_map(
        local,
        mesh=mesh,
        in_specs=placed,
        out_specs=(P(("magnet", "slab"), None), P("slab", "magnet", None)),
        check_vma=False,
    )
```

```python
import functools

import jax
import jax.numpy as jnp
from jax import lax
from jax.experimental import pallas as pl
from jax.experimental.pallas import tpu as pltpu
from jax.sharding import PartitionSpec as P

SUBSTEPS = 4
HALO = SUBSTEPS
ROWS = 8

leak_diag = 0.25
contact_gain = 4.0
copper_factor = 3.0
sheet_slope = 0.5
heat_factor = 1.5
time_step = 0.03
conduct_table = (0.3, 1.0, 2.0, 0.6)
capacity_table = (1.0, 1.5, 2.0, 1.2)
diffusivity_derivative = 0.4

SHIFT = 9.85
SCALE = 9.6
BOTH = ("magnet", "slab")


def place():
    size = lax.axis_size("slab")
    return lax.axis_index("magnet") * size + lax.axis_index("slab"), lax.axis_size("magnet") * size


def above(v):
    return pltpu.roll(v, 1, 0)


def below(v):
    return pltpu.roll(v, v.shape[0] - 1, 0)


def left(v):
    return pltpu.roll(v, 1, 1)


def right(v):
    return pltpu.roll(v, v.shape[1] - 1, 1)


def rows_inside(shape, margin):
    index, count = place()
    row = lax.broadcasted_iota(jnp.int32, shape, 0)
    low = jnp.where(index > 0, 0, margin)
    high = jnp.where(index < count - 1, shape[0], shape[0] - margin)
    return jnp.where((row >= low) & (row < high), 1.0, 0.0).astype(jnp.float32)


def basis_kernel(own, before, after, warmth_in, kind_in, packed, w0_out, w1_out, w2_out, down_out, right_out, left_out, cells_out):
    def window(i):
        part = slice(ROWS * i, ROWS * (i + 1))
        return jnp.concatenate([before[part, :], own[part, :], after[part, :]], axis=0)

    warmth, voltage, pattern = window(0), window(1), window(2)
    cells_out[...] = window(3)
    shape = warmth.shape
    inside = rows_inside(shape, ROWS)
    col = lax.broadcasted_iota(jnp.int32, shape, 1)
    last = col == shape[1] - 1
    sigma = inside * jnp.where(pattern == 1.0, copper_factor, 1.0) / (1.0 + sheet_slope * warmth)
    contact = jnp.where(pattern == 2.0, contact_gain, 0.0)
    c_down = 0.5 * (sigma + below(sigma))
    c_right = 0.5 * (sigma + jnp.where(last, 0.0, right(sigma)))
    c_left = jnp.where(col == 0, 0.5 * sigma, left(c_right))
    diagonal = leak_diag + contact + above(c_down) + c_down + c_left + c_right
    diagonal = (diagonal - SHIFT) * (1.0 / SCALE)
    o_down = c_down * inside * below(inside) * (1.0 / SCALE)
    o_up = above(o_down)
    o_right = jnp.where(last, 0.0, c_right) * (1.0 / SCALE)
    o_left = left(o_right)

    def apply(v):
        return diagonal * v - (o_up * above(v) + o_down * below(v)) - (o_left * left(v) + o_right * right(v))

    w0 = contact * voltage
    w1 = apply(w0)
    w2 = 2.0 * apply(w1) - w0
    w3 = apply(w2)
    w0_out[...] = w0
    w1_out[...] = w1
    w2_out[...] = w2
    down_out[...] = c_down
    right_out[...] = c_right
    left_out[...] = c_left
    a, b, c, d = (v[ROWS : 2 * ROWS] for v in (w0, w1, w2, w3))
    lane = lax.broadcasted_iota(jnp.int32, (1, 128), 1)
    line = jnp.zeros((1, 128), jnp.float32)
    for i, (u, v) in enumerate(((a, a), (a, b), (a, c), (b, b), (b, c), (c, c), (c, d))):
        line = jnp.where(lane == i, jnp.sum(u * v, keepdims=True), line)
    block = 2 * ROWS + 1
    for slab in range(packed.shape[0] // block):
        part = slice(ROWS * slab, ROWS * (slab + 1))
        at = block * slab
        packed[at : at + ROWS] = warmth_in[part]
        packed[at + ROWS : at + 2 * ROWS] = kind_in[part].astype(jnp.float32)
        packed[at + 2 * ROWS : at + block] = line


def solve_small(lines):
    total = jnp.sum(lines, axis=0, keepdims=True)
    g00, g01, g02, g11, g12, g22, k22 = (total[:, i : i + 1] for i in range(7))
    gram = ((g00, g01, g02), (g01, g11, g12), (g02, g12, g22))
    k11, k12 = 0.5 * (g12 + g01), 0.5 * (g22 + g02)
    shifted = ((g01, g11, g12), (g11, k11, k12), (g12, k12, k22))
    energy = [[SCALE * shifted[i][j] + SHIFT * gram[i][j] for j in range(3)] for i in range(3)]

    def form(m, v):
        return sum(v[i] * (v[i] * m[i][i] + 2.0 * sum((v[j] * m[i][j] for j in range(i + 1, len(v))), 0.0)) for i in range(len(v)))

    def ratio(num, den, low, high):
        return jnp.clip(num / jnp.maximum(den, 1e-37), low, high)

    alpha0 = g00 / energy[0][0]
    r = [1.0 - alpha0 * SHIFT, -alpha0 * SCALE]
    rr1 = jnp.maximum(form(gram, r), 0.0)
    beta = ratio(rr1, g00, 0.0, 1e4)
    p = [r[0] + beta, r[1]]
    alpha1 = ratio(rr1, form(energy, p), 0.05, 4.1)
    half = 0.5 * SCALE * p[1]
    image = [half + SHIFT * p[0], SCALE * p[0] + SHIFT * p[1], half]
    x = [alpha0 + alpha1 * p[0], alpha1 * p[1]]
    r = [r[0] - alpha1 * image[0], r[1] - alpha1 * image[1], -alpha1 * image[2]]
    rr2 = jnp.maximum(form(gram, r), 0.0)
    beta = ratio(rr2, rr1, 0.0, 1e4)
    p = [r[0] + beta * p[0], r[1] + beta * p[1], r[2]]
    alpha2 = ratio(rr2, form(energy, p), 0.05, 4.1)
    return x[0] + alpha2 * p[0], x[1] + alpha2 * p[1], alpha2 * p[2]


def heat_kernel(
    layers, lines, w0, w1, w2, c_down, c_right, c_left, cells, own, before, after, potential, heated, warm, cond, base, store
):
    span = ROWS + 2 * HALO
    spokes = heated.shape[-1]
    block = own.shape[0] // layers
    index, count = place()
    edge = 8
    body = slice(edge, edge + layers)
    inward, outward = slice(edge - 1, edge - 1 + layers), slice(edge + 1, edge + 1 + layers)
    blank = jnp.zeros((edge, spokes), jnp.float32)
    for row in range(span):
        source, at = (before, row + ROWS - HALO) if row < HALO else (own, row - HALO) if row < HALO + ROWS else (after, row - HALO - ROWS)
        there = jnp.where(index > 0, 1.0, 0.0) if row < HALO else jnp.where(index < count - 1, 1.0, 0.0) if row >= HALO + ROWS else 1.0
        kind = source[pl.ds(ROWS + at, layers, stride=block), :]

        def table(values):
            return jnp.where(kind == 0.0, values[0], jnp.where(kind == 1.0, values[1], jnp.where(kind == 2.0, values[2], values[3])))

        base[row] = table(conduct_table) * there
        store[row] = table([0.5 * time_step / c for c in capacity_table]) * there
        warm[0, row, body] = source[pl.ds(at, layers, stride=block), :]
        for field in (warm.at[0, row], warm.at[1, row], cond.at[row]):
            field[0:edge] = blank
            field[edge + layers : 2 * edge + layers] = blank

    f0, f1, f2 = solve_small(lines[...])
    shape = w0.shape
    inside = rows_inside(shape, ROWS)
    x = (f0 * w0[...] + f1 * w1[...] + f2 * w2[...]) * inside
    potential[...] = x[ROWS : 2 * ROWS]
    col = lax.broadcasted_iota(jnp.int32, shape, 1)
    step = x - below(x)
    q_down = c_down[...] * (step * step)
    step = x - jnp.where(col == shape[1] - 1, 0.0, right(x))
    q_right = c_right[...] * (step * step)
    q_left = jnp.where(col == 0, c_left[...] * (x * x), left(q_right))
    joule = heat_factor * ((q_down + above(q_down)) + (q_right + q_left))

    cell = cells[...].astype(jnp.int32)
    azimuth = cell & (spokes - 1)
    target = jnp.where(cell >= (layers - 1) * spokes, 7, 6)
    spoke = lax.broadcasted_iota(jnp.int32, (spokes, shape[1]), 0)
    sublane = lax.broadcasted_iota(jnp.int32, (8, shape[1]), 0)
    heat = {}
    for row in range(1, span - 1):
        at = slice(row + ROWS - HALO, row + ROWS - HALO + 1)
        pick = jnp.where(azimuth[at] == spoke, 1.0, 0.0).astype(jnp.bfloat16)
        part = jnp.where(target[at] == sublane, joule[at], 0.0)
        pieces = []
        for _ in range(3):
            piece = part.astype(jnp.bfloat16)
            part = part - piece.astype(jnp.float32)
            pieces.append(piece)
        total = lax.dot_general(
            jnp.concatenate(pieces, axis=0), pick, (((1,), (1,)), ((), ())), preferred_element_type=jnp.float32
        )
        heat[row] = 2.0 * (total[0:8] + (total[8:16] + total[16:24]))

    for substep in range(SUBSTEPS):
        now, then = substep % 2, 1 - substep % 2

        def conductivity(row):
            t = warm[now, row, body]
            k = base[row] * (1.0 + diffusivity_derivative * t)
            cond[row, body] = k
            return t, k

        def between(t, k, t_other, k_other):
            return (k + k_other) * (t_other - t)

        last = conductivity(substep)
        here = conductivity(substep + 1)
        inner = between(*last, *here)
        for row in range(substep + 1, span - 1 - substep):
            t, k = here
            here = conductivity(row + 1)
            outer = between(t, k, *here)
            flux = outer - inner
            inner = outer
            flux = flux + between(t, k, warm[now, row, inward], cond[row, inward])
            flux = flux + between(t, k, warm[now, row, outward], cond[row, outward])
            face = between(t, k, right(t), right(k))
            flux = flux + (face - left(face))
            flux = jnp.concatenate([flux[: layers - 8], flux[layers - 8 :] + heat[row]], axis=0)
            fresh = t + store[row] * flux
            if substep + 1 < SUBSTEPS:
                warm[then, row, body] = fresh
            else:
                heated[pl.ds(row - HALO, layers, stride=ROWS), :] = fresh


def vmem(count):
    return [pl.BlockSpec(memory_space=pltpu.VMEM)] * count


def local(foil_warmth, terminal_voltage_input, foil_segment_pattern, underlying_block_map, prior_block_warmth, substance_kind):
    f32 = jnp.float32
    magnets, layers = lax.axis_size("magnet"), lax.axis_size("slab")
    count = magnets * layers
    width, spokes = foil_warmth.shape[1], prior_block_warmth.shape[2]
    onward = [(i, i + 1) for i in range(count - 1)]
    backward = [(i + 1, i) for i in range(count - 1)]

    def around(block):
        return lax.ppermute(block, BOTH, onward), lax.ppermute(block, BOTH, backward)

    cells = lax.dynamic_slice_in_dim(underlying_block_map, lax.axis_index("slab") * ROWS, ROWS, axis=0)
    sheet = jnp.concatenate(
        [foil_warmth, terminal_voltage_input, foil_segment_pattern.astype(f32), cells.astype(f32)], axis=0
    )
    field = jax.ShapeDtypeStruct((3 * ROWS, width), f32)
    block = 2 * ROWS + 1
    packed, *fields = pl.pallas_call(
        basis_kernel,
        out_shape=(jax.ShapeDtypeStruct((layers * block, spokes), f32),) + (field,) * 7,
        in_specs=vmem(5),
        out_specs=vmem(8),
        name="basis",
    )(sheet, *around(sheet), prior_block_warmth.reshape(layers * ROWS, spokes), substance_kind.reshape(layers * ROWS, spokes))

    bricks = lax.all_to_all(packed.reshape(layers, block, 1, spokes), "slab", 0, 0)
    lines = jnp.sum(bricks[:, 2 * ROWS], axis=0, keepdims=True)
    lines = lax.all_to_all(jnp.broadcast_to(lines, (magnets, 1, spokes)), "magnet", 0, 0).reshape(magnets, spokes)
    bricks = bricks.reshape(layers * block, spokes)

    span = ROWS + 2 * HALO
    potential, heated = pl.pallas_call(
        functools.partial(heat_kernel, layers),
        out_shape=(jax.ShapeDtypeStruct((ROWS, width), f32), jax.ShapeDtypeStruct((layers * ROWS, spokes), f32)),
        in_specs=vmem(11),
        out_specs=vmem(2),
        scratch_shapes=[
            pltpu.VMEM((2, span, layers + 16, spokes), f32),
            pltpu.VMEM((span, layers + 16, spokes), f32),
            pltpu.VMEM((span, layers, spokes), f32),
            pltpu.VMEM((span, layers, spokes), f32),
        ],
        name="heat",
    )(lines, *fields, bricks, *around(bricks))
    heated = lax.all_to_all(heated.reshape(layers, ROWS, spokes), "slab", 0, 0)
    return potential, heated.reshape(prior_block_warmth.shape)


def solution(mesh):
    placed = (
        P(("magnet", "slab"), None),
        P(("magnet", "slab"), None),
        P(("magnet", "slab"), None),
        P("magnet", None),
        P("slab", "magnet", None),
        P("slab", "magnet", None),
    )
    return jax.shard_map(
        local,
        mesh=mesh,
        in_specs=placed,
        out_specs=(P(("magnet", "slab"), None), P("slab", "magnet", None)),
        check_vma=False,
    )
```

```python
import functools

import jax
import jax.numpy as jnp
from jax import lax
from jax.experimental import pallas as pl
from jax.experimental.pallas import tpu as pltpu
from jax.sharding import PartitionSpec as P

SUBSTEPS = 4
HALO = SUBSTEPS
ROWS = 8

leak_diag = 0.25
contact_gain = 4.0
copper_factor = 3.0
sheet_slope = 0.5
heat_factor = 1.5
time_step = 0.03
conduct_table = (0.3, 1.0, 2.0, 0.6)
capacity_table = (1.0, 1.5, 2.0, 1.2)
diffusivity_derivative = 0.4

SHIFT = 9.85
SCALE = 9.6
BOTH = ("magnet", "slab")


def place():
    size = lax.axis_size("slab")
    return lax.axis_index("magnet") * size + lax.axis_index("slab"), lax.axis_size("magnet") * size


def above(v):
    return pltpu.roll(v, 1, 0)


def below(v):
    return pltpu.roll(v, v.shape[0] - 1, 0)


def left(v):
    return pltpu.roll(v, 1, 1)


def right(v):
    return pltpu.roll(v, v.shape[1] - 1, 1)


def rows_inside(shape, margin):
    index, count = place()
    row = lax.broadcasted_iota(jnp.int32, shape, 0)
    low = jnp.where(index > 0, 0, margin)
    high = jnp.where(index < count - 1, shape[0], shape[0] - margin)
    return jnp.where((row >= low) & (row < high), 1.0, 0.0).astype(jnp.float32)


def basis_kernel(own, before, after, warmth_in, kind_in, packed, w0_out, w1_out, w2_out, down_out, right_out, left_out, cells_out):
    def window(i):
        part = slice(ROWS * i, ROWS * (i + 1))
        return jnp.concatenate([before[part, :], own[part, :], after[part, :]], axis=0)

    warmth, voltage, pattern = window(0), window(1), window(2)
    cells_out[...] = window(3)
    shape = warmth.shape
    inside = rows_inside(shape, ROWS)
    col = lax.broadcasted_iota(jnp.int32, shape, 1)
    last = col == shape[1] - 1
    sigma = inside * jnp.where(pattern == 1.0, copper_factor, 1.0) / (1.0 + sheet_slope * warmth)
    contact = jnp.where(pattern == 2.0, contact_gain, 0.0)
    c_down = 0.5 * (sigma + below(sigma))
    c_right = 0.5 * (sigma + jnp.where(last, 0.0, right(sigma)))
    c_left = jnp.where(col == 0, 0.5 * sigma, left(c_right))
    diagonal = leak_diag + contact + above(c_down) + c_down + c_left + c_right
    diagonal = (diagonal - SHIFT) * (1.0 / SCALE)
    o_down = c_down * inside * below(inside) * (1.0 / SCALE)
    o_up = above(o_down)
    o_right = jnp.where(last, 0.0, c_right) * (1.0 / SCALE)
    o_left = left(o_right)

    def apply(v):
        return diagonal * v - (o_up * above(v) + o_down * below(v)) - (o_left * left(v) + o_right * right(v))

    w0 = contact * voltage
    w1 = apply(w0)
    w2 = 2.0 * apply(w1) - w0
    w3 = apply(w2)
    w0_out[...] = w0
    w1_out[...] = w1
    w2_out[...] = w2
    down_out[...] = c_down
    right_out[...] = c_right
    left_out[...] = c_left
    a, b, c, d = (v[ROWS : 2 * ROWS] for v in (w0, w1, w2, w3))
    lane = lax.broadcasted_iota(jnp.int32, (1, 128), 1)
    line = jnp.zeros((1, 128), jnp.float32)
    for i, (u, v) in enumerate(((a, a), (a, b), (a, c), (b, b), (b, c), (c, c), (c, d))):
        line = jnp.where(lane == i, jnp.sum(u * v, keepdims=True), line)
    block = 2 * ROWS + 1
    for slab in range(packed.shape[0] // block):
        part = slice(ROWS * slab, ROWS * (slab + 1))
        at = block * slab
        packed[at : at + ROWS] = warmth_in[part]
        packed[at + ROWS : at + 2 * ROWS] = kind_in[part].astype(jnp.float32)
        packed[at + 2 * ROWS : at + block] = line


def solve_small(lines):
    total = jnp.sum(lines, axis=0, keepdims=True)
    g00, g01, g02, g11, g12, g22, k22 = (total[:, i : i + 1] for i in range(7))
    gram = ((g00, g01, g02), (g01, g11, g12), (g02, g12, g22))
    k11, k12 = 0.5 * (g12 + g01), 0.5 * (g22 + g02)
    shifted = ((g01, g11, g12), (g11, k11, k12), (g12, k12, k22))
    energy = [[SCALE * shifted[i][j] + SHIFT * gram[i][j] for j in range(3)] for i in range(3)]

    def form(m, v):
        return sum(v[i] * (v[i] * m[i][i] + 2.0 * sum((v[j] * m[i][j] for j in range(i + 1, len(v))), 0.0)) for i in range(len(v)))

    def ratio(num, den, low, high):
        return jnp.clip(num / jnp.maximum(den, 1e-37), low, high)

    alpha0 = g00 / energy[0][0]
    r = [1.0 - alpha0 * SHIFT, -alpha0 * SCALE]
    rr1 = jnp.maximum(form(gram, r), 0.0)
    beta = ratio(rr1, g00, 0.0, 1e4)
    p = [r[0] + beta, r[1]]
    alpha1 = ratio(rr1, form(energy, p), 0.05, 4.1)
    half = 0.5 * SCALE * p[1]
    image = [half + SHIFT * p[0], SCALE * p[0] + SHIFT * p[1], half]
    x = [alpha0 + alpha1 * p[0], alpha1 * p[1]]
    r = [r[0] - alpha1 * image[0], r[1] - alpha1 * image[1], -alpha1 * image[2]]
    rr2 = jnp.maximum(form(gram, r), 0.0)
    beta = ratio(rr2, rr1, 0.0, 1e4)
    p = [r[0] + beta * p[0], r[1] + beta * p[1], r[2]]
    alpha2 = ratio(rr2, form(energy, p), 0.05, 4.1)
    return x[0] + alpha2 * p[0], x[1] + alpha2 * p[1], alpha2 * p[2]


PAIRS = ((0, 0), (0, 1), (0, 2), (1, 1), (1, 2), (2, 2))
SPAN = ROWS + 2 * HALO
EDGE = 8


def deposit_kernel(layers, w0, w1, w2, c_down, c_right, c_left, cells, bins, heats):
    spokes = bins.shape[-1]
    shape = w0.shape
    inside = rows_inside(shape, ROWS)
    col = lax.broadcasted_iota(jnp.int32, shape, 1)
    last, first = col == shape[1] - 1, col == 0
    fields = [w[...] * inside for w in (w0, w1, w2)]
    falls = [w - below(w) for w in fields]
    steps = [w - jnp.where(last, 0.0, right(w)) for w in fields]
    wanted = slice(ROWS - HALO, ROWS - HALO + SPAN)
    for pair, (i, j) in enumerate(PAIRS):
        q_down = c_down[...] * (falls[i] * falls[j])
        q_right = c_right[...] * (steps[i] * steps[j])
        q_left = jnp.where(first, c_left[...] * (fields[i] * fields[j]), left(q_right))
        joule = (q_down + above(q_down)) + (q_right + q_left)
        factor = heat_factor if i == j else 2.0 * heat_factor
        joule = factor * joule[wanted]
        for part in range(heats.shape[0]):
            heats[part, SPAN * pair : SPAN * (pair + 1)] = joule[:, 128 * part : 128 * (part + 1)]
    for part in range(heats.shape[0]):
        heats[part, SPAN * len(PAIRS) :] = jnp.zeros((SPAN * (8 - len(PAIRS)), 128), jnp.float32)
    cell = cells[wanted].astype(jnp.int32)
    azimuth = cell & (spokes - 1)
    outermost = jnp.where(cell >= (layers - 1) * spokes, 1.0, 0.0)
    spoke = lax.broadcasted_iota(jnp.int32, (spokes, shape[1]), 0)
    for row in range(1, SPAN - 1):
        pick = jnp.where(azimuth[row : row + 1] == spoke, 1.0, 0.0).astype(jnp.bfloat16)
        joule = jnp.concatenate([heats[part, pl.ds(row, 8, stride=SPAN), :] for part in range(heats.shape[0])], axis=1)
        upper = joule * outermost[row : row + 1]
        pieces = []
        for part in (joule - upper, upper):
            for _ in range(3):
                piece = part.astype(jnp.bfloat16)
                part = part - piece.astype(jnp.float32)
                pieces.append(piece)
        total = lax.dot_general(
            jnp.concatenate(pieces, axis=0), pick, (((1,), (1,)), ((), ())), preferred_element_type=jnp.float32
        )
        bins[row, 0:8] = total[0:8] + (total[8:16] + total[16:24])
        bins[row, 8:16] = total[24:32] + (total[32:40] + total[40:48])


def substep_rows(rows, layers, warm, cond, base, done):
    body = slice(EDGE, EDGE + layers)
    inward, outward = slice(EDGE - 1, EDGE - 1 + layers), slice(EDGE + 1, EDGE + 1 + layers)

    def conductivity(row):
        t = warm[row, body]
        k = base[row] * (1.0 + diffusivity_derivative * t)
        cond[row, body] = k
        return t, k

    def between(t, k, t_other, k_other):
        return (k + k_other) * (t_other - t)

    below_row = conductivity(rows[0] - 1)
    here = conductivity(rows[0])
    inner = between(*below_row, *here)
    for row in rows:
        t, k = here
        here = conductivity(row + 1)
        outer = between(t, k, *here)
        flux = outer - inner
        inner = outer
        flux = flux + between(t, k, warm[row, inward], cond[row, inward])
        flux = flux + between(t, k, warm[row, outward], cond[row, outward])
        face = between(t, k, right(t), right(k))
        done(row, t, flux + (face - left(face)))


def clear_edges(layers, *fields):
    for field in fields:
        blank = jnp.zeros((EDGE, field.shape[-1]), jnp.float32)
        field[0:EDGE] = blank
        field[EDGE + layers : 2 * EDGE + layers] = blank


def first_kernel(layers, own, before, after, fresh, base, store, warm, cond):
    block = own.shape[0] // layers
    index, count = place()
    body = slice(EDGE, EDGE + layers)
    for row in range(SPAN):
        source, at, there = own, row - HALO, 1.0
        if row < HALO:
            source, at, there = before, row + ROWS - HALO, jnp.where(index > 0, 1.0, 0.0)
        elif row >= HALO + ROWS:
            source, at, there = after, row - HALO - ROWS, jnp.where(index < count - 1, 1.0, 0.0)
        kind = source[pl.ds(ROWS + at, layers, stride=block), :]

        def table(values):
            return jnp.where(kind == 0.0, values[0], jnp.where(kind == 1.0, values[1], jnp.where(kind == 2.0, values[2], values[3])))

        base[row] = table(conduct_table) * there
        store[row] = table([0.5 * time_step / c for c in capacity_table]) * there
        warm[row, body] = source[pl.ds(at, layers, stride=block), :]
        clear_edges(layers, warm.at[row], cond.at[row], fresh.at[row])

    def done(row, t, flux):
        fresh[row, body] = t + store[row] * flux

    substep_rows(range(1, SPAN - 1), layers, warm, cond, base, done)


def heat_kernel(layers, lines, w0, w1, w2, bins, fresh, base, store, potential, heated, warm, cond):
    spokes = heated.shape[-1]
    body = slice(EDGE, EDGE + layers)
    f = solve_small(lines[...])
    own = slice(ROWS, 2 * ROWS)
    potential[...] = f[0] * w0[own] + f[1] * w1[own] + f[2] * w2[own]
    sublane = lax.broadcasted_iota(jnp.int32, (8, spokes), 0)
    weight = jnp.zeros((8, spokes), jnp.float32)
    for pair, (i, j) in enumerate(PAIRS):
        weight = jnp.where(sublane == pair, f[i] * f[j], weight)
    weight = 2.0 * weight
    heat = {}
    top = slice(layers - 8, layers)
    for row in range(1, SPAN - 1):
        inner = jnp.sum(weight * bins[row, 0:8], axis=0, keepdims=True)
        outer = jnp.sum(weight * bins[row, 8:16], axis=0, keepdims=True)
        heat[row] = jnp.where(sublane == 6, inner, jnp.where(sublane == 7, outer, 0.0))
        warm[1, row] = fresh[row]
        warm[1, row, EDGE + layers - 8 : EDGE + layers] = fresh[row, EDGE + layers - 8 : EDGE + layers] + store[row, top] * heat[row]
        clear_edges(layers, warm.at[0, row], cond.at[row])

    for substep in range(1, SUBSTEPS):

        def done(row, t, flux):
            flux = jnp.concatenate([flux[: layers - 8], flux[top] + heat[row]], axis=0)
            t = t + store[row] * flux
            if substep + 1 < SUBSTEPS:
                warm[1 - substep % 2, row, body] = t
            else:
                heated[pl.ds(row - HALO, layers, stride=ROWS), :] = t

        substep_rows(range(substep + 1, SPAN - 1 - substep), layers, warm.at[substep % 2], cond, base, done)


def vmem(count):
    return [pl.BlockSpec(memory_space=pltpu.VMEM)] * count


def local(foil_warmth, terminal_voltage_input, foil_segment_pattern, underlying_block_map, prior_block_warmth, substance_kind):
    f32 = jnp.float32
    magnets, layers = lax.axis_size("magnet"), lax.axis_size("slab")
    count = magnets * layers
    width, spokes = foil_warmth.shape[1], prior_block_warmth.shape[2]
    onward = [(i, i + 1) for i in range(count - 1)]
    backward = [(i + 1, i) for i in range(count - 1)]

    def around(block):
        return lax.ppermute(block, BOTH, onward), lax.ppermute(block, BOTH, backward)

    cells = lax.dynamic_slice_in_dim(underlying_block_map, lax.axis_index("slab") * ROWS, ROWS, axis=0)
    sheet = jnp.concatenate(
        [foil_warmth, terminal_voltage_input, foil_segment_pattern.astype(f32), cells.astype(f32)], axis=0
    )
    field = jax.ShapeDtypeStruct((3 * ROWS, width), f32)
    block = 2 * ROWS + 1
    packed, *fields = pl.pallas_call(
        basis_kernel,
        out_shape=(jax.ShapeDtypeStruct((layers * block, spokes), f32),) + (field,) * 7,
        in_specs=vmem(5),
        out_specs=vmem(8),
        name="basis",
    )(sheet, *around(sheet), prior_block_warmth.reshape(layers * ROWS, spokes), substance_kind.reshape(layers * ROWS, spokes))

    bricks = lax.all_to_all(packed.reshape(layers, block, 1, spokes), "slab", 0, 0)
    bins = pl.pallas_call(
        functools.partial(deposit_kernel, layers),
        out_shape=jax.ShapeDtypeStruct((SPAN, 16, spokes), f32),
        in_specs=vmem(7),
        out_specs=vmem(1)[0],
        scratch_shapes=[pltpu.VMEM((width // 128, 8 * SPAN, 128), f32)],
        cost_estimate=pl.CostEstimate(flops=10**8, bytes_accessed=2 * 10**6, transcendentals=0),
        name="deposit",
    )(*fields)
    lines = jnp.sum(bricks[:, 2 * ROWS], axis=0, keepdims=True)
    lines = jnp.broadcast_to(lines, (magnets, 1, spokes))
    lines, bricks, bins = lax.optimization_barrier((lines, bricks.reshape(layers * block, spokes), bins))
    lines = lax.all_to_all(lines, "magnet", 0, 0).reshape(magnets, spokes)

    padded = (SPAN, layers + 2 * EDGE, spokes)
    plain = (SPAN, layers, spokes)
    stage = pl.pallas_call(
        functools.partial(first_kernel, layers),
        out_shape=tuple(jax.ShapeDtypeStruct(dims, f32) for dims in (padded, plain, plain)),
        in_specs=vmem(3),
        out_specs=vmem(3),
        scratch_shapes=[pltpu.VMEM(padded, f32), pltpu.VMEM(padded, f32)],
        cost_estimate=pl.CostEstimate(flops=10**7, bytes_accessed=2 * 10**6, transcendentals=0),
        name="first",
    )(bricks, *around(bricks))
    potential, heated = pl.pallas_call(
        functools.partial(heat_kernel, layers),
        out_shape=(jax.ShapeDtypeStruct((ROWS, width), f32), jax.ShapeDtypeStruct((layers * ROWS, spokes), f32)),
        in_specs=vmem(8),
        out_specs=vmem(2),
        scratch_shapes=[pltpu.VMEM((2,) + padded, f32), pltpu.VMEM(padded, f32)],
        name="heat",
    )(lines, *fields[:3], bins, *stage)
    heated = lax.all_to_all(heated.reshape(layers, ROWS, spokes), "slab", 0, 0)
    return potential, heated.reshape(prior_block_warmth.shape)


def solution(mesh):
    placed = (
        P(("magnet", "slab"), None),
        P(("magnet", "slab"), None),
        P(("magnet", "slab"), None),
        P("magnet", None),
        P("slab", "magnet", None),
        P("slab", "magnet", None),
    )
    return jax.shard_map(
        local,
        mesh=mesh,
        in_specs=placed,
        out_specs=(P(("magnet", "slab"), None), P("slab", "magnet", None)),
        check_vma=False,
    )
```

```python
import functools

import jax
import jax.numpy as jnp
from jax import lax
from jax.experimental import pallas as pl
from jax.experimental.pallas import tpu as pltpu
from jax.sharding import PartitionSpec as P

SUBSTEPS = 4
HALO = SUBSTEPS
ROWS = 8

leak_diag = 0.25
contact_gain = 4.0
copper_factor = 3.0
sheet_slope = 0.5
heat_factor = 1.5
time_step = 0.03
conduct_table = (0.3, 1.0, 2.0, 0.6)
capacity_table = (1.0, 1.5, 2.0, 1.2)
diffusivity_derivative = 0.4

SHIFT = 9.85
SCALE = 9.6
BOTH = ("magnet", "slab")


def place():
    size = lax.axis_size("slab")
    return lax.axis_index("magnet") * size + lax.axis_index("slab"), lax.axis_size("magnet") * size


def above(v):
    return pltpu.roll(v, 1, 0)


def below(v):
    return pltpu.roll(v, v.shape[0] - 1, 0)


def left(v):
    return pltpu.roll(v, 1, 1)


def right(v):
    return pltpu.roll(v, v.shape[1] - 1, 1)


def rows_inside(shape, margin):
    index, count = place()
    row = lax.broadcasted_iota(jnp.int32, shape, 0)
    low = jnp.where(index > 0, 0, margin)
    high = jnp.where(index < count - 1, shape[0], shape[0] - margin)
    return jnp.where((row >= low) & (row < high), 1.0, 0.0).astype(jnp.float32)


def basis_kernel(own, before, after, warmth_in, kind_in, packed, w0_out, w1_out, w2_out, down_out, right_out, left_out, cells_out):
    def window(i):
        part = slice(ROWS * i, ROWS * (i + 1))
        return jnp.concatenate([before[part, :], own[part, :], after[part, :]], axis=0)

    warmth, voltage, pattern = window(0), window(1), window(2)
    cells_out[...] = window(3)
    shape = warmth.shape
    inside = rows_inside(shape, ROWS)
    col = lax.broadcasted_iota(jnp.int32, shape, 1)
    last = col == shape[1] - 1
    sigma = inside * jnp.where(pattern == 1.0, copper_factor, 1.0) / (1.0 + sheet_slope * warmth)
    contact = jnp.where(pattern == 2.0, contact_gain, 0.0)
    c_down = 0.5 * (sigma + below(sigma))
    c_right = 0.5 * (sigma + jnp.where(last, 0.0, right(sigma)))
    c_left = jnp.where(col == 0, 0.5 * sigma, left(c_right))
    diagonal = leak_diag + contact + above(c_down) + c_down + c_left + c_right
    diagonal = (diagonal - SHIFT) * (1.0 / SCALE)
    o_down = c_down * inside * below(inside) * (1.0 / SCALE)
    o_up = above(o_down)
    o_right = jnp.where(last, 0.0, c_right) * (1.0 / SCALE)
    o_left = left(o_right)

    def apply(v):
        return diagonal * v - (o_up * above(v) + o_down * below(v)) - (o_left * left(v) + o_right * right(v))

    w0 = contact * voltage
    w1 = apply(w0)
    w2 = 2.0 * apply(w1) - w0
    w3 = apply(w2)
    w0_out[...] = w0
    w1_out[...] = w1
    w2_out[...] = w2
    down_out[...] = c_down
    right_out[...] = c_right
    left_out[...] = c_left
    a, b, c, d = (v[ROWS : 2 * ROWS] for v in (w0, w1, w2, w3))
    lane = lax.broadcasted_iota(jnp.int32, (1, 128), 1)
    line = jnp.zeros((1, 128), jnp.float32)
    for i, (u, v) in enumerate(((a, a), (a, b), (a, c), (b, b), (b, c), (c, c), (c, d))):
        line = jnp.where(lane == i, jnp.sum(u * v, keepdims=True), line)
    block = 2 * ROWS + 1
    for slab in range(packed.shape[0] // block):
        part = slice(ROWS * slab, ROWS * (slab + 1))
        at = block * slab
        packed[at : at + ROWS] = warmth_in[part]
        packed[at + ROWS : at + 2 * ROWS] = kind_in[part].astype(jnp.float32)
        packed[at + 2 * ROWS : at + block] = line


def solve_small(lines):
    total = jnp.sum(lines, axis=0, keepdims=True)
    g00, g01, g02, g11, g12, g22, k22 = (total[:, i : i + 1] for i in range(7))
    gram = ((g00, g01, g02), (g01, g11, g12), (g02, g12, g22))
    k11, k12 = 0.5 * (g12 + g01), 0.5 * (g22 + g02)
    shifted = ((g01, g11, g12), (g11, k11, k12), (g12, k12, k22))
    energy = [[SCALE * shifted[i][j] + SHIFT * gram[i][j] for j in range(3)] for i in range(3)]

    def form(m, v):
        return sum(v[i] * (v[i] * m[i][i] + 2.0 * sum((v[j] * m[i][j] for j in range(i + 1, len(v))), 0.0)) for i in range(len(v)))

    def ratio(num, den, low, high):
        return jnp.clip(num / jnp.maximum(den, 1e-37), low, high)

    alpha0 = g00 / energy[0][0]
    r = [1.0 - alpha0 * SHIFT, -alpha0 * SCALE]
    rr1 = jnp.maximum(form(gram, r), 0.0)
    beta = ratio(rr1, g00, 0.0, 1e4)
    p = [r[0] + beta, r[1]]
    alpha1 = ratio(rr1, form(energy, p), 0.05, 4.1)
    half = 0.5 * SCALE * p[1]
    image = [half + SHIFT * p[0], SCALE * p[0] + SHIFT * p[1], half]
    x = [alpha0 + alpha1 * p[0], alpha1 * p[1]]
    r = [r[0] - alpha1 * image[0], r[1] - alpha1 * image[1], -alpha1 * image[2]]
    rr2 = jnp.maximum(form(gram, r), 0.0)
    beta = ratio(rr2, rr1, 0.0, 1e4)
    p = [r[0] + beta * p[0], r[1] + beta * p[1], r[2]]
    alpha2 = ratio(rr2, form(energy, p), 0.05, 4.1)
    return x[0] + alpha2 * p[0], x[1] + alpha2 * p[1], alpha2 * p[2]


PAIRS = ((0, 0), (0, 1), (0, 2), (1, 1), (1, 2), (2, 2))
SPAN = ROWS + 2 * HALO
EDGE = 8


def deposit_kernel(layers, w0, w1, w2, c_down, c_right, c_left, cells, bins, heats):
    spokes = bins.shape[-1]
    shape = w0.shape
    inside = rows_inside(shape, ROWS)
    col = lax.broadcasted_iota(jnp.int32, shape, 1)
    last, first = col == shape[1] - 1, col == 0
    fields = [w[...] * inside for w in (w0, w1, w2)]
    falls = [w - below(w) for w in fields]
    steps = [w - jnp.where(last, 0.0, right(w)) for w in fields]
    wanted = slice(ROWS - HALO, ROWS - HALO + SPAN)
    for pair, (i, j) in enumerate(PAIRS):
        q_down = c_down[...] * (falls[i] * falls[j])
        q_right = c_right[...] * (steps[i] * steps[j])
        q_left = jnp.where(first, c_left[...] * (fields[i] * fields[j]), left(q_right))
        joule = (q_down + above(q_down)) + (q_right + q_left)
        factor = heat_factor if i == j else 2.0 * heat_factor
        joule = factor * joule[wanted]
        for part in range(heats.shape[0]):
            heats[part, SPAN * pair : SPAN * (pair + 1)] = joule[:, 128 * part : 128 * (part + 1)]
    for part in range(heats.shape[0]):
        heats[part, SPAN * len(PAIRS) :] = jnp.zeros((SPAN * (8 - len(PAIRS)), 128), jnp.float32)
    cell = cells[wanted].astype(jnp.int32)
    azimuth = cell & (spokes - 1)
    outermost = jnp.where(cell >= (layers - 1) * spokes, 1.0, 0.0)
    spoke = lax.broadcasted_iota(jnp.int32, (spokes, shape[1]), 0)
    for row in range(1, SPAN - 1):
        pick = jnp.where(azimuth[row : row + 1] == spoke, 1.0, 0.0).astype(jnp.bfloat16)
        joule = jnp.concatenate([heats[part, pl.ds(row, 8, stride=SPAN), :] for part in range(heats.shape[0])], axis=1)
        upper = joule * outermost[row : row + 1]
        pieces = []
        for part in (joule - upper, upper):
            for _ in range(3):
                piece = part.astype(jnp.bfloat16)
                part = part - piece.astype(jnp.float32)
                pieces.append(piece)
        total = lax.dot_general(
            jnp.concatenate(pieces, axis=0), pick, (((1,), (1,)), ((), ())), preferred_element_type=jnp.float32
        )
        bins[row, 0:8] = total[0:8] + (total[8:16] + total[16:24])
        bins[row, 8:16] = total[24:32] + (total[32:40] + total[40:48])


def substep_rows(rows, layers, warm, cond, base, done):
    body = slice(EDGE, EDGE + layers)
    inward, outward = slice(EDGE - 1, EDGE - 1 + layers), slice(EDGE + 1, EDGE + 1 + layers)

    def conductivity(row):
        t = warm[row, body]
        k = base[row] * (1.0 + diffusivity_derivative * t)
        cond[row, body] = k
        return t, k

    def between(t, k, t_other, k_other):
        return (k + k_other) * (t_other - t)

    below_row = conductivity(rows[0] - 1)
    here = conductivity(rows[0])
    inner = between(*below_row, *here)
    for row in rows:
        t, k = here
        here = conductivity(row + 1)
        outer = between(t, k, *here)
        flux = outer - inner
        inner = outer
        flux = flux + between(t, k, warm[row, inward], cond[row, inward])
        flux = flux + between(t, k, warm[row, outward], cond[row, outward])
        face = between(t, k, right(t), right(k))
        done(row, t, flux + (face - left(face)))


def clear_edges(layers, *fields):
    for field in fields:
        blank = jnp.zeros((EDGE, field.shape[-1]), jnp.float32)
        field[0:EDGE] = blank
        field[EDGE + layers : 2 * EDGE + layers] = blank


def first_kernel(layers, own, before, after, fresh, base, store, warm, cond):
    block = own.shape[0] // layers
    index, count = place()
    body = slice(EDGE, EDGE + layers)
    for row in range(SPAN):
        source, at, there = own, row - HALO, 1.0
        if row < HALO:
            source, at, there = before, row + ROWS - HALO, jnp.where(index > 0, 1.0, 0.0)
        elif row >= HALO + ROWS:
            source, at, there = after, row - HALO - ROWS, jnp.where(index < count - 1, 1.0, 0.0)
        kind = source[pl.ds(ROWS + at, layers, stride=block), :]

        def table(values):
            return jnp.where(kind == 0.0, values[0], jnp.where(kind == 1.0, values[1], jnp.where(kind == 2.0, values[2], values[3])))

        base[row] = table(conduct_table) * there
        store[row] = table([0.5 * time_step / c for c in capacity_table]) * there
        warm[row, body] = source[pl.ds(at, layers, stride=block), :]
        clear_edges(layers, warm.at[row], cond.at[row], fresh.at[row])

    def done(row, t, flux):
        fresh[row, body] = t + store[row] * flux

    substep_rows(range(1, SPAN - 1), layers, warm, cond, base, done)


def heat_kernel(layers, lines, w0, w1, w2, bins, fresh, base, store, potential, heated, warm, cond):
    spokes = heated.shape[-1]
    body = slice(EDGE, EDGE + layers)
    f = solve_small(lines[...])
    own = slice(ROWS, 2 * ROWS)
    potential[...] = f[0] * w0[own] + f[1] * w1[own] + f[2] * w2[own]
    sublane = lax.broadcasted_iota(jnp.int32, (8, spokes), 0)
    weight = jnp.zeros((8, spokes), jnp.float32)
    for pair, (i, j) in enumerate(PAIRS):
        weight = jnp.where(sublane == pair, f[i] * f[j], weight)
    weight = 2.0 * weight
    heat = {}
    top = slice(layers - 8, layers)
    for row in range(1, SPAN - 1):
        inner = jnp.sum(weight * bins[row, 0:8], axis=0, keepdims=True)
        outer = jnp.sum(weight * bins[row, 8:16], axis=0, keepdims=True)
        heat[row] = jnp.where(sublane == 6, inner, jnp.where(sublane == 7, outer, 0.0))
        warm[1, row] = fresh[row]
        warm[1, row, EDGE + layers - 8 : EDGE + layers] = fresh[row, EDGE + layers - 8 : EDGE + layers] + store[row, top] * heat[row]
        clear_edges(layers, warm.at[0, row], cond.at[row])

    for substep in range(1, SUBSTEPS):

        def done(row, t, flux):
            flux = jnp.concatenate([flux[: layers - 8], flux[top] + heat[row]], axis=0)
            t = t + store[row] * flux
            if substep + 1 < SUBSTEPS:
                warm[1 - substep % 2, row, body] = t
            else:
                heated[pl.ds(row - HALO, layers, stride=ROWS), :] = t

        substep_rows(range(substep + 1, SPAN - 1 - substep), layers, warm.at[substep % 2], cond, base, done)


def vmem(count):
    return [pl.BlockSpec(memory_space=pltpu.VMEM)] * count


def local(foil_warmth, terminal_voltage_input, foil_segment_pattern, underlying_block_map, prior_block_warmth, substance_kind):
    f32 = jnp.float32
    magnets, layers = lax.axis_size("magnet"), lax.axis_size("slab")
    count = magnets * layers
    width, spokes = foil_warmth.shape[1], prior_block_warmth.shape[2]
    onward = [(i, i + 1) for i in range(count - 1)]
    backward = [(i + 1, i) for i in range(count - 1)]

    def around(block):
        return lax.ppermute(block, BOTH, onward), lax.ppermute(block, BOTH, backward)

    cells = lax.dynamic_slice_in_dim(underlying_block_map, lax.axis_index("slab") * ROWS, ROWS, axis=0)
    sheet = jnp.concatenate(
        [foil_warmth, terminal_voltage_input, foil_segment_pattern.astype(f32), cells.astype(f32)], axis=0
    )
    field = jax.ShapeDtypeStruct((3 * ROWS, width), f32)
    block = 2 * ROWS + 1
    packed, *fields = pl.pallas_call(
        basis_kernel,
        out_shape=(jax.ShapeDtypeStruct((layers * block, spokes), f32),) + (field,) * 7,
        in_specs=vmem(5),
        out_specs=vmem(8),
        compiler_params=pltpu.CompilerParams(vmem_limit_bytes=8388608),
        name="basis",
    )(sheet, *around(sheet), prior_block_warmth.reshape(layers * ROWS, spokes), substance_kind.reshape(layers * ROWS, spokes))

    bricks = lax.all_to_all(packed.reshape(layers, block, 1, spokes), "slab", 0, 0)
    bins = pl.pallas_call(
        functools.partial(deposit_kernel, layers),
        out_shape=jax.ShapeDtypeStruct((SPAN, 16, spokes), f32),
        in_specs=vmem(7),
        out_specs=vmem(1)[0],
        scratch_shapes=[pltpu.VMEM((width // 128, 8 * SPAN, 128), f32)],
        cost_estimate=pl.CostEstimate(flops=10**8, bytes_accessed=2 * 10**6, transcendentals=0),
        compiler_params=pltpu.CompilerParams(vmem_limit_bytes=8388608),
        name="deposit",
    )(*fields)
    lines = jnp.sum(bricks[:, 2 * ROWS], axis=0, keepdims=True)
    lines = jnp.broadcast_to(lines, (magnets, 1, spokes))
    lines, bricks, bins = lax.optimization_barrier((lines, bricks.reshape(layers * block, spokes), bins))
    lines = lax.all_to_all(lines, "magnet", 0, 0).reshape(magnets, spokes)

    padded = (SPAN, layers + 2 * EDGE, spokes)
    plain = (SPAN, layers, spokes)
    stage = pl.pallas_call(
        functools.partial(first_kernel, layers),
        out_shape=tuple(jax.ShapeDtypeStruct(dims, f32) for dims in (padded, plain, plain)),
        in_specs=vmem(3),
        out_specs=vmem(3),
        scratch_shapes=[pltpu.VMEM(padded, f32), pltpu.VMEM(padded, f32)],
        cost_estimate=pl.CostEstimate(flops=10**7, bytes_accessed=2 * 10**6, transcendentals=0),
        compiler_params=pltpu.CompilerParams(vmem_limit_bytes=8388608),
        name="first",
    )(bricks, *around(bricks))
    potential, heated = pl.pallas_call(
        functools.partial(heat_kernel, layers),
        out_shape=(jax.ShapeDtypeStruct((ROWS, width), f32), jax.ShapeDtypeStruct((layers * ROWS, spokes), f32)),
        in_specs=vmem(8),
        out_specs=vmem(2),
        scratch_shapes=[pltpu.VMEM((2,) + padded, f32), pltpu.VMEM(padded, f32)],
        compiler_params=pltpu.CompilerParams(vmem_limit_bytes=8388608),
        name="heat",
    )(lines, *fields[:3], bins, *stage)
    heated = lax.all_to_all(heated.reshape(layers, ROWS, spokes), "slab", 0, 0)
    return potential, heated.reshape(prior_block_warmth.shape)


def solution(mesh):
    placed = (
        P(("magnet", "slab"), None),
        P(("magnet", "slab"), None),
        P(("magnet", "slab"), None),
        P("magnet", None),
        P("slab", "magnet", None),
        P("slab", "magnet", None),
    )
    return jax.shard_map(
        local,
        mesh=mesh,
        in_specs=placed,
        out_specs=(P(("magnet", "slab"), None), P("slab", "magnet", None)),
        check_vma=False,
    )
```

```python
import functools

import jax
import jax.numpy as jnp
from jax import lax
from jax.experimental import pallas as pl
from jax.experimental.pallas import tpu as pltpu
from jax.sharding import PartitionSpec as P

SUBSTEPS = 4
HALO = SUBSTEPS
ROWS = 8

leak_diag = 0.25
contact_gain = 4.0
copper_factor = 3.0
sheet_slope = 0.5
heat_factor = 1.5
time_step = 0.03
conduct_table = (0.3, 1.0, 2.0, 0.6)
capacity_table = (1.0, 1.5, 2.0, 1.2)
diffusivity_derivative = 0.4

SHIFT = 9.85
SCALE = 9.6
BOTH = ("magnet", "slab")
BLOCK = 2 * ROWS + 1


def place():
    size = lax.axis_size("slab")
    return lax.axis_index("magnet") * size + lax.axis_index("slab"), lax.axis_size("magnet") * size


def above(v):
    return pltpu.roll(v, 1, 0)


def below(v):
    return pltpu.roll(v, v.shape[0] - 1, 0)


def left(v):
    return pltpu.roll(v, 1, 1)


def right(v):
    return pltpu.roll(v, v.shape[1] - 1, 1)


def rows_inside(shape, margin, ends_here=False):
    index, count = place()
    row = lax.broadcasted_iota(jnp.int32, shape, 0)
    low = jnp.where(index > 0, 0, margin)
    high = shape[0] - margin if ends_here else jnp.where(index < count - 1, shape[0], shape[0] - margin)
    return jnp.where((row >= low) & (row < high), 1.0, 0.0).astype(jnp.float32)


def sheet_kernel(warmth, voltage, pattern, cells, sheet, pattern_here, cells_here, sems):
    at = pl.multiple_of(lax.axis_index("slab") * ROWS, ROWS)
    copies = [
        pltpu.make_async_copy(pattern, pattern_here, sems.at[0]),
        pltpu.make_async_copy(cells.at[pl.ds(at, ROWS)], cells_here, sems.at[1]),
        pltpu.make_async_copy(warmth, sheet.at[0:ROWS], sems.at[2]),
        pltpu.make_async_copy(voltage, sheet.at[ROWS : 2 * ROWS], sems.at[3]),
    ]
    for copy in copies:
        copy.start()
    copies[0].wait()
    sheet[2 * ROWS : 3 * ROWS] = pattern_here[...].astype(jnp.float32)
    copies[1].wait()
    sheet[3 * ROWS : 4 * ROWS] = cells_here[...].astype(jnp.float32)
    copies[2].wait()
    copies[3].wait()


def pack_kernel(warmth, kind, packed):
    for slab in range(packed.shape[0] // BLOCK):
        part = slice(ROWS * slab, ROWS * (slab + 1))
        at = BLOCK * slab
        packed[at : at + ROWS] = warmth[part]
        packed[at + ROWS : at + 2 * ROWS] = kind[part].astype(jnp.float32)
        packed[at + 2 * ROWS : at + BLOCK] = jnp.zeros((1, packed.shape[1]), jnp.float32)


def basis(before, own, after):
    def window(i):
        part = slice(ROWS * i, ROWS * (i + 1))
        mine = own[part]
        return jnp.concatenate([before[part], mine, jnp.zeros_like(mine) if after is None else after[part]], axis=0)

    warmth, voltage, pattern = window(0), window(1), window(2)
    shape = warmth.shape
    inside = rows_inside(shape, ROWS, after is None)
    col = lax.broadcasted_iota(jnp.int32, shape, 1)
    last = col == shape[1] - 1
    sigma = inside * jnp.where(pattern == 1.0, copper_factor, 1.0) / (1.0 + sheet_slope * warmth)
    contact = jnp.where(pattern == 2.0, contact_gain, 0.0)
    c_down = 0.5 * (sigma + below(sigma))
    c_right = 0.5 * (sigma + jnp.where(last, 0.0, right(sigma)))
    c_left = jnp.where(col == 0, 0.5 * sigma, left(c_right))
    diagonal = leak_diag + contact + above(c_down) + c_down + c_left + c_right
    diagonal = (diagonal - SHIFT) * (1.0 / SCALE)
    o_down = c_down * inside * below(inside) * (1.0 / SCALE)
    o_up = above(o_down)
    o_right = jnp.where(last, 0.0, c_right) * (1.0 / SCALE)
    o_left = left(o_right)

    def apply(v):
        return diagonal * v - (o_up * above(v) + o_down * below(v)) - (o_left * left(v) + o_right * right(v))

    w0 = contact * voltage
    w1 = apply(w0)
    w2 = 2.0 * apply(w1) - w0
    return (w0, w1, w2), apply, inside, (c_down, c_right, c_left)


def gram_kernel(own, before, packed_in, packed):
    (w0, w1, w2), apply, _, _ = basis(before, own, None)
    w3 = apply(w2)
    index, count = place()
    row = lax.broadcasted_iota(jnp.int32, w0.shape, 0)
    taken = (row >= ROWS - HALO) & (row < jnp.where(index < count - 1, 2 * ROWS - HALO, 2 * ROWS))
    lane = lax.broadcasted_iota(jnp.int32, (1, 128), 1)
    line = jnp.zeros((1, 128), jnp.float32)
    for i, (u, v) in enumerate(((w0, w0), (w0, w1), (w0, w2), (w1, w1), (w1, w2), (w2, w2), (w2, w3))):
        line = jnp.where(lane == i, jnp.sum(jnp.where(taken, u * v, 0.0), keepdims=True), line)
    for slab in range(packed.shape[0] // BLOCK):
        at = BLOCK * slab
        packed[at : at + 2 * ROWS] = packed_in[at : at + 2 * ROWS]
        packed[at + 2 * ROWS : at + BLOCK] = line


def solve_small(lines):
    total = jnp.sum(lines, axis=0, keepdims=True)
    g00, g01, g02, g11, g12, g22, k22 = (total[:, i : i + 1] for i in range(7))
    gram = ((g00, g01, g02), (g01, g11, g12), (g02, g12, g22))
    k11, k12 = 0.5 * (g12 + g01), 0.5 * (g22 + g02)
    shifted = ((g01, g11, g12), (g11, k11, k12), (g12, k12, k22))
    energy = [[SCALE * shifted[i][j] + SHIFT * gram[i][j] for j in range(3)] for i in range(3)]

    def form(m, v):
        return sum(v[i] * (v[i] * m[i][i] + 2.0 * sum((v[j] * m[i][j] for j in range(i + 1, len(v))), 0.0)) for i in range(len(v)))

    def ratio(num, den, low, high):
        return jnp.clip(num / jnp.maximum(den, 1e-37), low, high)

    alpha0 = g00 / energy[0][0]
    r = [1.0 - alpha0 * SHIFT, -alpha0 * SCALE]
    rr1 = jnp.maximum(form(gram, r), 0.0)
    beta = ratio(rr1, g00, 0.0, 1e4)
    p = [r[0] + beta, r[1]]
    alpha1 = ratio(rr1, form(energy, p), 0.05, 4.1)
    half = 0.5 * SCALE * p[1]
    image = [half + SHIFT * p[0], SCALE * p[0] + SHIFT * p[1], half]
    x = [alpha0 + alpha1 * p[0], alpha1 * p[1]]
    r = [r[0] - alpha1 * image[0], r[1] - alpha1 * image[1], -alpha1 * image[2]]
    rr2 = jnp.maximum(form(gram, r), 0.0)
    beta = ratio(rr2, rr1, 0.0, 1e4)
    p = [r[0] + beta * p[0], r[1] + beta * p[1], r[2]]
    alpha2 = ratio(rr2, form(energy, p), 0.05, 4.1)
    return x[0] + alpha2 * p[0], x[1] + alpha2 * p[1], alpha2 * p[2]


PAIRS = ((0, 0), (0, 1), (0, 2), (1, 1), (1, 2), (2, 2))
SPAN = ROWS + 2 * HALO
EDGE = 8


def deposit_kernel(layers, own, before, after, bins, w0_out, w1_out, w2_out, heats):
    spokes = bins.shape[-1]
    fields, _, inside, (c_down, c_right, c_left) = basis(before, own, after)
    for out, w in zip((w0_out, w1_out, w2_out), fields):
        out[...] = w[ROWS : 2 * ROWS]
    shape = inside.shape
    col = lax.broadcasted_iota(jnp.int32, shape, 1)
    last, first = col == shape[1] - 1, col == 0
    fields = [w * inside for w in fields]
    falls = [w - below(w) for w in fields]
    steps = [w - jnp.where(last, 0.0, right(w)) for w in fields]
    wanted = slice(ROWS - HALO, ROWS - HALO + SPAN)
    for pair, (i, j) in enumerate(PAIRS):
        q_down = c_down * (falls[i] * falls[j])
        q_right = c_right * (steps[i] * steps[j])
        q_left = jnp.where(first, c_left * (fields[i] * fields[j]), left(q_right))
        joule = (q_down + above(q_down)) + (q_right + q_left)
        factor = heat_factor if i == j else 2.0 * heat_factor
        joule = factor * joule[wanted]
        for part in range(heats.shape[0]):
            heats[part, SPAN * pair : SPAN * (pair + 1)] = joule[:, 128 * part : 128 * (part + 1)]
    for part in range(heats.shape[0]):
        heats[part, SPAN * len(PAIRS) :] = jnp.zeros((SPAN * (8 - len(PAIRS)), 128), jnp.float32)
    part = slice(3 * ROWS, 4 * ROWS)
    cell = jnp.concatenate([before[part], own[part], after[part]], axis=0)[wanted].astype(jnp.int32)
    azimuth = cell & (spokes - 1)
    outermost = jnp.where(cell >= (layers - 1) * spokes, 1.0, 0.0)
    spoke = lax.broadcasted_iota(jnp.int32, (spokes, shape[1]), 0)
    for row in range(1, SPAN - 1):
        pick = jnp.where(azimuth[row : row + 1] == spoke, 1.0, 0.0).astype(jnp.bfloat16)
        joule = jnp.concatenate([heats[part, pl.ds(row, 8, stride=SPAN), :] for part in range(heats.shape[0])], axis=1)
        upper = joule * outermost[row : row + 1]
        pieces = []
        for part in (joule - upper, upper):
            for _ in range(3):
                piece = part.astype(jnp.bfloat16)
                part = part - piece.astype(jnp.float32)
                pieces.append(piece)
        total = lax.dot_general(
            jnp.concatenate(pieces, axis=0), pick, (((1,), (1,)), ((), ())), preferred_element_type=jnp.float32
        )
        bins[row, 0:8] = total[0:8] + (total[8:16] + total[16:24])
        bins[row, 8:16] = total[24:32] + (total[32:40] + total[40:48])


def substep_rows(rows, layers, warm, cond, base, done):
    body = slice(EDGE, EDGE + layers)
    inward, outward = slice(EDGE - 1, EDGE - 1 + layers), slice(EDGE + 1, EDGE + 1 + layers)

    def conductivity(row):
        t = warm[row, body]
        k = base[row] * (1.0 + diffusivity_derivative * t)
        cond[row, body] = k
        return t, k

    def between(t, k, t_other, k_other):
        return (k + k_other) * (t_other - t)

    below_row = conductivity(rows[0] - 1)
    here = conductivity(rows[0])
    inner = between(*below_row, *here)
    for row in rows:
        t, k = here
        here = conductivity(row + 1)
        outer = between(t, k, *here)
        flux = outer - inner
        inner = outer
        flux = flux + between(t, k, warm[row, inward], cond[row, inward])
        flux = flux + between(t, k, warm[row, outward], cond[row, outward])
        face = between(t, k, right(t), right(k))
        done(row, t, flux + (face - left(face)))


def clear_edges(layers, *fields):
    for field in fields:
        blank = jnp.zeros((EDGE, field.shape[-1]), jnp.float32)
        field[0:EDGE] = blank
        field[EDGE + layers : 2 * EDGE + layers] = blank


def first_kernel(layers, own, before, after, fresh, base, store, warm, cond):
    block = own.shape[0] // layers
    index, count = place()
    body = slice(EDGE, EDGE + layers)
    for row in range(SPAN):
        source, at, there = own, row - HALO, 1.0
        if row < HALO:
            source, at, there = before, row + ROWS - HALO, jnp.where(index > 0, 1.0, 0.0)
        elif row >= HALO + ROWS:
            source, at, there = after, row - HALO - ROWS, jnp.where(index < count - 1, 1.0, 0.0)
        kind = source[pl.ds(ROWS + at, layers, stride=block), :]

        def table(values):
            return jnp.where(kind == 0.0, values[0], jnp.where(kind == 1.0, values[1], jnp.where(kind == 2.0, values[2], values[3])))

        base[row] = table(conduct_table) * there
        store[row] = table([0.5 * time_step / c for c in capacity_table]) * there
        warm[row, body] = source[pl.ds(at, layers, stride=block), :]
        clear_edges(layers, warm.at[row], cond.at[row], fresh.at[row])

    def done(row, t, flux):
        fresh[row, body] = t + store[row] * flux

    substep_rows(range(1, SPAN - 1), layers, warm, cond, base, done)


def heat_kernel(layers, lines, w0, w1, w2, bins, fresh, base, store, potential, heated, warm, cond):
    spokes = heated.shape[-1]
    body = slice(EDGE, EDGE + layers)
    f = solve_small(lines[...])
    potential[...] = f[0] * w0[...] + f[1] * w1[...] + f[2] * w2[...]
    sublane = lax.broadcasted_iota(jnp.int32, (8, spokes), 0)
    weight = jnp.zeros((8, spokes), jnp.float32)
    for pair, (i, j) in enumerate(PAIRS):
        weight = jnp.where(sublane == pair, f[i] * f[j], weight)
    weight = 2.0 * weight
    heat = {}
    top = slice(layers - 8, layers)
    for row in range(1, SPAN - 1):
        inner = jnp.sum(weight * bins[row, 0:8], axis=0, keepdims=True)
        outer = jnp.sum(weight * bins[row, 8:16], axis=0, keepdims=True)
        heat[row] = jnp.where(sublane == 6, inner, jnp.where(sublane == 7, outer, 0.0))
        warm[1, row] = fresh[row]
        warm[1, row, EDGE + layers - 8 : EDGE + layers] = fresh[row, EDGE + layers - 8 : EDGE + layers] + store[row, top] * heat[row]
        clear_edges(layers, warm.at[0, row], cond.at[row])

    for substep in range(1, SUBSTEPS):

        def done(row, t, flux):
            flux = jnp.concatenate([flux[: layers - 8], flux[top] + heat[row]], axis=0)
            t = t + store[row] * flux
            if substep + 1 < SUBSTEPS:
                warm[1 - substep % 2, row, body] = t
            else:
                heated[pl.ds(row - HALO, layers, stride=ROWS), :] = t

        substep_rows(range(substep + 1, SPAN - 1 - substep), layers, warm.at[substep % 2], cond, base, done)


def local(foil_warmth, terminal_voltage_input, foil_segment_pattern, underlying_block_map, prior_block_warmth, substance_kind):
    f32 = jnp.float32
    magnets, layers = lax.axis_size("magnet"), lax.axis_size("slab")
    count = magnets * layers
    width, spokes = foil_warmth.shape[1], prior_block_warmth.shape[2]
    onward = [(i, i + 1) for i in range(count - 1)]
    backward = [(i + 1, i) for i in range(count - 1)]

    def call(kernel, name, shapes, *operands, scratch=(), spaces=None, cost=None, room=8 << 20):
        return pl.pallas_call(
            kernel,
            out_shape=tuple(jax.ShapeDtypeStruct(dims, f32) for dims in shapes),
            in_specs=[pl.BlockSpec(memory_space=spaces or pltpu.VMEM)] * len(operands),
            out_specs=(pl.BlockSpec(memory_space=pltpu.VMEM),) * len(shapes),
            scratch_shapes=scratch,
            cost_estimate=cost,
            compiler_params=pltpu.CompilerParams(vmem_limit_bytes=room),
            name=name,
        )(*operands)

    rows = (ROWS, width)
    (sheet,) = call(
        sheet_kernel,
        "sheet",
        [(4 * ROWS, width)],
        foil_warmth,
        terminal_voltage_input,
        foil_segment_pattern,
        underlying_block_map,
        scratch=[pltpu.VMEM(rows, jnp.int32), pltpu.VMEM(rows, jnp.int32), pltpu.SemaphoreType.DMA((4,))],
        spaces=pltpu.HBM,
        room=66846720,
    )
    before = lax.ppermute(sheet, BOTH, onward)
    stack = (layers * BLOCK, spokes)
    (packed,) = call(
        pack_kernel, "pack", [stack], prior_block_warmth.reshape(-1, spokes), substance_kind.reshape(-1, spokes)
    )
    (packed,) = call(gram_kernel, "gram", [stack], sheet, before, packed)

    packed, later = lax.optimization_barrier((packed, sheet))
    bricks = lax.all_to_all(packed.reshape(layers, BLOCK, 1, spokes), "slab", 0, 0)
    after = lax.ppermute(later, BOTH, backward)
    bins, *fields = call(
        functools.partial(deposit_kernel, layers),
        "deposit",
        [(SPAN, 16, spokes), rows, rows, rows],
        sheet,
        before,
        after,
        scratch=[pltpu.VMEM((width // 128, 8 * SPAN, 128), f32)],
        cost=pl.CostEstimate(flops=10**8, bytes_accessed=2 * 10**6, transcendentals=0),
    )
    lines = jnp.sum(bricks[:, 2 * ROWS], axis=0, keepdims=True)
    lines = jnp.broadcast_to(lines, (magnets, 1, spokes))
    lines, bricks, bins = lax.optimization_barrier((lines, bricks.reshape(stack), bins))
    lines = lax.all_to_all(lines, "magnet", 0, 0).reshape(magnets, spokes)

    padded = (SPAN, layers + 2 * EDGE, spokes)
    plain = (SPAN, layers, spokes)
    stage = call(
        functools.partial(first_kernel, layers),
        "first",
        [padded, plain, plain],
        bricks,
        lax.ppermute(bricks, BOTH, onward),
        lax.ppermute(bricks, BOTH, backward),
        scratch=[pltpu.VMEM(padded, f32), pltpu.VMEM(padded, f32)],
        cost=pl.CostEstimate(flops=10**7, bytes_accessed=2 * 10**6, transcendentals=0),
    )
    potential, heated = call(
        functools.partial(heat_kernel, layers),
        "heat",
        [rows, (layers * ROWS, spokes)],
        lines,
        *fields,
        bins,
        *stage,
        scratch=[pltpu.VMEM((2,) + padded, f32), pltpu.VMEM(padded, f32)],
    )
    heated = lax.all_to_all(heated.reshape(layers, ROWS, spokes), "slab", 0, 0)
    return potential, heated.reshape(prior_block_warmth.shape)


def solution(mesh):
    placed = (
        P(("magnet", "slab"), None),
        P(("magnet", "slab"), None),
        P(("magnet", "slab"), None),
        P("magnet", None),
        P("slab", "magnet", None),
        P("slab", "magnet", None),
    )
    return jax.shard_map(
        local,
        mesh=mesh,
        in_specs=placed,
        out_specs=(P(("magnet", "slab"), None), P("slab", "magnet", None)),
        check_vma=False,
    )
```

```python
import functools

import jax
import jax.numpy as jnp
from jax import lax
from jax.experimental import pallas as pl
from jax.experimental.pallas import tpu as pltpu
from jax.sharding import PartitionSpec as P

SUBSTEPS = 4
HALO = SUBSTEPS
ROWS = 8

leak_diag = 0.25
contact_gain = 4.0
copper_factor = 3.0
sheet_slope = 0.5
heat_factor = 1.5
time_step = 0.03
conduct_table = (0.3, 1.0, 2.0, 0.6)
capacity_table = (1.0, 1.5, 2.0, 1.2)
diffusivity_derivative = 0.4

SHIFT = 9.85
SCALE = 9.6
BOTH = ("magnet", "slab")
BLOCK = 2 * ROWS + 1


def place():
    size = lax.axis_size("slab")
    return lax.axis_index("magnet") * size + lax.axis_index("slab"), lax.axis_size("magnet") * size


def above(v):
    return pltpu.roll(v, 1, 0)


def below(v):
    return pltpu.roll(v, v.shape[0] - 1, 0)


def left(v):
    return pltpu.roll(v, 1, 1)


def right(v):
    return pltpu.roll(v, v.shape[1] - 1, 1)


def rows_inside(shape, margin):
    index, count = place()
    row = lax.broadcasted_iota(jnp.int32, shape, 0)
    low = jnp.where(index > 0, 0, margin)
    high = jnp.where(index < count - 1, shape[0], shape[0] - margin)
    return jnp.where((row >= low) & (row < high), 1.0, 0.0).astype(jnp.float32)


def sheet_kernel(warmth, voltage, pattern, cells, sheet, pattern_here, cells_here, sems):
    at = pl.multiple_of(lax.axis_index("slab") * ROWS, ROWS)
    copies = [
        pltpu.make_async_copy(pattern, pattern_here, sems.at[0]),
        pltpu.make_async_copy(cells.at[pl.ds(at, ROWS)], cells_here, sems.at[1]),
        pltpu.make_async_copy(warmth, sheet.at[0:ROWS], sems.at[2]),
        pltpu.make_async_copy(voltage, sheet.at[ROWS : 2 * ROWS], sems.at[3]),
    ]
    for copy in copies:
        copy.start()
    copies[0].wait()
    sheet[2 * ROWS : 3 * ROWS] = pattern_here[...].astype(jnp.float32)
    copies[1].wait()
    sheet[3 * ROWS : 4 * ROWS] = cells_here[...].astype(jnp.float32)
    copies[2].wait()
    copies[3].wait()


def pack_kernel(warmth, kind, packed):
    for slab in range(packed.shape[0] // BLOCK):
        part = slice(ROWS * slab, ROWS * (slab + 1))
        at = BLOCK * slab
        packed[at : at + ROWS] = warmth[part]
        packed[at + ROWS : at + 2 * ROWS] = kind[part].astype(jnp.float32)
        packed[at + 2 * ROWS : at + BLOCK] = jnp.zeros((1, packed.shape[1]), jnp.float32)


def sides(index, mate, cross):
    even = index % 2 == 0
    return jnp.where(even, cross, mate), jnp.where(even, mate, cross)


def window_of(own, mate, cross, i):
    part = slice(ROWS * i, ROWS * (i + 1))
    before, after = sides(place()[0], mate[part], cross[part])
    return jnp.concatenate([before, own[part], after], axis=0)


def basis(own, mate, cross):
    def window(i):
        return window_of(own, mate, cross, i)

    warmth, voltage, pattern = window(0), window(1), window(2)
    shape = warmth.shape
    inside = rows_inside(shape, ROWS)
    col = lax.broadcasted_iota(jnp.int32, shape, 1)
    last = col == shape[1] - 1
    sigma = inside * jnp.where(pattern == 1.0, copper_factor, 1.0) / (1.0 + sheet_slope * warmth)
    contact = jnp.where(pattern == 2.0, contact_gain, 0.0)
    c_down = 0.5 * (sigma + below(sigma))
    c_right = 0.5 * (sigma + jnp.where(last, 0.0, right(sigma)))
    c_left = jnp.where(col == 0, 0.5 * sigma, left(c_right))
    diagonal = leak_diag + contact + above(c_down) + c_down + c_left + c_right
    diagonal = (diagonal - SHIFT) * (1.0 / SCALE)
    o_down = c_down * inside * below(inside) * (1.0 / SCALE)
    o_up = above(o_down)
    o_right = jnp.where(last, 0.0, c_right) * (1.0 / SCALE)
    o_left = left(o_right)

    def apply(v):
        return diagonal * v - (o_up * above(v) + o_down * below(v)) - (o_left * left(v) + o_right * right(v))

    w0 = contact * voltage
    w1 = apply(w0)
    w2 = 2.0 * apply(w1) - w0
    return (w0, w1, w2), apply, inside, (c_down, c_right, c_left)


def gram_kernel(own, mate, cross, packed_in, packed):
    (w0, w1, w2), apply, _, _ = basis(own, mate, cross)
    w0, w1, w2, w3 = (w[ROWS : 2 * ROWS] for w in (w0, w1, w2, apply(w2)))
    lane = lax.broadcasted_iota(jnp.int32, (1, 128), 1)
    line = jnp.zeros((1, 128), jnp.float32)
    for i, (u, v) in enumerate(((w0, w0), (w0, w1), (w0, w2), (w1, w1), (w1, w2), (w2, w2), (w2, w3))):
        line = jnp.where(lane == i, jnp.sum(u * v, keepdims=True), line)
    for slab in range(packed.shape[0] // BLOCK):
        at = BLOCK * slab
        packed[at : at + 2 * ROWS] = packed_in[at : at + 2 * ROWS]
        packed[at + 2 * ROWS : at + BLOCK] = line


def solve_small(lines):
    total = jnp.sum(lines, axis=0, keepdims=True)
    g00, g01, g02, g11, g12, g22, k22 = (total[:, i : i + 1] for i in range(7))
    gram = ((g00, g01, g02), (g01, g11, g12), (g02, g12, g22))
    k11, k12 = 0.5 * (g12 + g01), 0.5 * (g22 + g02)
    shifted = ((g01, g11, g12), (g11, k11, k12), (g12, k12, k22))
    energy = [[SCALE * shifted[i][j] + SHIFT * gram[i][j] for j in range(3)] for i in range(3)]

    def form(m, v):
        return sum(v[i] * (v[i] * m[i][i] + 2.0 * sum((v[j] * m[i][j] for j in range(i + 1, len(v))), 0.0)) for i in range(len(v)))

    def ratio(num, den, low, high):
        return jnp.clip(num / jnp.maximum(den, 1e-37), low, high)

    alpha0 = g00 / energy[0][0]
    r = [1.0 - alpha0 * SHIFT, -alpha0 * SCALE]
    rr1 = jnp.maximum(form(gram, r), 0.0)
    beta = ratio(rr1, g00, 0.0, 1e4)
    p = [r[0] + beta, r[1]]
    alpha1 = ratio(rr1, form(energy, p), 0.05, 4.1)
    half = 0.5 * SCALE * p[1]
    image = [half + SHIFT * p[0], SCALE * p[0] + SHIFT * p[1], half]
    x = [alpha0 + alpha1 * p[0], alpha1 * p[1]]
    r = [r[0] - alpha1 * image[0], r[1] - alpha1 * image[1], -alpha1 * image[2]]
    rr2 = jnp.maximum(form(gram, r), 0.0)
    beta = ratio(rr2, rr1, 0.0, 1e4)
    p = [r[0] + beta * p[0], r[1] + beta * p[1], r[2]]
    alpha2 = ratio(rr2, form(energy, p), 0.05, 4.1)
    return x[0] + alpha2 * p[0], x[1] + alpha2 * p[1], alpha2 * p[2]


PAIRS = ((0, 0), (0, 1), (0, 2), (1, 1), (1, 2), (2, 2))
SPAN = ROWS + 2 * HALO
EDGE = 8


def deposit_kernel(layers, own, mate, cross, bins, w0_out, w1_out, w2_out, heats):
    spokes = bins.shape[-1]
    fields, _, inside, (c_down, c_right, c_left) = basis(own, mate, cross)
    for out, w in zip((w0_out, w1_out, w2_out), fields):
        out[...] = w[ROWS : 2 * ROWS]
    shape = inside.shape
    col = lax.broadcasted_iota(jnp.int32, shape, 1)
    last, first = col == shape[1] - 1, col == 0
    fields = [w * inside for w in fields]
    falls = [w - below(w) for w in fields]
    steps = [w - jnp.where(last, 0.0, right(w)) for w in fields]
    wanted = slice(ROWS - HALO, ROWS - HALO + SPAN)
    for pair, (i, j) in enumerate(PAIRS):
        q_down = c_down * (falls[i] * falls[j])
        q_right = c_right * (steps[i] * steps[j])
        q_left = jnp.where(first, c_left * (fields[i] * fields[j]), left(q_right))
        joule = (q_down + above(q_down)) + (q_right + q_left)
        factor = heat_factor if i == j else 2.0 * heat_factor
        joule = factor * joule[wanted]
        for part in range(heats.shape[0]):
            heats[part, SPAN * pair : SPAN * (pair + 1)] = joule[:, 128 * part : 128 * (part + 1)]
    for part in range(heats.shape[0]):
        heats[part, SPAN * len(PAIRS) :] = jnp.zeros((SPAN * (8 - len(PAIRS)), 128), jnp.float32)
    cell = window_of(own, mate, cross, 3)[wanted].astype(jnp.int32)
    azimuth = cell & (spokes - 1)
    outermost = jnp.where(cell >= (layers - 1) * spokes, 1.0, 0.0)
    spoke = lax.broadcasted_iota(jnp.int32, (spokes, shape[1]), 0)
    for row in range(1, SPAN - 1):
        pick = jnp.where(azimuth[row : row + 1] == spoke, 1.0, 0.0).astype(jnp.bfloat16)
        joule = jnp.concatenate([heats[part, pl.ds(row, 8, stride=SPAN), :] for part in range(heats.shape[0])], axis=1)
        upper = joule * outermost[row : row + 1]
        pieces = []
        for part in (joule - upper, upper):
            for _ in range(3):
                piece = part.astype(jnp.bfloat16)
                part = part - piece.astype(jnp.float32)
                pieces.append(piece)
        total = lax.dot_general(
            jnp.concatenate(pieces, axis=0), pick, (((1,), (1,)), ((), ())), preferred_element_type=jnp.float32
        )
        bins[row, 0:8] = total[0:8] + (total[8:16] + total[16:24])
        bins[row, 8:16] = total[24:32] + (total[32:40] + total[40:48])


def substep_rows(rows, layers, warm, cond, base, done):
    body = slice(EDGE, EDGE + layers)
    inward, outward = slice(EDGE - 1, EDGE - 1 + layers), slice(EDGE + 1, EDGE + 1 + layers)

    def conductivity(row):
        t = warm[row, body]
        k = base[row] * (1.0 + diffusivity_derivative * t)
        cond[row, body] = k
        return t, k

    def between(t, k, t_other, k_other):
        return (k + k_other) * (t_other - t)

    below_row = conductivity(rows[0] - 1)
    here = conductivity(rows[0])
    inner = between(*below_row, *here)
    for row in rows:
        t, k = here
        here = conductivity(row + 1)
        outer = between(t, k, *here)
        flux = outer - inner
        inner = outer
        flux = flux + between(t, k, warm[row, inward], cond[row, inward])
        flux = flux + between(t, k, warm[row, outward], cond[row, outward])
        face = between(t, k, right(t), right(k))
        done(row, t, flux + (face - left(face)))


def clear_edges(layers, *fields):
    for field in fields:
        blank = jnp.zeros((EDGE, field.shape[-1]), jnp.float32)
        field[0:EDGE] = blank
        field[EDGE + layers : 2 * EDGE + layers] = blank


def first_kernel(layers, own, mate, cross, fresh, base, store, warm, cond):
    block = own.shape[0] // layers
    index, count = place()
    body = slice(EDGE, EDGE + layers)
    for row in range(SPAN):

        def rows_of(first):
            if HALO <= row < HALO + ROWS:
                return own[pl.ds(first + row - HALO, layers, stride=block), :]
            at = first + (row + ROWS - HALO) % ROWS
            return sides(index, *(ref[pl.ds(at, layers, stride=block), :] for ref in (mate, cross)))[int(row >= HALO)]

        there = 1.0
        if row < HALO:
            there = jnp.where(index > 0, 1.0, 0.0)
        elif row >= HALO + ROWS:
            there = jnp.where(index < count - 1, 1.0, 0.0)
        kind = rows_of(ROWS)

        def table(values):
            return jnp.where(kind == 0.0, values[0], jnp.where(kind == 1.0, values[1], jnp.where(kind == 2.0, values[2], values[3])))

        base[row] = table(conduct_table) * there
        store[row] = table([0.5 * time_step / c for c in capacity_table]) * there
        warm[row, body] = rows_of(0)
        clear_edges(layers, warm.at[row], cond.at[row], fresh.at[row])

    def done(row, t, flux):
        fresh[row, body] = t + store[row] * flux

    substep_rows(range(1, SPAN - 1), layers, warm, cond, base, done)


def heat_kernel(layers, lines, w0, w1, w2, bins, fresh, base, store, potential, heated, warm, cond):
    spokes = heated.shape[-1]
    body = slice(EDGE, EDGE + layers)
    f = solve_small(lines[...])
    potential[...] = f[0] * w0[...] + f[1] * w1[...] + f[2] * w2[...]
    sublane = lax.broadcasted_iota(jnp.int32, (8, spokes), 0)
    weight = jnp.zeros((8, spokes), jnp.float32)
    for pair, (i, j) in enumerate(PAIRS):
        weight = jnp.where(sublane == pair, f[i] * f[j], weight)
    weight = 2.0 * weight
    heat = {}
    top = slice(layers - 8, layers)
    for row in range(1, SPAN - 1):
        inner = jnp.sum(weight * bins[row, 0:8], axis=0, keepdims=True)
        outer = jnp.sum(weight * bins[row, 8:16], axis=0, keepdims=True)
        heat[row] = jnp.where(sublane == 6, inner, jnp.where(sublane == 7, outer, 0.0))
        warm[1, row] = fresh[row]
        warm[1, row, EDGE + layers - 8 : EDGE + layers] = fresh[row, EDGE + layers - 8 : EDGE + layers] + store[row, top] * heat[row]
        clear_edges(layers, warm.at[0, row], cond.at[row])

    for substep in range(1, SUBSTEPS):

        def done(row, t, flux):
            flux = jnp.concatenate([flux[: layers - 8], flux[top] + heat[row]], axis=0)
            t = t + store[row] * flux
            if substep + 1 < SUBSTEPS:
                warm[1 - substep % 2, row, body] = t
            else:
                heated[pl.ds(row - HALO, layers, stride=ROWS), :] = t

        substep_rows(range(substep + 1, SPAN - 1 - substep), layers, warm.at[substep % 2], cond, base, done)


def local(foil_warmth, terminal_voltage_input, foil_segment_pattern, underlying_block_map, prior_block_warmth, substance_kind):
    f32 = jnp.float32
    magnets, layers = lax.axis_size("magnet"), lax.axis_size("slab")
    count = magnets * layers
    width, spokes = foil_warmth.shape[1], prior_block_warmth.shape[2]
    mates = [(i, i ^ 1) for i in range(count)]
    crossing = [(i, i + 1) for i in range(1, count - 1, 2)] + [(i + 1, i) for i in range(1, count - 1, 2)]

    def exchange(array):
        return lax.ppermute(array, BOTH, mates), lax.ppermute(array, BOTH, crossing)

    def call(kernel, name, shapes, *operands, scratch=(), spaces=None, cost=None, room=8 << 20):
        return pl.pallas_call(
            kernel,
            out_shape=tuple(jax.ShapeDtypeStruct(dims, f32) for dims in shapes),
            in_specs=[pl.BlockSpec(memory_space=spaces or pltpu.VMEM)] * len(operands),
            out_specs=(pl.BlockSpec(memory_space=pltpu.VMEM),) * len(shapes),
            scratch_shapes=scratch,
            cost_estimate=cost,
            compiler_params=pltpu.CompilerParams(vmem_limit_bytes=room),
            name=name,
        )(*operands)

    rows = (ROWS, width)
    (sheet,) = call(
        sheet_kernel,
        "sheet",
        [(4 * ROWS, width)],
        foil_warmth,
        terminal_voltage_input,
        foil_segment_pattern,
        underlying_block_map,
        scratch=[pltpu.VMEM(rows, jnp.int32), pltpu.VMEM(rows, jnp.int32), pltpu.SemaphoreType.DMA((4,))],
        spaces=pltpu.HBM,
        room=66846720,
    )
    around = exchange(sheet)
    stack = (layers * BLOCK, spokes)
    (packed,) = call(
        pack_kernel, "pack", [stack], prior_block_warmth.reshape(-1, spokes), substance_kind.reshape(-1, spokes)
    )
    (packed,) = call(gram_kernel, "gram", [stack], sheet, *around, packed)

    bricks = lax.all_to_all(packed.reshape(layers, BLOCK, 1, spokes), "slab", 0, 0)
    bins, *fields = call(
        functools.partial(deposit_kernel, layers),
        "deposit",
        [(SPAN, 16, spokes), rows, rows, rows],
        sheet,
        *around,
        scratch=[pltpu.VMEM((width // 128, 8 * SPAN, 128), f32)],
        cost=pl.CostEstimate(flops=10**8, bytes_accessed=2 * 10**6, transcendentals=0),
    )
    lines = jnp.sum(bricks[:, 2 * ROWS], axis=0, keepdims=True)
    lines = jnp.broadcast_to(lines, (magnets, 1, spokes))
    lines, bricks, bins = lax.optimization_barrier((lines, bricks.reshape(stack), bins))
    lines = lax.all_to_all(lines, "magnet", 0, 0).reshape(magnets, spokes)

    padded = (SPAN, layers + 2 * EDGE, spokes)
    plain = (SPAN, layers, spokes)
    stage = call(
        functools.partial(first_kernel, layers),
        "first",
        [padded, plain, plain],
        bricks,
        *exchange(bricks),
        scratch=[pltpu.VMEM(padded, f32), pltpu.VMEM(padded, f32)],
        cost=pl.CostEstimate(flops=10**7, bytes_accessed=2 * 10**6, transcendentals=0),
    )
    potential, heated = call(
        functools.partial(heat_kernel, layers),
        "heat",
        [rows, (layers * ROWS, spokes)],
        lines,
        *fields,
        bins,
        *stage,
        scratch=[pltpu.VMEM((2,) + padded, f32), pltpu.VMEM(padded, f32)],
    )
    heated = lax.all_to_all(heated.reshape(layers, ROWS, spokes), "slab", 0, 0)
    return potential, heated.reshape(prior_block_warmth.shape)


def solution(mesh):
    placed = (
        P(("magnet", "slab"), None),
        P(("magnet", "slab"), None),
        P(("magnet", "slab"), None),
        P("magnet", None),
        P("slab", "magnet", None),
        P("slab", "magnet", None),
    )
    return jax.shard_map(
        local,
        mesh=mesh,
        in_specs=placed,
        out_specs=(P(("magnet", "slab"), None), P("slab", "magnet", None)),
        check_vma=False,
    )
```

```python
import functools

import jax
import jax.numpy as jnp
from jax import lax
from jax.experimental import pallas as pl
from jax.experimental.pallas import tpu as pltpu
from jax.sharding import PartitionSpec as P

SUBSTEPS = 4
HALO = SUBSTEPS
ROWS = 8

leak_diag = 0.25
contact_gain = 4.0
copper_factor = 3.0
sheet_slope = 0.5
heat_factor = 1.5
time_step = 0.03
conduct_table = (0.3, 1.0, 2.0, 0.6)
capacity_table = (1.0, 1.5, 2.0, 1.2)
diffusivity_derivative = 0.4

SHIFT = 9.85
SCALE = 9.6
BOTH = ("magnet", "slab")
BLOCK = 2 * ROWS + 1


def place():
    size = lax.axis_size("slab")
    return lax.axis_index("magnet") * size + lax.axis_index("slab"), lax.axis_size("magnet") * size


def above(v):
    return pltpu.roll(v, 1, 0)


def below(v):
    return pltpu.roll(v, v.shape[0] - 1, 0)


def left(v):
    return pltpu.roll(v, 1, 1)


def right(v):
    return pltpu.roll(v, v.shape[1] - 1, 1)


def rows_inside(shape, margin):
    index, count = place()
    row = lax.broadcasted_iota(jnp.int32, shape, 0)
    low = jnp.where(index > 0, 0, margin)
    high = jnp.where(index < count - 1, shape[0], shape[0] - margin)
    return jnp.where((row >= low) & (row < high), 1.0, 0.0).astype(jnp.float32)


def sheet_kernel(warmth, voltage, pattern, cells, sheet, pattern_here, cells_here, sems):
    at = pl.multiple_of(lax.axis_index("slab") * ROWS, ROWS)
    copies = [
        pltpu.make_async_copy(pattern, pattern_here, sems.at[0]),
        pltpu.make_async_copy(cells.at[pl.ds(at, ROWS)], cells_here, sems.at[1]),
        pltpu.make_async_copy(warmth, sheet.at[0:ROWS], sems.at[2]),
        pltpu.make_async_copy(voltage, sheet.at[ROWS : 2 * ROWS], sems.at[3]),
    ]
    for copy in copies:
        copy.start()
    copies[0].wait()
    sheet[2 * ROWS : 3 * ROWS] = pattern_here[...].astype(jnp.float32)
    copies[1].wait()
    sheet[3 * ROWS : 4 * ROWS] = cells_here[...].astype(jnp.float32)
    copies[2].wait()
    copies[3].wait()


def pack_kernel(warmth, kind, packed):
    for slab in range(packed.shape[0] // BLOCK):
        part = slice(ROWS * slab, ROWS * (slab + 1))
        at = BLOCK * slab
        packed[at : at + ROWS] = warmth[part]
        packed[at + ROWS : at + 2 * ROWS] = kind[part].astype(jnp.float32)
        packed[at + 2 * ROWS : at + BLOCK] = jnp.zeros((1, packed.shape[1]), jnp.float32)


def sides(index, mate, cross):
    even = index % 2 == 0
    return jnp.where(even, cross, mate), jnp.where(even, mate, cross)


def window_of(own, mate, cross, i):
    part = slice(ROWS * i, ROWS * (i + 1))
    before, after = sides(place()[0], mate[part], cross[part])
    return jnp.concatenate([before, own[part], after], axis=0)


def basis(own, mate, cross):
    def window(i):
        return window_of(own, mate, cross, i)

    warmth, voltage, pattern = window(0), window(1), window(2)
    shape = warmth.shape
    inside = rows_inside(shape, ROWS)
    col = lax.broadcasted_iota(jnp.int32, shape, 1)
    last = col == shape[1] - 1
    sigma = inside * jnp.where(pattern == 1.0, copper_factor, 1.0) / (1.0 + sheet_slope * warmth)
    contact = jnp.where(pattern == 2.0, contact_gain, 0.0)
    c_down = 0.5 * (sigma + below(sigma))
    c_right = 0.5 * (sigma + jnp.where(last, 0.0, right(sigma)))
    c_left = jnp.where(col == 0, 0.5 * sigma, left(c_right))
    diagonal = leak_diag + contact + above(c_down) + c_down + c_left + c_right
    diagonal = (diagonal - SHIFT) * (1.0 / SCALE)
    o_down = c_down * inside * below(inside) * (1.0 / SCALE)
    o_up = above(o_down)
    o_right = jnp.where(last, 0.0, c_right) * (1.0 / SCALE)
    o_left = left(o_right)

    def apply(v):
        return diagonal * v - (o_up * above(v) + o_down * below(v)) - (o_left * left(v) + o_right * right(v))

    w0 = contact * voltage
    w1 = apply(w0)
    w2 = 2.0 * apply(w1) - w0
    return (w0, w1, w2), apply, inside, (c_down, c_right, c_left)


def gram_kernel(own, mate, cross, packed_in, packed):
    (w0, w1, w2), apply, _, _ = basis(own, mate, cross)
    w0, w1, w2, w3 = (w[ROWS : 2 * ROWS] for w in (w0, w1, w2, apply(w2)))
    lane = lax.broadcasted_iota(jnp.int32, (1, 128), 1)
    line = jnp.zeros((1, 128), jnp.float32)
    for i, (u, v) in enumerate(((w0, w0), (w0, w1), (w0, w2), (w1, w1), (w1, w2), (w2, w2), (w2, w3))):
        line = jnp.where(lane == i, jnp.sum(u * v, keepdims=True), line)
    for slab in range(packed.shape[0] // BLOCK):
        at = BLOCK * slab
        packed[at : at + 2 * ROWS] = packed_in[at : at + 2 * ROWS]
        packed[at + 2 * ROWS : at + BLOCK] = line


def solve_small(lines):
    total = jnp.sum(lines, axis=0, keepdims=True)
    g00, g01, g02, g11, g12, g22, k22 = (total[:, i : i + 1] for i in range(7))
    gram = ((g00, g01, g02), (g01, g11, g12), (g02, g12, g22))
    k11, k12 = 0.5 * (g12 + g01), 0.5 * (g22 + g02)
    shifted = ((g01, g11, g12), (g11, k11, k12), (g12, k12, k22))
    energy = [[SCALE * shifted[i][j] + SHIFT * gram[i][j] for j in range(3)] for i in range(3)]

    def form(m, v):
        return sum(v[i] * (v[i] * m[i][i] + 2.0 * sum((v[j] * m[i][j] for j in range(i + 1, len(v))), 0.0)) for i in range(len(v)))

    def ratio(num, den, low, high):
        return jnp.clip(num / jnp.maximum(den, 1e-37), low, high)

    alpha0 = g00 / energy[0][0]
    r = [1.0 - alpha0 * SHIFT, -alpha0 * SCALE]
    rr1 = jnp.maximum(form(gram, r), 0.0)
    beta = ratio(rr1, g00, 0.0, 1e4)
    p = [r[0] + beta, r[1]]
    alpha1 = ratio(rr1, form(energy, p), 0.05, 4.1)
    half = 0.5 * SCALE * p[1]
    image = [half + SHIFT * p[0], SCALE * p[0] + SHIFT * p[1], half]
    x = [alpha0 + alpha1 * p[0], alpha1 * p[1]]
    r = [r[0] - alpha1 * image[0], r[1] - alpha1 * image[1], -alpha1 * image[2]]
    rr2 = jnp.maximum(form(gram, r), 0.0)
    beta = ratio(rr2, rr1, 0.0, 1e4)
    p = [r[0] + beta * p[0], r[1] + beta * p[1], r[2]]
    alpha2 = ratio(rr2, form(energy, p), 0.05, 4.1)
    return x[0] + alpha2 * p[0], x[1] + alpha2 * p[1], alpha2 * p[2]


PAIRS = ((0, 0), (0, 1), (0, 2), (1, 1), (1, 2), (2, 2))
SPAN = ROWS + 2 * HALO
EDGE = 8


def deposit_kernel(layers, own, mate, cross, bins, w0_out, w1_out, w2_out, heats):
    spokes = bins.shape[-1]
    fields, _, inside, (c_down, c_right, c_left) = basis(own, mate, cross)
    for out, w in zip((w0_out, w1_out, w2_out), fields):
        out[...] = w[ROWS : 2 * ROWS]
    shape = inside.shape
    col = lax.broadcasted_iota(jnp.int32, shape, 1)
    last, first = col == shape[1] - 1, col == 0
    fields = [w * inside for w in fields]
    falls = [w - below(w) for w in fields]
    steps = [w - jnp.where(last, 0.0, right(w)) for w in fields]
    wanted = slice(ROWS - HALO, ROWS - HALO + SPAN)
    for pair, (i, j) in enumerate(PAIRS):
        q_down = c_down * (falls[i] * falls[j])
        q_right = c_right * (steps[i] * steps[j])
        q_left = jnp.where(first, c_left * (fields[i] * fields[j]), left(q_right))
        joule = (q_down + above(q_down)) + (q_right + q_left)
        factor = heat_factor if i == j else 2.0 * heat_factor
        joule = factor * joule[wanted]
        for part in range(heats.shape[0]):
            heats[part, SPAN * pair : SPAN * (pair + 1)] = joule[:, 128 * part : 128 * (part + 1)]
    for part in range(heats.shape[0]):
        heats[part, SPAN * len(PAIRS) :] = jnp.zeros((SPAN * (8 - len(PAIRS)), 128), jnp.float32)
    cell = window_of(own, mate, cross, 3)[wanted].astype(jnp.int32)
    azimuth = cell & (spokes - 1)
    outermost = jnp.where(cell >= (layers - 1) * spokes, 1.0, 0.0)
    spoke = lax.broadcasted_iota(jnp.int32, (spokes, shape[1]), 0)
    for row in range(1, SPAN - 1):
        pick = jnp.where(azimuth[row : row + 1] == spoke, 1.0, 0.0).astype(jnp.bfloat16)
        joule = jnp.concatenate([heats[part, pl.ds(row, 8, stride=SPAN), :] for part in range(heats.shape[0])], axis=1)
        upper = joule * outermost[row : row + 1]
        pieces = []
        for part in (joule - upper, upper):
            for _ in range(3):
                piece = part.astype(jnp.bfloat16)
                part = part - piece.astype(jnp.float32)
                pieces.append(piece)
        total = lax.dot_general(
            jnp.concatenate(pieces, axis=0), pick, (((1,), (1,)), ((), ())), preferred_element_type=jnp.float32
        )
        bins[row, 0:8] = total[0:8] + (total[8:16] + total[16:24])
        bins[row, 8:16] = total[24:32] + (total[32:40] + total[40:48])


def substep_rows(rows, layers, warm, cond, base, done):
    body = slice(EDGE, EDGE + layers)
    inward, outward = slice(EDGE - 1, EDGE - 1 + layers), slice(EDGE + 1, EDGE + 1 + layers)

    def conductivity(row):
        t = warm[row, body]
        k = base[row] * (1.0 + diffusivity_derivative * t)
        cond[row, body] = k
        return t, k

    def between(t, k, t_other, k_other):
        return (k + k_other) * (t_other - t)

    below_row = conductivity(rows[0] - 1)
    here = conductivity(rows[0])
    inner = between(*below_row, *here)
    for row in rows:
        t, k = here
        here = conductivity(row + 1)
        outer = between(t, k, *here)
        flux = outer - inner
        inner = outer
        flux = flux + between(t, k, warm[row, inward], cond[row, inward])
        flux = flux + between(t, k, warm[row, outward], cond[row, outward])
        face = between(t, k, right(t), right(k))
        done(row, t, flux + (face - left(face)))


def clear_edges(layers, *fields):
    for field in fields:
        blank = jnp.zeros((EDGE, field.shape[-1]), jnp.float32)
        field[0:EDGE] = blank
        field[EDGE + layers : 2 * EDGE + layers] = blank


def share_kernel(layers, own, lines, for_mate, for_cross):
    mine = own[pl.ds(2 * ROWS, layers, stride=BLOCK), :]
    for magnet in range(lines.shape[0] // layers):
        lines[layers * magnet : layers * (magnet + 1)] = mine
    even = place()[0] % 2 == 0
    for layer in range(layers):
        at = BLOCK * layer

        def rows_from(first):
            return jnp.concatenate([own[at + i + first : at + i + first + HALO] for i in (0, ROWS)], axis=0)

        early, late = rows_from(0), rows_from(ROWS - HALO)
        part = slice(2 * HALO * layer, 2 * HALO * (layer + 1))
        for_mate[part] = jnp.where(even, late, early)
        for_cross[part] = jnp.where(even, early, late)


def first_kernel(layers, own, mate, cross, fresh, base, store, warm, cond):
    block = own.shape[0] // layers
    index, count = place()
    body = slice(EDGE, EDGE + layers)
    for row in range(SPAN):

        def rows_of(array):
            if HALO <= row < HALO + ROWS:
                return own[pl.ds(ROWS * array + row - HALO, layers, stride=block), :]
            at = HALO * array + row % HALO
            return sides(index, *(ref[pl.ds(at, layers, stride=2 * HALO), :] for ref in (mate, cross)))[int(row >= HALO)]

        there = 1.0
        if row < HALO:
            there = jnp.where(index > 0, 1.0, 0.0)
        elif row >= HALO + ROWS:
            there = jnp.where(index < count - 1, 1.0, 0.0)
        kind = rows_of(1)

        def table(values):
            return jnp.where(kind == 0.0, values[0], jnp.where(kind == 1.0, values[1], jnp.where(kind == 2.0, values[2], values[3])))

        base[row] = table(conduct_table) * there
        store[row] = table([0.5 * time_step / c for c in capacity_table]) * there
        warm[row, body] = rows_of(0)
        clear_edges(layers, warm.at[row], cond.at[row], fresh.at[row])

    def done(row, t, flux):
        fresh[row, body] = t + store[row] * flux

    substep_rows(range(1, SPAN - 1), layers, warm, cond, base, done)


def heat_kernel(layers, lines, w0, w1, w2, bins, fresh, base, store, potential, heated, warm, cond):
    spokes = heated.shape[-1]
    body = slice(EDGE, EDGE + layers)
    f = solve_small(lines[...])
    potential[...] = f[0] * w0[...] + f[1] * w1[...] + f[2] * w2[...]
    sublane = lax.broadcasted_iota(jnp.int32, (8, spokes), 0)
    weight = jnp.zeros((8, spokes), jnp.float32)
    for pair, (i, j) in enumerate(PAIRS):
        weight = jnp.where(sublane == pair, f[i] * f[j], weight)
    weight = 2.0 * weight
    heat = {}
    top = slice(layers - 8, layers)
    for row in range(1, SPAN - 1):
        inner = jnp.sum(weight * bins[row, 0:8], axis=0, keepdims=True)
        outer = jnp.sum(weight * bins[row, 8:16], axis=0, keepdims=True)
        heat[row] = jnp.where(sublane == 6, inner, jnp.where(sublane == 7, outer, 0.0))
        warm[1, row] = fresh[row]
        warm[1, row, EDGE + layers - 8 : EDGE + layers] = fresh[row, EDGE + layers - 8 : EDGE + layers] + store[row, top] * heat[row]
        clear_edges(layers, warm.at[0, row], cond.at[row])

    for substep in range(1, SUBSTEPS):

        def done(row, t, flux):
            flux = jnp.concatenate([flux[: layers - 8], flux[top] + heat[row]], axis=0)
            t = t + store[row] * flux
            if substep + 1 < SUBSTEPS:
                warm[1 - substep % 2, row, body] = t
            else:
                heated[pl.ds(row - HALO, layers, stride=ROWS), :] = t

        substep_rows(range(substep + 1, SPAN - 1 - substep), layers, warm.at[substep % 2], cond, base, done)


def local(foil_warmth, terminal_voltage_input, foil_segment_pattern, underlying_block_map, prior_block_warmth, substance_kind):
    f32 = jnp.float32
    magnets, layers = lax.axis_size("magnet"), lax.axis_size("slab")
    count = magnets * layers
    width, spokes = foil_warmth.shape[1], prior_block_warmth.shape[2]
    mates = [(i, i ^ 1) for i in range(count)]
    crossing = [(i, i + 1) for i in range(1, count - 1, 2)] + [(i + 1, i) for i in range(1, count - 1, 2)]

    def exchange(for_mate, for_cross):
        return lax.ppermute(for_mate, BOTH, mates), lax.ppermute(for_cross, BOTH, crossing)

    def call(kernel, name, shapes, *operands, scratch=(), spaces=None, cost=None, room=8 << 20):
        return pl.pallas_call(
            kernel,
            out_shape=tuple(jax.ShapeDtypeStruct(dims, f32) for dims in shapes),
            in_specs=[pl.BlockSpec(memory_space=spaces or pltpu.VMEM)] * len(operands),
            out_specs=(pl.BlockSpec(memory_space=pltpu.VMEM),) * len(shapes),
            scratch_shapes=scratch,
            cost_estimate=cost,
            compiler_params=pltpu.CompilerParams(vmem_limit_bytes=room),
            name=name,
        )(*operands)

    rows = (ROWS, width)
    (sheet,) = call(
        sheet_kernel,
        "sheet",
        [(4 * ROWS, width)],
        foil_warmth,
        terminal_voltage_input,
        foil_segment_pattern,
        underlying_block_map,
        scratch=[pltpu.VMEM(rows, jnp.int32), pltpu.VMEM(rows, jnp.int32), pltpu.SemaphoreType.DMA((4,))],
        spaces=pltpu.HBM,
        room=66846720,
    )
    around = exchange(sheet, sheet)
    stack = (layers * BLOCK, spokes)
    (packed,) = call(
        pack_kernel, "pack", [stack], prior_block_warmth.reshape(-1, spokes), substance_kind.reshape(-1, spokes)
    )
    (packed,) = call(gram_kernel, "gram", [stack], sheet, *around, packed)

    bricks = lax.all_to_all(packed.reshape(layers, BLOCK, 1, spokes), "slab", 0, 0)
    bins, *fields = call(
        functools.partial(deposit_kernel, layers),
        "deposit",
        [(SPAN, 16, spokes), rows, rows, rows],
        sheet,
        *around,
        scratch=[pltpu.VMEM((width // 128, 8 * SPAN, 128), f32)],
        cost=pl.CostEstimate(flops=10**8, bytes_accessed=2 * 10**6, transcendentals=0),
    )
    bricks, bins = lax.optimization_barrier((bricks.reshape(stack), bins))
    lines, *edges = call(
        functools.partial(share_kernel, layers),
        "share",
        [(magnets * layers, spokes)] + [(2 * HALO * layers, spokes)] * 2,
        bricks,
    )
    lines = lax.all_to_all(lines.reshape(magnets, layers, spokes), "magnet", 0, 0).reshape(count, spokes)

    padded = (SPAN, layers + 2 * EDGE, spokes)
    plain = (SPAN, layers, spokes)
    stage = call(
        functools.partial(first_kernel, layers),
        "first",
        [padded, plain, plain],
        bricks,
        *exchange(*edges),
        scratch=[pltpu.VMEM(padded, f32), pltpu.VMEM(padded, f32)],
        cost=pl.CostEstimate(flops=0, bytes_accessed=0, transcendentals=0),
    )
    potential, heated = call(
        functools.partial(heat_kernel, layers),
        "heat",
        [rows, (layers * ROWS, spokes)],
        lines,
        *fields,
        bins,
        *stage,
        scratch=[pltpu.VMEM((2,) + padded, f32), pltpu.VMEM(padded, f32)],
    )
    heated = lax.all_to_all(heated.reshape(layers, ROWS, spokes), "slab", 0, 0)
    return potential, heated.reshape(prior_block_warmth.shape)


def solution(mesh):
    placed = (
        P(("magnet", "slab"), None),
        P(("magnet", "slab"), None),
        P(("magnet", "slab"), None),
        P("magnet", None),
        P("slab", "magnet", None),
        P("slab", "magnet", None),
    )
    return jax.shard_map(
        local,
        mesh=mesh,
        in_specs=placed,
        out_specs=(P(("magnet", "slab"), None), P("slab", "magnet", None)),
        check_vma=False,
    )
```

```python
import functools

import jax
import jax.numpy as jnp
from jax import lax
from jax.experimental import pallas as pl
from jax.experimental.pallas import tpu as pltpu
from jax.sharding import PartitionSpec as P

SUBSTEPS = 4
HALO = SUBSTEPS
ROWS = 8

leak_diag = 0.25
contact_gain = 4.0
copper_factor = 3.0
sheet_slope = 0.5
heat_factor = 1.5
time_step = 0.03
conduct_table = (0.3, 1.0, 2.0, 0.6)
capacity_table = (1.0, 1.5, 2.0, 1.2)
diffusivity_derivative = 0.4

SHIFT = 9.85
SCALE = 9.6
BOTH = ("magnet", "slab")
BLOCK = 2 * ROWS + 1


def place():
    size = lax.axis_size("slab")
    return lax.axis_index("magnet") * size + lax.axis_index("slab"), lax.axis_size("magnet") * size


def above(v):
    return pltpu.roll(v, 1, 0)


def below(v):
    return pltpu.roll(v, v.shape[0] - 1, 0)


def left(v):
    return pltpu.roll(v, 1, 1)


def right(v):
    return pltpu.roll(v, v.shape[1] - 1, 1)


def rows_inside(shape, margin):
    index, count = place()
    row = lax.broadcasted_iota(jnp.int32, shape, 0)
    low = jnp.where(index > 0, 0, margin)
    high = jnp.where(index < count - 1, shape[0], shape[0] - margin)
    return jnp.where((row >= low) & (row < high), 1.0, 0.0).astype(jnp.float32)


def sheet_kernel(warmth, voltage, pattern, cells, sheet, pattern_here, cells_here, sems):
    at = pl.multiple_of(lax.axis_index("slab") * ROWS, ROWS)
    copies = [
        pltpu.make_async_copy(pattern, pattern_here, sems.at[0]),
        pltpu.make_async_copy(cells.at[pl.ds(at, ROWS)], cells_here, sems.at[1]),
        pltpu.make_async_copy(warmth, sheet.at[0:ROWS], sems.at[2]),
        pltpu.make_async_copy(voltage, sheet.at[ROWS : 2 * ROWS], sems.at[3]),
    ]
    for copy in copies:
        copy.start()
    copies[0].wait()
    sheet[2 * ROWS : 3 * ROWS] = pattern_here[...].astype(jnp.float32)
    copies[1].wait()
    sheet[3 * ROWS : 4 * ROWS] = cells_here[...].astype(jnp.float32)
    copies[2].wait()
    copies[3].wait()


def pack_kernel(warmth, kind, packed):
    for slab in range(packed.shape[0] // BLOCK):
        part = slice(ROWS * slab, ROWS * (slab + 1))
        at = BLOCK * slab
        packed[at : at + ROWS] = warmth[part]
        packed[at + ROWS : at + 2 * ROWS] = kind[part].astype(jnp.float32)
        packed[at + 2 * ROWS : at + BLOCK] = jnp.zeros((1, packed.shape[1]), jnp.float32)


def sides(index, mate, cross):
    even = index % 2 == 0
    return jnp.where(even, cross, mate), jnp.where(even, mate, cross)


def window_of(own, mate, cross, i):
    part = slice(ROWS * i, ROWS * (i + 1))
    before, after = sides(place()[0], mate[part], cross[part])
    return jnp.concatenate([before, own[part], after], axis=0)


def basis(own, mate, cross):
    def window(i):
        return window_of(own, mate, cross, i)

    warmth, voltage, pattern = window(0), window(1), window(2)
    shape = warmth.shape
    inside = rows_inside(shape, ROWS)
    col = lax.broadcasted_iota(jnp.int32, shape, 1)
    last = col == shape[1] - 1
    sigma = inside * jnp.where(pattern == 1.0, copper_factor, 1.0) / (1.0 + sheet_slope * warmth)
    contact = jnp.where(pattern == 2.0, contact_gain, 0.0)
    c_down = 0.5 * (sigma + below(sigma))
    c_right = 0.5 * (sigma + jnp.where(last, 0.0, right(sigma)))
    c_left = jnp.where(col == 0, 0.5 * sigma, left(c_right))
    diagonal = leak_diag + contact + above(c_down) + c_down + c_left + c_right
    diagonal = (diagonal - SHIFT) * (1.0 / SCALE)
    o_down = c_down * inside * below(inside) * (1.0 / SCALE)
    o_up = above(o_down)
    o_right = jnp.where(last, 0.0, c_right) * (1.0 / SCALE)
    o_left = left(o_right)

    def apply(v):
        return diagonal * v - (o_up * above(v) + o_down * below(v)) - (o_left * left(v) + o_right * right(v))

    w0 = contact * voltage
    w1 = apply(w0)
    w2 = 2.0 * apply(w1) - w0
    return (w0, w1, w2), apply, inside, (c_down, c_right, c_left)


def gram_kernel(own, mate, cross, packed_in, packed):
    (w0, w1, w2), apply, _, _ = basis(own, mate, cross)
    w0, w1, w2, w3 = (w[ROWS : 2 * ROWS] for w in (w0, w1, w2, apply(w2)))
    lane = lax.broadcasted_iota(jnp.int32, (1, 128), 1)
    line = jnp.zeros((1, 128), jnp.float32)
    for i, (u, v) in enumerate(((w0, w0), (w0, w1), (w0, w2), (w1, w1), (w1, w2), (w2, w2), (w2, w3))):
        line = jnp.where(lane == i, jnp.sum(u * v, keepdims=True), line)
    for slab in range(packed.shape[0] // BLOCK):
        at = BLOCK * slab
        packed[at : at + 2 * ROWS] = packed_in[at : at + 2 * ROWS]
        packed[at + 2 * ROWS : at + BLOCK] = line


def solve_small(lines):
    total = jnp.sum(lines, axis=0, keepdims=True)
    g00, g01, g02, g11, g12, g22, k22 = (total[:, i : i + 1] for i in range(7))
    gram = ((g00, g01, g02), (g01, g11, g12), (g02, g12, g22))
    k11, k12 = 0.5 * (g12 + g01), 0.5 * (g22 + g02)
    shifted = ((g01, g11, g12), (g11, k11, k12), (g12, k12, k22))
    energy = [[SCALE * shifted[i][j] + SHIFT * gram[i][j] for j in range(3)] for i in range(3)]

    def form(m, v):
        return sum(v[i] * (v[i] * m[i][i] + 2.0 * sum((v[j] * m[i][j] for j in range(i + 1, len(v))), 0.0)) for i in range(len(v)))

    def ratio(num, den, low, high):
        return jnp.clip(num / jnp.maximum(den, 1e-37), low, high)

    alpha0 = g00 / energy[0][0]
    r = [1.0 - alpha0 * SHIFT, -alpha0 * SCALE]
    rr1 = jnp.maximum(form(gram, r), 0.0)
    beta = ratio(rr1, g00, 0.0, 1e4)
    p = [r[0] + beta, r[1]]
    alpha1 = ratio(rr1, form(energy, p), 0.05, 4.1)
    half = 0.5 * SCALE * p[1]
    image = [half + SHIFT * p[0], SCALE * p[0] + SHIFT * p[1], half]
    x = [alpha0 + alpha1 * p[0], alpha1 * p[1]]
    r = [r[0] - alpha1 * image[0], r[1] - alpha1 * image[1], -alpha1 * image[2]]
    rr2 = jnp.maximum(form(gram, r), 0.0)
    beta = ratio(rr2, rr1, 0.0, 1e4)
    p = [r[0] + beta * p[0], r[1] + beta * p[1], r[2]]
    alpha2 = ratio(rr2, form(energy, p), 0.05, 4.1)
    return x[0] + alpha2 * p[0], x[1] + alpha2 * p[1], alpha2 * p[2]


PAIRS = ((0, 0), (0, 1), (0, 2), (1, 1), (1, 2), (2, 2))
SPAN = ROWS + 2 * HALO
EDGE = 8


def deposit_kernel(layers, own, mate, cross, bins, w0_out, w1_out, w2_out, heats):
    spokes = bins.shape[-1]
    fields, _, inside, (c_down, c_right, c_left) = basis(own, mate, cross)
    for out, w in zip((w0_out, w1_out, w2_out), fields):
        out[...] = w[ROWS : 2 * ROWS]
    shape = inside.shape
    col = lax.broadcasted_iota(jnp.int32, shape, 1)
    last, first = col == shape[1] - 1, col == 0
    fields = [w * inside for w in fields]
    falls = [w - below(w) for w in fields]
    steps = [w - jnp.where(last, 0.0, right(w)) for w in fields]
    wanted = slice(ROWS - HALO, ROWS - HALO + SPAN)
    for pair, (i, j) in enumerate(PAIRS):
        q_down = c_down * (falls[i] * falls[j])
        q_right = c_right * (steps[i] * steps[j])
        q_left = jnp.where(first, c_left * (fields[i] * fields[j]), left(q_right))
        joule = (q_down + above(q_down)) + (q_right + q_left)
        factor = heat_factor if i == j else 2.0 * heat_factor
        joule = factor * joule[wanted]
        for part in range(heats.shape[0]):
            heats[part, SPAN * pair : SPAN * (pair + 1)] = joule[:, 128 * part : 128 * (part + 1)]
    for part in range(heats.shape[0]):
        heats[part, SPAN * len(PAIRS) :] = jnp.zeros((SPAN * (8 - len(PAIRS)), 128), jnp.float32)
    cell = window_of(own, mate, cross, 3)[wanted].astype(jnp.int32)
    azimuth = cell & (spokes - 1)
    outermost = jnp.where(cell >= (layers - 1) * spokes, 1.0, 0.0)
    spoke = lax.broadcasted_iota(jnp.int32, (spokes, shape[1]), 0)
    for row in range(1, SPAN - 1):
        pick = jnp.where(azimuth[row : row + 1] == spoke, 1.0, 0.0).astype(jnp.bfloat16)
        joule = jnp.concatenate([heats[part, pl.ds(row, 8, stride=SPAN), :] for part in range(heats.shape[0])], axis=1)
        upper = joule * outermost[row : row + 1]
        pieces = []
        for part in (joule - upper, upper):
            for _ in range(3):
                piece = part.astype(jnp.bfloat16)
                part = part - piece.astype(jnp.float32)
                pieces.append(piece)
        total = lax.dot_general(
            jnp.concatenate(pieces, axis=0), pick, (((1,), (1,)), ((), ())), preferred_element_type=jnp.float32
        )
        bins[row, 0:8] = total[0:8] + (total[8:16] + total[16:24])
        bins[row, 8:16] = total[24:32] + (total[32:40] + total[40:48])


def substep_rows(rows, layers, warm, cond, base, done):
    body = slice(EDGE, EDGE + layers)
    inward, outward = slice(EDGE - 1, EDGE - 1 + layers), slice(EDGE + 1, EDGE + 1 + layers)

    def conductivity(row):
        t = warm[row, body]
        k = base[row] * (1.0 + diffusivity_derivative * t)
        cond[row, body] = k
        return t, k

    def between(t, k, t_other, k_other):
        return (k + k_other) * (t_other - t)

    below_row = conductivity(rows[0] - 1)
    here = conductivity(rows[0])
    inner = between(*below_row, *here)
    for row in rows:
        t, k = here
        here = conductivity(row + 1)
        outer = between(t, k, *here)
        flux = outer - inner
        inner = outer
        flux = flux + between(t, k, warm[row, inward], cond[row, inward])
        flux = flux + between(t, k, warm[row, outward], cond[row, outward])
        face = between(t, k, right(t), right(k))
        done(row, t, flux + (face - left(face)))


def clear_edges(layers, *fields):
    for field in fields:
        blank = jnp.zeros((EDGE, field.shape[-1]), jnp.float32)
        field[0:EDGE] = blank
        field[EDGE + layers : 2 * EDGE + layers] = blank


def share_kernel(layers, own, lines, for_cross, for_mate):
    mine = own[pl.ds(2 * ROWS, layers, stride=BLOCK), :]
    for magnet in range(lines.shape[0] // layers):
        lines[layers * magnet : layers * (magnet + 1)] = mine
    even = place()[0] % 2 == 0
    for layer in range(layers):
        at = BLOCK * layer

        def rows_from(first):
            return jnp.concatenate([own[at + i + first : at + i + first + HALO] for i in (0, ROWS)], axis=0)

        early, late = rows_from(0), rows_from(ROWS - HALO)
        part = slice(2 * HALO * layer, 2 * HALO * (layer + 1))
        for_mate[part] = jnp.where(even, late, early)
        for_cross[part] = jnp.where(even, early, late)


def first_kernel(layers, own, cross, mate, fresh, base, store, warm, cond):
    block = own.shape[0] // layers
    index, count = place()
    body = slice(EDGE, EDGE + layers)
    for row in range(SPAN):

        def rows_of(array):
            if HALO <= row < HALO + ROWS:
                return own[pl.ds(ROWS * array + row - HALO, layers, stride=block), :]
            at = HALO * array + row % HALO
            return sides(index, *(ref[pl.ds(at, layers, stride=2 * HALO), :] for ref in (mate, cross)))[int(row >= HALO)]

        there = 1.0
        if row < HALO:
            there = jnp.where(index > 0, 1.0, 0.0)
        elif row >= HALO + ROWS:
            there = jnp.where(index < count - 1, 1.0, 0.0)
        kind = rows_of(1)

        def table(values):
            return jnp.where(kind == 0.0, values[0], jnp.where(kind == 1.0, values[1], jnp.where(kind == 2.0, values[2], values[3])))

        base[row] = table(conduct_table) * there
        store[row] = table([0.5 * time_step / c for c in capacity_table]) * there
        warm[row, body] = rows_of(0)
        clear_edges(layers, warm.at[row], cond.at[row], fresh.at[row])

    def done(row, t, flux):
        fresh[row, body] = t + store[row] * flux

    substep_rows(range(1, SPAN - 1), layers, warm, cond, base, done)


def heat_kernel(layers, lines, w0, w1, w2, bins, fresh, base, store, potential, heated, warm, cond):
    spokes = heated.shape[-1]
    body = slice(EDGE, EDGE + layers)
    f = solve_small(lines[...])
    potential[...] = f[0] * w0[...] + f[1] * w1[...] + f[2] * w2[...]
    sublane = lax.broadcasted_iota(jnp.int32, (8, spokes), 0)
    weight = jnp.zeros((8, spokes), jnp.float32)
    for pair, (i, j) in enumerate(PAIRS):
        weight = jnp.where(sublane == pair, f[i] * f[j], weight)
    weight = 2.0 * weight
    heat = {}
    top = slice(layers - 8, layers)
    for row in range(1, SPAN - 1):
        inner = jnp.sum(weight * bins[row, 0:8], axis=0, keepdims=True)
        outer = jnp.sum(weight * bins[row, 8:16], axis=0, keepdims=True)
        heat[row] = jnp.where(sublane == 6, inner, jnp.where(sublane == 7, outer, 0.0))
        warm[1, row] = fresh[row]
        warm[1, row, EDGE + layers - 8 : EDGE + layers] = fresh[row, EDGE + layers - 8 : EDGE + layers] + store[row, top] * heat[row]
        clear_edges(layers, warm.at[0, row], cond.at[row])

    for substep in range(1, SUBSTEPS):

        def done(row, t, flux):
            flux = jnp.concatenate([flux[: layers - 8], flux[top] + heat[row]], axis=0)
            t = t + store[row] * flux
            if substep + 1 < SUBSTEPS:
                warm[1 - substep % 2, row, body] = t
            else:
                heated[pl.ds(row - HALO, layers, stride=ROWS), :] = t

        substep_rows(range(substep + 1, SPAN - 1 - substep), layers, warm.at[substep % 2], cond, base, done)


def local(foil_warmth, terminal_voltage_input, foil_segment_pattern, underlying_block_map, prior_block_warmth, substance_kind):
    f32 = jnp.float32
    magnets, layers = lax.axis_size("magnet"), lax.axis_size("slab")
    count = magnets * layers
    width, spokes = foil_warmth.shape[1], prior_block_warmth.shape[2]
    mates = [(i, i ^ 1) for i in range(count)]
    crossing = [(i, i + 1) for i in range(1, count - 1, 2)] + [(i + 1, i) for i in range(1, count - 1, 2)]

    def exchange(for_mate, for_cross):
        over = lax.ppermute(for_cross, BOTH, crossing)
        return lax.ppermute(for_mate, BOTH, mates), over

    def call(kernel, name, shapes, *operands, scratch=(), spaces=None, cost=None, room=8 << 20):
        return pl.pallas_call(
            kernel,
            out_shape=tuple(jax.ShapeDtypeStruct(dims, f32) for dims in shapes),
            in_specs=[pl.BlockSpec(memory_space=spaces or pltpu.VMEM)] * len(operands),
            out_specs=(pl.BlockSpec(memory_space=pltpu.VMEM),) * len(shapes),
            scratch_shapes=scratch,
            cost_estimate=cost,
            compiler_params=pltpu.CompilerParams(vmem_limit_bytes=room),
            name=name,
        )(*operands)

    rows = (ROWS, width)
    (sheet,) = call(
        sheet_kernel,
        "sheet",
        [(4 * ROWS, width)],
        foil_warmth,
        terminal_voltage_input,
        foil_segment_pattern,
        underlying_block_map,
        scratch=[pltpu.VMEM(rows, jnp.int32), pltpu.VMEM(rows, jnp.int32), pltpu.SemaphoreType.DMA((4,))],
        spaces=pltpu.HBM,
        room=66846720,
    )
    around = exchange(sheet, sheet)
    stack = (layers * BLOCK, spokes)
    (packed,) = call(
        pack_kernel, "pack", [stack], prior_block_warmth.reshape(-1, spokes), substance_kind.reshape(-1, spokes)
    )
    (packed,) = call(gram_kernel, "gram", [stack], sheet, *around, packed)

    bricks = lax.all_to_all(packed.reshape(layers, BLOCK, 1, spokes), "slab", 0, 0)
    bins, *fields = call(
        functools.partial(deposit_kernel, layers),
        "deposit",
        [(SPAN, 16, spokes), rows, rows, rows],
        sheet,
        *around,
        scratch=[pltpu.VMEM((width // 128, 8 * SPAN, 128), f32)],
        cost=pl.CostEstimate(flops=10**8, bytes_accessed=2 * 10**6, transcendentals=0),
    )
    bricks, bins = lax.optimization_barrier((bricks.reshape(stack), bins))
    lines, over, beside = call(
        functools.partial(share_kernel, layers),
        "share",
        [(magnets * layers, spokes)] + [(2 * HALO * layers, spokes)] * 2,
        bricks,
    )
    lines = lax.all_to_all(lines.reshape(magnets, layers, spokes), "magnet", 0, 0).reshape(count, spokes)

    padded = (SPAN, layers + 2 * EDGE, spokes)
    plain = (SPAN, layers, spokes)
    stage = call(
        functools.partial(first_kernel, layers),
        "first",
        [padded, plain, plain],
        bricks,
        *exchange(beside, over)[::-1],
        scratch=[pltpu.VMEM(padded, f32), pltpu.VMEM(padded, f32)],
        cost=pl.CostEstimate(flops=0, bytes_accessed=0, transcendentals=0),
    )
    potential, heated = call(
        functools.partial(heat_kernel, layers),
        "heat",
        [rows, (layers * ROWS, spokes)],
        lines,
        *fields,
        bins,
        *stage,
        scratch=[pltpu.VMEM((2,) + padded, f32), pltpu.VMEM(padded, f32)],
    )
    heated = lax.all_to_all(heated.reshape(layers, ROWS, spokes), "slab", 0, 0)
    return potential, heated.reshape(prior_block_warmth.shape)


def solution(mesh):
    placed = (
        P(("magnet", "slab"), None),
        P(("magnet", "slab"), None),
        P(("magnet", "slab"), None),
        P("magnet", None),
        P("slab", "magnet", None),
        P("slab", "magnet", None),
    )
    return jax.shard_map(
        local,
        mesh=mesh,
        in_specs=placed,
        out_specs=(P(("magnet", "slab"), None), P("slab", "magnet", None)),
        check_vma=False,
    )
```

```python
import functools

import jax
import jax.numpy as jnp
from jax import lax
from jax.experimental import pallas as pl
from jax.experimental.pallas import tpu as pltpu
from jax.sharding import PartitionSpec as P

SUBSTEPS = 4
HALO = SUBSTEPS
ROWS = 8

leak_diag = 0.25
contact_gain = 4.0
copper_factor = 3.0
sheet_slope = 0.5
heat_factor = 1.5
time_step = 0.03
conduct_table = (0.3, 1.0, 2.0, 0.6)
capacity_table = (1.0, 1.5, 2.0, 1.2)
diffusivity_derivative = 0.4

SHIFT = 9.85
SCALE = 9.6
BOTH = ("magnet", "slab")
BLOCK = 2 * ROWS + 1


def place():
    size = lax.axis_size("slab")
    return lax.axis_index("magnet") * size + lax.axis_index("slab"), lax.axis_size("magnet") * size


def above(v):
    return pltpu.roll(v, 1, 0)


def below(v):
    return pltpu.roll(v, v.shape[0] - 1, 0)


def left(v):
    return pltpu.roll(v, 1, 1)


def right(v):
    return pltpu.roll(v, v.shape[1] - 1, 1)


def rows_inside(shape, margin):
    index, count = place()
    row = lax.broadcasted_iota(jnp.int32, shape, 0)
    low = jnp.where(index > 0, 0, margin)
    high = jnp.where(index < count - 1, shape[0], shape[0] - margin)
    return jnp.where((row >= low) & (row < high), 1.0, 0.0).astype(jnp.float32)


def sheet_kernel(warmth, voltage, pattern, cells, sheet, pattern_here, cells_here, sems):
    at = pl.multiple_of(lax.axis_index("slab") * ROWS, ROWS)
    copies = [
        pltpu.make_async_copy(pattern, pattern_here, sems.at[0]),
        pltpu.make_async_copy(cells.at[pl.ds(at, ROWS)], cells_here, sems.at[1]),
        pltpu.make_async_copy(warmth, sheet.at[0:ROWS], sems.at[2]),
        pltpu.make_async_copy(voltage, sheet.at[ROWS : 2 * ROWS], sems.at[3]),
    ]
    for copy in copies:
        copy.start()
    copies[0].wait()
    sheet[2 * ROWS : 3 * ROWS] = pattern_here[...].astype(jnp.float32)
    copies[1].wait()
    sheet[3 * ROWS : 4 * ROWS] = cells_here[...].astype(jnp.float32)
    copies[2].wait()
    copies[3].wait()


def pack_kernel(warmth, kind, packed):
    for slab in range(packed.shape[0] // BLOCK):
        part = slice(ROWS * slab, ROWS * (slab + 1))
        at = BLOCK * slab
        packed[at : at + ROWS] = warmth[part]
        packed[at + ROWS : at + 2 * ROWS] = kind[part].astype(jnp.float32)
        packed[at + 2 * ROWS : at + BLOCK] = jnp.zeros((1, packed.shape[1]), jnp.float32)


def sides(index, mate, cross):
    even = index % 2 == 0
    return jnp.where(even, cross, mate), jnp.where(even, mate, cross)


def window_of(own, mate, cross, i):
    part = slice(ROWS * i, ROWS * (i + 1))
    before, after = sides(place()[0], mate[part], cross[part])
    return jnp.concatenate([before, own[part], after], axis=0)


def basis(own, mate, cross):
    def window(i):
        return window_of(own, mate, cross, i)

    warmth, voltage, pattern = window(0), window(1), window(2)
    shape = warmth.shape
    inside = rows_inside(shape, ROWS)
    col = lax.broadcasted_iota(jnp.int32, shape, 1)
    last = col == shape[1] - 1
    sigma = inside * jnp.where(pattern == 1.0, copper_factor, 1.0) / (1.0 + sheet_slope * warmth)
    contact = jnp.where(pattern == 2.0, contact_gain, 0.0)
    c_down = 0.5 * (sigma + below(sigma))
    c_right = 0.5 * (sigma + jnp.where(last, 0.0, right(sigma)))
    c_left = jnp.where(col == 0, 0.5 * sigma, left(c_right))
    diagonal = leak_diag + contact + above(c_down) + c_down + c_left + c_right
    diagonal = (diagonal - SHIFT) * (1.0 / SCALE)
    o_down = c_down * inside * below(inside) * (1.0 / SCALE)
    o_up = above(o_down)
    o_right = jnp.where(last, 0.0, c_right) * (1.0 / SCALE)
    o_left = left(o_right)

    def apply(v):
        return diagonal * v - (o_up * above(v) + o_down * below(v)) - (o_left * left(v) + o_right * right(v))

    w0 = contact * voltage
    w1 = apply(w0)
    w2 = 2.0 * apply(w1) - w0
    return (w0, w1, w2), apply, inside, (c_down, c_right, c_left)


def gram_kernel(own, mate, cross, packed_in, packed):
    (w0, w1, w2), apply, _, _ = basis(own, mate, cross)
    w0, w1, w2, w3 = (w[ROWS : 2 * ROWS] for w in (w0, w1, w2, apply(w2)))
    lane = lax.broadcasted_iota(jnp.int32, (1, 128), 1)
    line = jnp.zeros((1, 128), jnp.float32)
    for i, (u, v) in enumerate(((w0, w0), (w0, w1), (w0, w2), (w1, w1), (w1, w2), (w2, w2), (w2, w3))):
        line = jnp.where(lane == i, jnp.sum(u * v, keepdims=True), line)
    for slab in range(packed.shape[0] // BLOCK):
        at = BLOCK * slab
        packed[at : at + 2 * ROWS] = packed_in[at : at + 2 * ROWS]
        packed[at + 2 * ROWS : at + BLOCK] = line


def solve_small(lines):
    total = jnp.sum(lines, axis=0, keepdims=True)
    g00, g01, g02, g11, g12, g22, k22 = (total[:, i : i + 1] for i in range(7))
    gram = ((g00, g01, g02), (g01, g11, g12), (g02, g12, g22))
    k11, k12 = 0.5 * (g12 + g01), 0.5 * (g22 + g02)
    shifted = ((g01, g11, g12), (g11, k11, k12), (g12, k12, k22))
    energy = [[SCALE * shifted[i][j] + SHIFT * gram[i][j] for j in range(3)] for i in range(3)]

    def form(m, v):
        return sum(v[i] * (v[i] * m[i][i] + 2.0 * sum((v[j] * m[i][j] for j in range(i + 1, len(v))), 0.0)) for i in range(len(v)))

    def ratio(num, den, low, high):
        return jnp.clip(num / jnp.maximum(den, 1e-37), low, high)

    alpha0 = g00 / energy[0][0]
    r = [1.0 - alpha0 * SHIFT, -alpha0 * SCALE]
    rr1 = jnp.maximum(form(gram, r), 0.0)
    beta = ratio(rr1, g00, 0.0, 1e4)
    p = [r[0] + beta, r[1]]
    alpha1 = ratio(rr1, form(energy, p), 0.05, 4.1)
    half = 0.5 * SCALE * p[1]
    image = [half + SHIFT * p[0], SCALE * p[0] + SHIFT * p[1], half]
    x = [alpha0 + alpha1 * p[0], alpha1 * p[1]]
    r = [r[0] - alpha1 * image[0], r[1] - alpha1 * image[1], -alpha1 * image[2]]
    rr2 = jnp.maximum(form(gram, r), 0.0)
    beta = ratio(rr2, rr1, 0.0, 1e4)
    p = [r[0] + beta * p[0], r[1] + beta * p[1], r[2]]
    alpha2 = ratio(rr2, form(energy, p), 0.05, 4.1)
    return x[0] + alpha2 * p[0], x[1] + alpha2 * p[1], alpha2 * p[2]


PAIRS = ((0, 0), (0, 1), (0, 2), (1, 1), (1, 2), (2, 2))
SPAN = ROWS + 2 * HALO
EDGE = 8


def deposit_kernel(layers, own, mate, cross, bins, w0_out, w1_out, w2_out, heats):
    spokes = bins.shape[-1]
    fields, _, inside, (c_down, c_right, c_left) = basis(own, mate, cross)
    for out, w in zip((w0_out, w1_out, w2_out), fields):
        out[...] = w[ROWS : 2 * ROWS]
    shape = inside.shape
    col = lax.broadcasted_iota(jnp.int32, shape, 1)
    last, first = col == shape[1] - 1, col == 0
    fields = [w * inside for w in fields]
    falls = [w - below(w) for w in fields]
    steps = [w - jnp.where(last, 0.0, right(w)) for w in fields]
    wanted = slice(ROWS - HALO, ROWS - HALO + SPAN)
    for pair, (i, j) in enumerate(PAIRS):
        q_down = c_down * (falls[i] * falls[j])
        q_right = c_right * (steps[i] * steps[j])
        q_left = jnp.where(first, c_left * (fields[i] * fields[j]), left(q_right))
        joule = (q_down + above(q_down)) + (q_right + q_left)
        factor = heat_factor if i == j else 2.0 * heat_factor
        joule = factor * joule[wanted]
        for part in range(heats.shape[0]):
            heats[part, SPAN * pair : SPAN * (pair + 1)] = joule[:, 128 * part : 128 * (part + 1)]
    for part in range(heats.shape[0]):
        heats[part, SPAN * len(PAIRS) :] = jnp.zeros((SPAN * (8 - len(PAIRS)), 128), jnp.float32)
    cell = window_of(own, mate, cross, 3)[wanted].astype(jnp.int32)
    azimuth = cell & (spokes - 1)
    outermost = jnp.where(cell >= (layers - 1) * spokes, 1.0, 0.0)
    spoke = lax.broadcasted_iota(jnp.int32, (spokes, shape[1]), 0)
    for row in range(1, SPAN - 1):
        pick = jnp.where(azimuth[row : row + 1] == spoke, 1.0, 0.0).astype(jnp.bfloat16)
        joule = jnp.concatenate([heats[part, pl.ds(row, 8, stride=SPAN), :] for part in range(heats.shape[0])], axis=1)
        upper = joule * outermost[row : row + 1]
        pieces = []
        for part in (joule - upper, upper):
            for _ in range(3):
                piece = part.astype(jnp.bfloat16)
                part = part - piece.astype(jnp.float32)
                pieces.append(piece)
        total = lax.dot_general(
            jnp.concatenate(pieces, axis=0), pick, (((1,), (1,)), ((), ())), preferred_element_type=jnp.float32
        )
        bins[row, 0:8] = total[0:8] + (total[8:16] + total[16:24])
        bins[row, 8:16] = total[24:32] + (total[32:40] + total[40:48])


def substep_rows(rows, layers, warm, cond, base, done):
    body = slice(EDGE, EDGE + layers)
    inward, outward = slice(EDGE - 1, EDGE - 1 + layers), slice(EDGE + 1, EDGE + 1 + layers)

    def conductivity(row):
        t = warm[row, body]
        k = base[row] * (1.0 + diffusivity_derivative * t)
        cond[row, body] = k
        return t, k

    def between(t, k, t_other, k_other):
        return (k + k_other) * (t_other - t)

    below_row = conductivity(rows[0] - 1)
    here = conductivity(rows[0])
    inner = between(*below_row, *here)
    for row in rows:
        t, k = here
        here = conductivity(row + 1)
        outer = between(t, k, *here)
        flux = outer - inner
        inner = outer
        flux = flux + between(t, k, warm[row, inward], cond[row, inward])
        flux = flux + between(t, k, warm[row, outward], cond[row, outward])
        face = between(t, k, right(t), right(k))
        done(row, t, flux + (face - left(face)))


def clear_edges(layers, *fields):
    for field in fields:
        blank = jnp.zeros((EDGE, field.shape[-1]), jnp.float32)
        field[0:EDGE] = blank
        field[EDGE + layers : 2 * EDGE + layers] = blank


def share_kernel(layers, own, lines, for_cross, for_mate):
    mine = own[pl.ds(2 * ROWS, layers, stride=BLOCK), :]
    for magnet in range(lines.shape[0] // layers):
        lines[layers * magnet : layers * (magnet + 1)] = mine
    even = place()[0] % 2 == 0
    for layer in range(layers):
        at = BLOCK * layer

        def rows_from(first):
            return jnp.concatenate([own[at + i + first : at + i + first + HALO] for i in (0, ROWS)], axis=0)

        early, late = rows_from(0), rows_from(ROWS - HALO)
        part = slice(2 * HALO * layer, 2 * HALO * (layer + 1))
        for_mate[part] = jnp.where(even, late, early)
        for_cross[part] = jnp.where(even, early, late)


def first_kernel(layers, own, edge, cross, mate, fresh, base, store, warm, cond):
    block = own.shape[0] // layers
    index, count = place()
    body = slice(EDGE, EDGE + layers)
    for row in range(SPAN):

        def rows_of(array):
            if HALO <= row < HALO + ROWS:
                return own[pl.ds(ROWS * array + row - HALO, layers, stride=block), :]
            at = HALO * array + row % HALO
            near = sides(index, *(ref[pl.ds(at, layers, stride=2 * HALO), :] for ref in (mate, cross)))[int(row >= HALO)]
            at = ROWS * array + (row + ROWS - HALO if row < HALO else row - HALO - ROWS)
            last = lax.axis_index("slab") == (0 if row < HALO else layers - 1)
            return jnp.where(last, edge[pl.ds(at, layers, stride=block), :], near)

        there = 1.0
        if row < HALO:
            there = jnp.where(index > 0, 1.0, 0.0)
        elif row >= HALO + ROWS:
            there = jnp.where(index < count - 1, 1.0, 0.0)
        kind = rows_of(1)

        def table(values):
            return jnp.where(kind == 0.0, values[0], jnp.where(kind == 1.0, values[1], jnp.where(kind == 2.0, values[2], values[3])))

        base[row] = table(conduct_table) * there
        store[row] = table([0.5 * time_step / c for c in capacity_table]) * there
        warm[row, body] = rows_of(0)
        clear_edges(layers, warm.at[row], cond.at[row], fresh.at[row])

    def done(row, t, flux):
        fresh[row, body] = t + store[row] * flux

    substep_rows(range(1, SPAN - 1), layers, warm, cond, base, done)


def heat_kernel(layers, lines, w0, w1, w2, bins, fresh, base, store, potential, heated, warm, cond):
    spokes = heated.shape[-1]
    body = slice(EDGE, EDGE + layers)
    f = solve_small(lines[...])
    potential[...] = f[0] * w0[...] + f[1] * w1[...] + f[2] * w2[...]
    sublane = lax.broadcasted_iota(jnp.int32, (8, spokes), 0)
    weight = jnp.zeros((8, spokes), jnp.float32)
    for pair, (i, j) in enumerate(PAIRS):
        weight = jnp.where(sublane == pair, f[i] * f[j], weight)
    weight = 2.0 * weight
    heat = {}
    top = slice(layers - 8, layers)
    for row in range(1, SPAN - 1):
        inner = jnp.sum(weight * bins[row, 0:8], axis=0, keepdims=True)
        outer = jnp.sum(weight * bins[row, 8:16], axis=0, keepdims=True)
        heat[row] = jnp.where(sublane == 6, inner, jnp.where(sublane == 7, outer, 0.0))
        warm[1, row] = fresh[row]
        warm[1, row, EDGE + layers - 8 : EDGE + layers] = fresh[row, EDGE + layers - 8 : EDGE + layers] + store[row, top] * heat[row]
        clear_edges(layers, warm.at[0, row], cond.at[row])

    for substep in range(1, SUBSTEPS):

        def done(row, t, flux):
            flux = jnp.concatenate([flux[: layers - 8], flux[top] + heat[row]], axis=0)
            t = t + store[row] * flux
            if substep + 1 < SUBSTEPS:
                warm[1 - substep % 2, row, body] = t
            else:
                heated[pl.ds(row - HALO, layers, stride=ROWS), :] = t

        substep_rows(range(substep + 1, SPAN - 1 - substep), layers, warm.at[substep % 2], cond, base, done)


def local(foil_warmth, terminal_voltage_input, foil_segment_pattern, underlying_block_map, prior_block_warmth, substance_kind):
    f32 = jnp.float32
    magnets, layers = lax.axis_size("magnet"), lax.axis_size("slab")
    count = magnets * layers
    width, spokes = foil_warmth.shape[1], prior_block_warmth.shape[2]
    mates = [(i, i + 1) for i in range(0, count, 2)]
    crossing = [(i, i + 1) for i in range(1, count - 1, 2)]
    ends = [pair for pair in crossing if pair[1] % layers == 0]
    inner = [pair for pair in crossing if pair[1] % layers]

    def swap(array, pairs):
        return lax.ppermute(array, BOTH, pairs + [(j, i) for i, j in pairs])

    def call(kernel, name, shapes, *operands, scratch=(), spaces=None, cost=None, room=8 << 20):
        return pl.pallas_call(
            kernel,
            out_shape=tuple(jax.ShapeDtypeStruct(dims, f32) for dims in shapes),
            in_specs=[pl.BlockSpec(memory_space=spaces or pltpu.VMEM)] * len(operands),
            out_specs=(pl.BlockSpec(memory_space=pltpu.VMEM),) * len(shapes),
            scratch_shapes=scratch,
            cost_estimate=cost,
            compiler_params=pltpu.CompilerParams(vmem_limit_bytes=room),
            name=name,
        )(*operands)

    rows = (ROWS, width)
    (sheet,) = call(
        sheet_kernel,
        "sheet",
        [(4 * ROWS, width)],
        foil_warmth,
        terminal_voltage_input,
        foil_segment_pattern,
        underlying_block_map,
        scratch=[pltpu.VMEM(rows, jnp.int32), pltpu.VMEM(rows, jnp.int32), pltpu.SemaphoreType.DMA((4,))],
        spaces=pltpu.HBM,
        room=66846720,
    )
    across = swap(sheet, crossing)
    around = (swap(sheet, mates), across)
    stack = (layers * BLOCK, spokes)
    (packed,) = call(
        pack_kernel, "pack", [stack], prior_block_warmth.reshape(-1, spokes), substance_kind.reshape(-1, spokes)
    )
    (packed,) = call(gram_kernel, "gram", [stack], sheet, *around, packed)

    bricks = lax.all_to_all(packed.reshape(layers, BLOCK, 1, spokes), "slab", 0, 0)
    bins, *fields = call(
        functools.partial(deposit_kernel, layers),
        "deposit",
        [(SPAN, 16, spokes), rows, rows, rows],
        sheet,
        *around,
        scratch=[pltpu.VMEM((width // 128, 8 * SPAN, 128), f32)],
        cost=pl.CostEstimate(flops=10**8, bytes_accessed=2 * 10**6, transcendentals=0),
    )
    bricks, bins = lax.optimization_barrier((bricks.reshape(stack), bins))
    lines, over, beside = call(
        functools.partial(share_kernel, layers),
        "share",
        [(magnets * layers, spokes)] + [(2 * HALO * layers, spokes)] * 2,
        bricks,
    )
    lines = lax.all_to_all(lines.reshape(magnets, layers, spokes), "magnet", 0, 0).reshape(count, spokes)

    padded = (SPAN, layers + 2 * EDGE, spokes)
    plain = (SPAN, layers, spokes)
    stage = call(
        functools.partial(first_kernel, layers),
        "first",
        [padded, plain, plain],
        bricks,
        swap(bricks, ends),
        swap(over, inner),
        swap(beside, mates),
        scratch=[pltpu.VMEM(padded, f32), pltpu.VMEM(padded, f32)],
        cost=pl.CostEstimate(flops=0, bytes_accessed=0, transcendentals=0),
    )
    potential, heated = call(
        functools.partial(heat_kernel, layers),
        "heat",
        [rows, (layers * ROWS, spokes)],
        lines,
        *fields,
        bins,
        *stage,
        scratch=[pltpu.VMEM((2,) + padded, f32), pltpu.VMEM(padded, f32)],
    )
    heated = lax.all_to_all(heated.reshape(layers, ROWS, spokes), "slab", 0, 0)
    return potential, heated.reshape(prior_block_warmth.shape)


def solution(mesh):
    placed = (
        P(("magnet", "slab"), None),
        P(("magnet", "slab"), None),
        P(("magnet", "slab"), None),
        P("magnet", None),
        P("slab", "magnet", None),
        P("slab", "magnet", None),
    )
    return jax.shard_map(
        local,
        mesh=mesh,
        in_specs=placed,
        out_specs=(P(("magnet", "slab"), None), P("slab", "magnet", None)),
        check_vma=False,
    )
```

```python
import functools

import jax
import jax.numpy as jnp
from jax import lax
from jax.experimental import pallas as pl
from jax.experimental.pallas import tpu as pltpu
from jax.sharding import PartitionSpec as P

SUBSTEPS = 4
HALO = SUBSTEPS
ROWS = 8

leak_diag = 0.25
contact_gain = 4.0
copper_factor = 3.0
sheet_slope = 0.5
heat_factor = 1.5
time_step = 0.03
conduct_table = (0.3, 1.0, 2.0, 0.6)
capacity_table = (1.0, 1.5, 2.0, 1.2)
diffusivity_derivative = 0.4

SHIFT = 9.85
SCALE = 9.6
BOTH = ("magnet", "slab")
BLOCK = 2 * ROWS + 1


def place():
    size = lax.axis_size("slab")
    return lax.axis_index("magnet") * size + lax.axis_index("slab"), lax.axis_size("magnet") * size


def above(v):
    return pltpu.roll(v, 1, 0)


def below(v):
    return pltpu.roll(v, v.shape[0] - 1, 0)


def left(v):
    return pltpu.roll(v, 1, 1)


def right(v):
    return pltpu.roll(v, v.shape[1] - 1, 1)


def rows_inside(shape, margin):
    index, count = place()
    row = lax.broadcasted_iota(jnp.int32, shape, 0)
    low = jnp.where(index > 0, 0, margin)
    high = jnp.where(index < count - 1, shape[0], shape[0] - margin)
    return jnp.where((row >= low) & (row < high), 1.0, 0.0).astype(jnp.float32)


def sheet_kernel(warmth, voltage, pattern, cells, sheet, pattern_here, cells_here, sems):
    at = pl.multiple_of(lax.axis_index("slab") * ROWS, ROWS)
    copies = [
        pltpu.make_async_copy(pattern, pattern_here, sems.at[0]),
        pltpu.make_async_copy(cells.at[pl.ds(at, ROWS)], cells_here, sems.at[1]),
        pltpu.make_async_copy(warmth, sheet.at[0:ROWS], sems.at[2]),
        pltpu.make_async_copy(voltage, sheet.at[ROWS : 2 * ROWS], sems.at[3]),
    ]
    for copy in copies:
        copy.start()
    copies[0].wait()
    sheet[2 * ROWS : 3 * ROWS] = pattern_here[...].astype(jnp.float32)
    copies[1].wait()
    sheet[3 * ROWS : 4 * ROWS] = cells_here[...].astype(jnp.float32)
    copies[2].wait()
    copies[3].wait()


def pack_kernel(warmth, kind, packed):
    for slab in range(packed.shape[0] // BLOCK):
        part = slice(ROWS * slab, ROWS * (slab + 1))
        at = BLOCK * slab
        packed[at : at + ROWS] = warmth[part]
        packed[at + ROWS : at + 2 * ROWS] = kind[part].astype(jnp.float32)
        packed[at + 2 * ROWS : at + BLOCK] = jnp.zeros((1, packed.shape[1]), jnp.float32)


def sides(index, mate, cross):
    even = index % 2 == 0
    return jnp.where(even, cross, mate), jnp.where(even, mate, cross)


def window_of(own, mate, cross, i):
    part = slice(ROWS * i, ROWS * (i + 1))
    before, after = sides(place()[0], mate[part], cross[part])
    return jnp.concatenate([before, own[part], after], axis=0)


def basis(own, mate, cross):
    def window(i):
        return window_of(own, mate, cross, i)

    warmth, voltage, pattern = window(0), window(1), window(2)
    shape = warmth.shape
    inside = rows_inside(shape, ROWS)
    col = lax.broadcasted_iota(jnp.int32, shape, 1)
    last = col == shape[1] - 1
    sigma = inside * jnp.where(pattern == 1.0, copper_factor, 1.0) / (1.0 + sheet_slope * warmth)
    contact = jnp.where(pattern == 2.0, contact_gain, 0.0)
    c_down = 0.5 * (sigma + below(sigma))
    c_right = 0.5 * (sigma + jnp.where(last, 0.0, right(sigma)))
    c_left = jnp.where(col == 0, 0.5 * sigma, left(c_right))
    diagonal = leak_diag + contact + above(c_down) + c_down + c_left + c_right
    diagonal = (diagonal - SHIFT) * (1.0 / SCALE)
    o_down = c_down * inside * below(inside) * (1.0 / SCALE)
    o_up = above(o_down)
    o_right = jnp.where(last, 0.0, c_right) * (1.0 / SCALE)
    o_left = left(o_right)

    def apply(v):
        return diagonal * v - (o_up * above(v) + o_down * below(v)) - (o_left * left(v) + o_right * right(v))

    w0 = contact * voltage
    w1 = apply(w0)
    w2 = 2.0 * apply(w1) - w0
    return (w0, w1, w2), apply, inside, (c_down, c_right, c_left)


def gram_kernel(own, mate, cross, packed_in, packed):
    (w0, w1, w2), apply, _, _ = basis(own, mate, cross)
    w0, w1, w2, w3 = (w[ROWS : 2 * ROWS] for w in (w0, w1, w2, apply(w2)))
    lane = lax.broadcasted_iota(jnp.int32, (1, 128), 1)
    line = jnp.zeros((1, 128), jnp.float32)
    for i, (u, v) in enumerate(((w0, w0), (w0, w1), (w0, w2), (w1, w1), (w1, w2), (w2, w2), (w2, w3))):
        line = jnp.where(lane == i, jnp.sum(u * v, keepdims=True), line)
    for slab in range(packed.shape[0] // BLOCK):
        at = BLOCK * slab
        packed[at : at + 2 * ROWS] = packed_in[at : at + 2 * ROWS]
        packed[at + 2 * ROWS : at + BLOCK] = line


def solve_small(lines):
    total = jnp.sum(lines, axis=0, keepdims=True)
    g00, g01, g02, g11, g12, g22, k22 = (total[:, i : i + 1] for i in range(7))
    gram = ((g00, g01, g02), (g01, g11, g12), (g02, g12, g22))
    k11, k12 = 0.5 * (g12 + g01), 0.5 * (g22 + g02)
    shifted = ((g01, g11, g12), (g11, k11, k12), (g12, k12, k22))
    energy = [[SCALE * shifted[i][j] + SHIFT * gram[i][j] for j in range(3)] for i in range(3)]

    def form(m, v):
        return sum(v[i] * (v[i] * m[i][i] + 2.0 * sum((v[j] * m[i][j] for j in range(i + 1, len(v))), 0.0)) for i in range(len(v)))

    def ratio(num, den, low, high):
        return jnp.clip(num / jnp.maximum(den, 1e-37), low, high)

    alpha0 = g00 / energy[0][0]
    r = [1.0 - alpha0 * SHIFT, -alpha0 * SCALE]
    rr1 = jnp.maximum(form(gram, r), 0.0)
    beta = ratio(rr1, g00, 0.0, 1e4)
    p = [r[0] + beta, r[1]]
    alpha1 = ratio(rr1, form(energy, p), 0.05, 4.1)
    half = 0.5 * SCALE * p[1]
    image = [half + SHIFT * p[0], SCALE * p[0] + SHIFT * p[1], half]
    x = [alpha0 + alpha1 * p[0], alpha1 * p[1]]
    r = [r[0] - alpha1 * image[0], r[1] - alpha1 * image[1], -alpha1 * image[2]]
    rr2 = jnp.maximum(form(gram, r), 0.0)
    beta = ratio(rr2, rr1, 0.0, 1e4)
    p = [r[0] + beta * p[0], r[1] + beta * p[1], r[2]]
    alpha2 = ratio(rr2, form(energy, p), 0.05, 4.1)
    return x[0] + alpha2 * p[0], x[1] + alpha2 * p[1], alpha2 * p[2]


PAIRS = ((0, 0), (0, 1), (0, 2), (1, 1), (1, 2), (2, 2))
SPAN = ROWS + 2 * HALO
EDGE = 8


def deposit_kernel(layers, own, mate, cross, bins, w0_out, w1_out, w2_out, heats):
    spokes = bins.shape[-1]
    fields, _, inside, (c_down, c_right, c_left) = basis(own, mate, cross)
    for out, w in zip((w0_out, w1_out, w2_out), fields):
        out[...] = w[ROWS : 2 * ROWS]
    shape = inside.shape
    col = lax.broadcasted_iota(jnp.int32, shape, 1)
    last, first = col == shape[1] - 1, col == 0
    fields = [w * inside for w in fields]
    falls = [w - below(w) for w in fields]
    steps = [w - jnp.where(last, 0.0, right(w)) for w in fields]
    wanted = slice(ROWS - HALO, ROWS - HALO + SPAN)
    for pair, (i, j) in enumerate(PAIRS):
        q_down = c_down * (falls[i] * falls[j])
        q_right = c_right * (steps[i] * steps[j])
        q_left = jnp.where(first, c_left * (fields[i] * fields[j]), left(q_right))
        joule = (q_down + above(q_down)) + (q_right + q_left)
        factor = heat_factor if i == j else 2.0 * heat_factor
        joule = factor * joule[wanted]
        for part in range(heats.shape[0]):
            heats[part, SPAN * pair : SPAN * (pair + 1)] = joule[:, 128 * part : 128 * (part + 1)]
    for part in range(heats.shape[0]):
        heats[part, SPAN * len(PAIRS) :] = jnp.zeros((SPAN * (8 - len(PAIRS)), 128), jnp.float32)
    cell = window_of(own, mate, cross, 3)[wanted].astype(jnp.int32)
    azimuth = cell & (spokes - 1)
    outermost = jnp.where(cell >= (layers - 1) * spokes, 1.0, 0.0)
    spoke = lax.broadcasted_iota(jnp.int32, (spokes, shape[1]), 0)
    for row in range(1, SPAN - 1):
        pick = jnp.where(azimuth[row : row + 1] == spoke, 1.0, 0.0).astype(jnp.bfloat16)
        joule = jnp.concatenate([heats[part, pl.ds(row, 8, stride=SPAN), :] for part in range(heats.shape[0])], axis=1)
        upper = joule * outermost[row : row + 1]
        pieces = []
        for part in (joule - upper, upper):
            for _ in range(3):
                piece = part.astype(jnp.bfloat16)
                part = part - piece.astype(jnp.float32)
                pieces.append(piece)
        total = lax.dot_general(
            jnp.concatenate(pieces, axis=0), pick, (((1,), (1,)), ((), ())), preferred_element_type=jnp.float32
        )
        bins[row, 0:8] = total[0:8] + (total[8:16] + total[16:24])
        bins[row, 8:16] = total[24:32] + (total[32:40] + total[40:48])


def substep_rows(rows, layers, warm, cond, base, done):
    body = slice(EDGE, EDGE + layers)
    inward, outward = slice(EDGE - 1, EDGE - 1 + layers), slice(EDGE + 1, EDGE + 1 + layers)

    def conductivity(row):
        t = warm[row, body]
        k = base[row] * (1.0 + diffusivity_derivative * t)
        cond[row, body] = k
        return t, k

    def between(t, k, t_other, k_other):
        return (k + k_other) * (t_other - t)

    below_row = conductivity(rows[0] - 1)
    here = conductivity(rows[0])
    inner = between(*below_row, *here)
    for row in rows:
        t, k = here
        here = conductivity(row + 1)
        outer = between(t, k, *here)
        flux = outer - inner
        inner = outer
        flux = flux + between(t, k, warm[row, inward], cond[row, inward])
        flux = flux + between(t, k, warm[row, outward], cond[row, outward])
        face = between(t, k, right(t), right(k))
        done(row, t, flux + (face - left(face)))


def clear_edges(layers, *fields):
    for field in fields:
        blank = jnp.zeros((EDGE, field.shape[-1]), jnp.float32)
        field[0:EDGE] = blank
        field[EDGE + layers : 2 * EDGE + layers] = blank


def share_kernel(layers, own, lines, for_cross, for_mate, for_end):
    mine = own[pl.ds(2 * ROWS, layers, stride=BLOCK), :]
    for magnet in range(lines.shape[0] // layers):
        lines[layers * magnet : layers * (magnet + 1)] = mine
    even = place()[0] % 2 == 0
    for layer in range(layers):
        at = BLOCK * layer

        def rows_from(first):
            return jnp.concatenate([own[at + i + first : at + i + first + HALO] for i in (0, ROWS)], axis=0)

        early, late = rows_from(0), rows_from(ROWS - HALO)
        part = slice(2 * HALO * layer, 2 * HALO * (layer + 1))
        for_mate[part] = jnp.where(even, late, early)
        for_cross[part] = jnp.where(even, early, late)
        for_end[part] = jnp.where(even, early, late)


def first_kernel(layers, own, cross, mate, end, fresh, base, store, warm, cond):
    block = own.shape[0] // layers
    index, count = place()
    body = slice(EDGE, EDGE + layers)
    for row in range(SPAN):

        def rows_of(array):
            if HALO <= row < HALO + ROWS:
                return own[pl.ds(ROWS * array + row - HALO, layers, stride=block), :]
            at = pl.ds(HALO * array + row % HALO, layers, stride=2 * HALO)
            near = sides(index, mate[at, :], cross[at, :])[int(row >= HALO)]
            last = lax.axis_index("slab") == (0 if row < HALO else layers - 1)
            return jnp.where(last, end[at, :], near)

        there = 1.0
        if row < HALO:
            there = jnp.where(index > 0, 1.0, 0.0)
        elif row >= HALO + ROWS:
            there = jnp.where(index < count - 1, 1.0, 0.0)
        kind = rows_of(1)

        def table(values):
            return jnp.where(kind == 0.0, values[0], jnp.where(kind == 1.0, values[1], jnp.where(kind == 2.0, values[2], values[3])))

        base[row] = table(conduct_table) * there
        store[row] = table([0.5 * time_step / c for c in capacity_table]) * there
        warm[row, body] = rows_of(0)
        clear_edges(layers, warm.at[row], cond.at[row], fresh.at[row])

    def done(row, t, flux):
        fresh[row, body] = t + store[row] * flux

    substep_rows(range(1, SPAN - 1), layers, warm, cond, base, done)


def heat_kernel(layers, lines, w0, w1, w2, bins, fresh, base, store, potential, heated, warm, cond):
    spokes = heated.shape[-1]
    body = slice(EDGE, EDGE + layers)
    f = solve_small(lines[...])
    potential[...] = f[0] * w0[...] + f[1] * w1[...] + f[2] * w2[...]
    sublane = lax.broadcasted_iota(jnp.int32, (8, spokes), 0)
    weight = jnp.zeros((8, spokes), jnp.float32)
    for pair, (i, j) in enumerate(PAIRS):
        weight = jnp.where(sublane == pair, f[i] * f[j], weight)
    weight = 2.0 * weight
    heat = {}
    top = slice(layers - 8, layers)
    for row in range(1, SPAN - 1):
        inner = jnp.sum(weight * bins[row, 0:8], axis=0, keepdims=True)
        outer = jnp.sum(weight * bins[row, 8:16], axis=0, keepdims=True)
        heat[row] = jnp.where(sublane == 6, inner, jnp.where(sublane == 7, outer, 0.0))
        warm[1, row] = fresh[row]
        warm[1, row, EDGE + layers - 8 : EDGE + layers] = fresh[row, EDGE + layers - 8 : EDGE + layers] + store[row, top] * heat[row]
        clear_edges(layers, warm.at[0, row], cond.at[row])

    for substep in range(1, SUBSTEPS):

        def done(row, t, flux):
            flux = jnp.concatenate([flux[: layers - 8], flux[top] + heat[row]], axis=0)
            t = t + store[row] * flux
            if substep + 1 < SUBSTEPS:
                warm[1 - substep % 2, row, body] = t
            else:
                heated[pl.ds(row - HALO, layers, stride=ROWS), :] = t

        substep_rows(range(substep + 1, SPAN - 1 - substep), layers, warm.at[substep % 2], cond, base, done)


def local(foil_warmth, terminal_voltage_input, foil_segment_pattern, underlying_block_map, prior_block_warmth, substance_kind):
    f32 = jnp.float32
    magnets, layers = lax.axis_size("magnet"), lax.axis_size("slab")
    count = magnets * layers
    width, spokes = foil_warmth.shape[1], prior_block_warmth.shape[2]
    mates = [(i, i + 1) for i in range(0, count, 2)]
    crossing = [(i, i + 1) for i in range(1, count - 1, 2)]
    ends = [pair for pair in crossing if pair[1] % layers == 0]
    inner = [pair for pair in crossing if pair[1] % layers]

    def swap(array, pairs):
        return lax.ppermute(array, BOTH, pairs + [(j, i) for i, j in pairs])

    def call(kernel, name, shapes, *operands, scratch=(), spaces=None, cost=None, room=8 << 20):
        return pl.pallas_call(
            kernel,
            out_shape=tuple(jax.ShapeDtypeStruct(dims, f32) for dims in shapes),
            in_specs=[pl.BlockSpec(memory_space=spaces or pltpu.VMEM)] * len(operands),
            out_specs=(pl.BlockSpec(memory_space=pltpu.VMEM),) * len(shapes),
            scratch_shapes=scratch,
            cost_estimate=cost,
            compiler_params=pltpu.CompilerParams(vmem_limit_bytes=room),
            name=name,
        )(*operands)

    rows = (ROWS, width)
    (sheet,) = call(
        sheet_kernel,
        "sheet",
        [(4 * ROWS, width)],
        foil_warmth,
        terminal_voltage_input,
        foil_segment_pattern,
        underlying_block_map,
        scratch=[pltpu.VMEM(rows, jnp.int32), pltpu.VMEM(rows, jnp.int32), pltpu.SemaphoreType.DMA((4,))],
        spaces=pltpu.HBM,
        room=66846720,
    )
    across = swap(sheet, crossing)
    around = (swap(sheet, mates), across)
    stack = (layers * BLOCK, spokes)
    (packed,) = call(
        pack_kernel, "pack", [stack], prior_block_warmth.reshape(-1, spokes), substance_kind.reshape(-1, spokes)
    )
    (packed,) = call(gram_kernel, "gram", [stack], sheet, *around, packed)

    bricks = lax.all_to_all(packed.reshape(layers, BLOCK, 1, spokes), "slab", 0, 0)
    bins, *fields = call(
        functools.partial(deposit_kernel, layers),
        "deposit",
        [(SPAN, 16, spokes), rows, rows, rows],
        sheet,
        *around,
        scratch=[pltpu.VMEM((width // 128, 8 * SPAN, 128), f32)],
        cost=pl.CostEstimate(flops=10**8, bytes_accessed=2 * 10**6, transcendentals=0),
    )
    bricks, bins = lax.optimization_barrier((bricks.reshape(stack), bins))
    lines, over, beside, end = call(
        functools.partial(share_kernel, layers),
        "share",
        [(magnets * layers, spokes)] + [(2 * HALO * layers, spokes)] * 3,
        bricks,
    )
    lines = lax.all_to_all(lines.reshape(magnets, layers, spokes), "magnet", 0, 0).reshape(count, spokes)

    padded = (SPAN, layers + 2 * EDGE, spokes)
    plain = (SPAN, layers, spokes)
    stage = call(
        functools.partial(first_kernel, layers),
        "first",
        [padded, plain, plain],
        bricks,
        swap(over, inner),
        swap(beside, mates),
        swap(end, ends),
        scratch=[pltpu.VMEM(padded, f32), pltpu.VMEM(padded, f32)],
        cost=pl.CostEstimate(flops=0, bytes_accessed=0, transcendentals=0),
    )
    potential, heated = call(
        functools.partial(heat_kernel, layers),
        "heat",
        [rows, (layers * ROWS, spokes)],
        lines,
        *fields,
        bins,
        *stage,
        scratch=[pltpu.VMEM((2,) + padded, f32), pltpu.VMEM(padded, f32)],
    )
    heated = lax.all_to_all(heated.reshape(layers, ROWS, spokes), "slab", 0, 0)
    return potential, heated.reshape(prior_block_warmth.shape)


def solution(mesh):
    placed = (
        P(("magnet", "slab"), None),
        P(("magnet", "slab"), None),
        P(("magnet", "slab"), None),
        P("magnet", None),
        P("slab", "magnet", None),
        P("slab", "magnet", None),
    )
    return jax.shard_map(
        local,
        mesh=mesh,
        in_specs=placed,
        out_specs=(P(("magnet", "slab"), None), P("slab", "magnet", None)),
        check_vma=False,
    )
```

```python
import functools

import jax
import jax.numpy as jnp
from jax import lax
from jax.experimental import pallas as pl
from jax.experimental.pallas import tpu as pltpu
from jax.sharding import PartitionSpec as P

SUBSTEPS = 4
HALO = SUBSTEPS
ROWS = 8

leak_diag = 0.25
contact_gain = 4.0
copper_factor = 3.0
sheet_slope = 0.5
heat_factor = 1.5
time_step = 0.03
conduct_table = (0.3, 1.0, 2.0, 0.6)
capacity_table = (1.0, 1.5, 2.0, 1.2)
diffusivity_derivative = 0.4

SHIFT = 9.85
SCALE = 9.6
BOTH = ("magnet", "slab")
BLOCK = 2 * ROWS + 1


def place():
    size = lax.axis_size("slab")
    return lax.axis_index("magnet") * size + lax.axis_index("slab"), lax.axis_size("magnet") * size


def above(v):
    return pltpu.roll(v, 1, 0)


def below(v):
    return pltpu.roll(v, v.shape[0] - 1, 0)


def left(v):
    return pltpu.roll(v, 1, 1)


def right(v):
    return pltpu.roll(v, v.shape[1] - 1, 1)


def rows_inside(shape, margin):
    index, count = place()
    row = lax.broadcasted_iota(jnp.int32, shape, 0)
    low = jnp.where(index > 0, 0, margin)
    high = jnp.where(index < count - 1, shape[0], shape[0] - margin)
    return jnp.where((row >= low) & (row < high), 1.0, 0.0).astype(jnp.float32)


def sheet_kernel(warmth, voltage, pattern, cells, sheet, pattern_here, cells_here, sems):
    at = pl.multiple_of(lax.axis_index("slab") * ROWS, ROWS)
    copies = [
        pltpu.make_async_copy(pattern, pattern_here, sems.at[0]),
        pltpu.make_async_copy(cells.at[pl.ds(at, ROWS)], cells_here, sems.at[1]),
        pltpu.make_async_copy(warmth, sheet.at[0:ROWS], sems.at[2]),
        pltpu.make_async_copy(voltage, sheet.at[ROWS : 2 * ROWS], sems.at[3]),
    ]
    for copy in copies:
        copy.start()
    copies[0].wait()
    sheet[2 * ROWS : 3 * ROWS] = pattern_here[...].astype(jnp.float32)
    copies[1].wait()
    sheet[3 * ROWS : 4 * ROWS] = cells_here[...].astype(jnp.float32)
    copies[2].wait()
    copies[3].wait()


def pack_kernel(warmth, kind, packed):
    for slab in range(packed.shape[0] // BLOCK):
        part = slice(ROWS * slab, ROWS * (slab + 1))
        at = BLOCK * slab
        packed[at : at + ROWS] = warmth[part]
        packed[at + ROWS : at + 2 * ROWS] = kind[part].astype(jnp.float32)
        packed[at + 2 * ROWS : at + BLOCK] = jnp.zeros((1, packed.shape[1]), jnp.float32)


def sides(index, mate, cross):
    even = index % 2 == 0
    return jnp.where(even, cross, mate), jnp.where(even, mate, cross)


def window_of(own, mate, cross, i):
    part = slice(ROWS * i, ROWS * (i + 1))
    before, after = sides(place()[0], mate[part], cross[part])
    return jnp.concatenate([before, own[part], after], axis=0)


def basis(own, mate, cross):
    def window(i):
        return window_of(own, mate, cross, i)

    warmth, voltage, pattern = window(0), window(1), window(2)
    shape = warmth.shape
    inside = rows_inside(shape, ROWS)
    col = lax.broadcasted_iota(jnp.int32, shape, 1)
    last = col == shape[1] - 1
    sigma = inside * jnp.where(pattern == 1.0, copper_factor, 1.0) / (1.0 + sheet_slope * warmth)
    contact = jnp.where(pattern == 2.0, contact_gain, 0.0)
    c_down = 0.5 * (sigma + below(sigma))
    c_right = 0.5 * (sigma + jnp.where(last, 0.0, right(sigma)))
    c_left = jnp.where(col == 0, 0.5 * sigma, left(c_right))
    diagonal = leak_diag + contact + above(c_down) + c_down + c_left + c_right
    diagonal = (diagonal - SHIFT) * (1.0 / SCALE)
    o_down = c_down * inside * below(inside) * (1.0 / SCALE)
    o_up = above(o_down)
    o_right = jnp.where(last, 0.0, c_right) * (1.0 / SCALE)
    o_left = left(o_right)

    def apply(v):
        return diagonal * v - (o_up * above(v) + o_down * below(v)) - (o_left * left(v) + o_right * right(v))

    w0 = contact * voltage
    w1 = apply(w0)
    w2 = 2.0 * apply(w1) - w0
    return (w0, w1, w2), apply, inside, (c_down, c_right, c_left)


def gram_kernel(own, mate, cross, packed_in, packed):
    (w0, w1, w2), apply, _, _ = basis(own, mate, cross)
    w0, w1, w2, w3 = (w[ROWS : 2 * ROWS] for w in (w0, w1, w2, apply(w2)))
    lane = lax.broadcasted_iota(jnp.int32, (1, 128), 1)
    line = jnp.zeros((1, 128), jnp.float32)
    for i, (u, v) in enumerate(((w0, w0), (w0, w1), (w0, w2), (w1, w1), (w1, w2), (w2, w2), (w2, w3))):
        line = jnp.where(lane == i, jnp.sum(u * v, keepdims=True), line)
    for slab in range(packed.shape[0] // BLOCK):
        at = BLOCK * slab
        packed[at : at + 2 * ROWS] = packed_in[at : at + 2 * ROWS]
        packed[at + 2 * ROWS : at + BLOCK] = line


def solve_small(lines):
    total = jnp.sum(lines, axis=0, keepdims=True)
    g00, g01, g02, g11, g12, g22, k22 = (total[:, i : i + 1] for i in range(7))
    gram = ((g00, g01, g02), (g01, g11, g12), (g02, g12, g22))
    k11, k12 = 0.5 * (g12 + g01), 0.5 * (g22 + g02)
    shifted = ((g01, g11, g12), (g11, k11, k12), (g12, k12, k22))
    energy = [[SCALE * shifted[i][j] + SHIFT * gram[i][j] for j in range(3)] for i in range(3)]

    def form(m, v):
        return sum(v[i] * (v[i] * m[i][i] + 2.0 * sum((v[j] * m[i][j] for j in range(i + 1, len(v))), 0.0)) for i in range(len(v)))

    def ratio(num, den, low, high):
        return jnp.clip(num / jnp.maximum(den, 1e-37), low, high)

    alpha0 = g00 / energy[0][0]
    r = [1.0 - alpha0 * SHIFT, -alpha0 * SCALE]
    rr1 = jnp.maximum(form(gram, r), 0.0)
    beta = ratio(rr1, g00, 0.0, 1e4)
    p = [r[0] + beta, r[1]]
    alpha1 = ratio(rr1, form(energy, p), 0.05, 4.1)
    half = 0.5 * SCALE * p[1]
    image = [half + SHIFT * p[0], SCALE * p[0] + SHIFT * p[1], half]
    x = [alpha0 + alpha1 * p[0], alpha1 * p[1]]
    r = [r[0] - alpha1 * image[0], r[1] - alpha1 * image[1], -alpha1 * image[2]]
    rr2 = jnp.maximum(form(gram, r), 0.0)
    beta = ratio(rr2, rr1, 0.0, 1e4)
    p = [r[0] + beta * p[0], r[1] + beta * p[1], r[2]]
    alpha2 = ratio(rr2, form(energy, p), 0.05, 4.1)
    return x[0] + alpha2 * p[0], x[1] + alpha2 * p[1], alpha2 * p[2]


PAIRS = ((0, 0), (0, 1), (0, 2), (1, 1), (1, 2), (2, 2))
SPAN = ROWS + 2 * HALO
EDGE = 8


def deposit_kernel(layers, own, mate, cross, bins, w0_out, w1_out, w2_out, heats):
    spokes = bins.shape[-1]
    fields, _, inside, (c_down, c_right, c_left) = basis(own, mate, cross)
    for out, w in zip((w0_out, w1_out, w2_out), fields):
        out[...] = w[ROWS : 2 * ROWS]
    shape = inside.shape
    col = lax.broadcasted_iota(jnp.int32, shape, 1)
    last, first = col == shape[1] - 1, col == 0
    fields = [w * inside for w in fields]
    falls = [w - below(w) for w in fields]
    steps = [w - jnp.where(last, 0.0, right(w)) for w in fields]
    wanted = slice(ROWS - HALO, ROWS - HALO + SPAN)
    for pair, (i, j) in enumerate(PAIRS):
        q_down = c_down * (falls[i] * falls[j])
        q_right = c_right * (steps[i] * steps[j])
        q_left = jnp.where(first, c_left * (fields[i] * fields[j]), left(q_right))
        joule = (q_down + above(q_down)) + (q_right + q_left)
        factor = heat_factor if i == j else 2.0 * heat_factor
        joule = factor * joule[wanted]
        for part in range(heats.shape[0]):
            heats[part, SPAN * pair : SPAN * (pair + 1)] = joule[:, 128 * part : 128 * (part + 1)]
    for part in range(heats.shape[0]):
        heats[part, SPAN * len(PAIRS) :] = jnp.zeros((SPAN * (8 - len(PAIRS)), 128), jnp.float32)
    cell = window_of(own, mate, cross, 3)[wanted].astype(jnp.int32)
    azimuth = cell & (spokes - 1)
    outermost = jnp.where(cell >= (layers - 1) * spokes, 1.0, 0.0)
    spoke = lax.broadcasted_iota(jnp.int32, (spokes, shape[1]), 0)
    for row in range(1, SPAN - 1):
        pick = jnp.where(azimuth[row : row + 1] == spoke, 1.0, 0.0).astype(jnp.bfloat16)
        joule = jnp.concatenate([heats[part, pl.ds(row, 8, stride=SPAN), :] for part in range(heats.shape[0])], axis=1)
        upper = joule * outermost[row : row + 1]
        pieces = []
        for part in (joule - upper, upper):
            for _ in range(3):
                piece = part.astype(jnp.bfloat16)
                part = part - piece.astype(jnp.float32)
                pieces.append(piece)
        total = lax.dot_general(
            jnp.concatenate(pieces, axis=0), pick, (((1,), (1,)), ((), ())), preferred_element_type=jnp.float32
        )
        bins[row, 0:8] = total[0:8] + (total[8:16] + total[16:24])
        bins[row, 8:16] = total[24:32] + (total[32:40] + total[40:48])


def substep_rows(rows, layers, warm, cond, base, done):
    body = slice(EDGE, EDGE + layers)
    inward, outward = slice(EDGE - 1, EDGE - 1 + layers), slice(EDGE + 1, EDGE + 1 + layers)

    def conductivity(row):
        t = warm[row, body]
        k = base[row] * (1.0 + diffusivity_derivative * t)
        cond[row, body] = k
        return t, k

    def between(t, k, t_other, k_other):
        return (k + k_other) * (t_other - t)

    below_row = conductivity(rows[0] - 1)
    here = conductivity(rows[0])
    inner = between(*below_row, *here)
    for row in rows:
        t, k = here
        here = conductivity(row + 1)
        outer = between(t, k, *here)
        flux = outer - inner
        inner = outer
        flux = flux + between(t, k, warm[row, inward], cond[row, inward])
        flux = flux + between(t, k, warm[row, outward], cond[row, outward])
        face = between(t, k, right(t), right(k))
        done(row, t, flux + (face - left(face)))


def clear_edges(layers, *fields):
    for field in fields:
        blank = jnp.zeros((EDGE, field.shape[-1]), jnp.float32)
        field[0:EDGE] = blank
        field[EDGE + layers : 2 * EDGE + layers] = blank


def share_kernel(layers, own, lines, early, late):
    mine = own[pl.ds(2 * ROWS, layers, stride=BLOCK), :]
    for magnet in range(lines.shape[0] // layers):
        lines[layers * magnet : layers * (magnet + 1)] = mine
    for layer in range(layers):
        part = slice(2 * HALO * layer, 2 * HALO * (layer + 1))
        for out, first in ((early, BLOCK * layer), (late, BLOCK * layer + ROWS - HALO)):
            out[part] = jnp.concatenate([own[first : first + HALO], own[first + ROWS : first + ROWS + HALO]], axis=0)


def first_kernel(layers, own, after, before, fresh, base, store, warm, cond):
    block = own.shape[0] // layers
    index, count = place()
    body = slice(EDGE, EDGE + layers)
    for row in range(SPAN):

        def rows_of(array):
            if HALO <= row < HALO + ROWS:
                return own[pl.ds(ROWS * array + row - HALO, layers, stride=block), :]
            source = before if row < HALO else after
            return source[pl.ds(HALO * array + row % HALO, layers, stride=2 * HALO), :]

        there = 1.0
        if row < HALO:
            there = jnp.where(index > 0, 1.0, 0.0)
        elif row >= HALO + ROWS:
            there = jnp.where(index < count - 1, 1.0, 0.0)
        kind = rows_of(1)

        def table(values):
            return jnp.where(kind == 0.0, values[0], jnp.where(kind == 1.0, values[1], jnp.where(kind == 2.0, values[2], values[3])))

        base[row] = table(conduct_table) * there
        store[row] = table([0.5 * time_step / c for c in capacity_table]) * there
        warm[row, body] = rows_of(0)
        clear_edges(layers, warm.at[row], cond.at[row], fresh.at[row])

    def done(row, t, flux):
        fresh[row, body] = t + store[row] * flux

    substep_rows(range(1, SPAN - 1), layers, warm, cond, base, done)


def heat_kernel(layers, lines, w0, w1, w2, bins, fresh, base, store, potential, heated, warm, cond):
    spokes = heated.shape[-1]
    body = slice(EDGE, EDGE + layers)
    f = solve_small(lines[...])
    potential[...] = f[0] * w0[...] + f[1] * w1[...] + f[2] * w2[...]
    sublane = lax.broadcasted_iota(jnp.int32, (8, spokes), 0)
    weight = jnp.zeros((8, spokes), jnp.float32)
    for pair, (i, j) in enumerate(PAIRS):
        weight = jnp.where(sublane == pair, f[i] * f[j], weight)
    weight = 2.0 * weight
    heat = {}
    top = slice(layers - 8, layers)
    for row in range(1, SPAN - 1):
        inner = jnp.sum(weight * bins[row, 0:8], axis=0, keepdims=True)
        outer = jnp.sum(weight * bins[row, 8:16], axis=0, keepdims=True)
        heat[row] = jnp.where(sublane == 6, inner, jnp.where(sublane == 7, outer, 0.0))
        warm[1, row] = fresh[row]
        warm[1, row, EDGE + layers - 8 : EDGE + layers] = fresh[row, EDGE + layers - 8 : EDGE + layers] + store[row, top] * heat[row]
        clear_edges(layers, warm.at[0, row], cond.at[row])

    for substep in range(1, SUBSTEPS):

        def done(row, t, flux):
            flux = jnp.concatenate([flux[: layers - 8], flux[top] + heat[row]], axis=0)
            t = t + store[row] * flux
            if substep + 1 < SUBSTEPS:
                warm[1 - substep % 2, row, body] = t
            else:
                heated[pl.ds(row - HALO, layers, stride=ROWS), :] = t

        substep_rows(range(substep + 1, SPAN - 1 - substep), layers, warm.at[substep % 2], cond, base, done)


def local(foil_warmth, terminal_voltage_input, foil_segment_pattern, underlying_block_map, prior_block_warmth, substance_kind):
    f32 = jnp.float32
    magnets, layers = lax.axis_size("magnet"), lax.axis_size("slab")
    count = magnets * layers
    width, spokes = foil_warmth.shape[1], prior_block_warmth.shape[2]
    mates = [(i, i ^ 1) for i in range(count)]
    onward = [(i, i + 1) for i in range(count - 1)]
    backward = [(i + 1, i) for i in range(count - 1)]
    crossing = onward[1::2] + backward[1::2]

    def call(kernel, name, shapes, *operands, scratch=(), spaces=None, cost=None, room=8 << 20):
        return pl.pallas_call(
            kernel,
            out_shape=tuple(jax.ShapeDtypeStruct(dims, f32) for dims in shapes),
            in_specs=[pl.BlockSpec(memory_space=spaces or pltpu.VMEM)] * len(operands),
            out_specs=(pl.BlockSpec(memory_space=pltpu.VMEM),) * len(shapes),
            scratch_shapes=scratch,
            cost_estimate=cost,
            compiler_params=pltpu.CompilerParams(vmem_limit_bytes=room),
            name=name,
        )(*operands)

    rows = (ROWS, width)
    (sheet,) = call(
        sheet_kernel,
        "sheet",
        [(4 * ROWS, width)],
        foil_warmth,
        terminal_voltage_input,
        foil_segment_pattern,
        underlying_block_map,
        scratch=[pltpu.VMEM(rows, jnp.int32), pltpu.VMEM(rows, jnp.int32), pltpu.SemaphoreType.DMA((4,))],
        spaces=pltpu.HBM,
        room=66846720,
    )
    across = lax.ppermute(sheet, BOTH, crossing)
    around = (lax.ppermute(sheet, BOTH, mates), across)
    stack = (layers * BLOCK, spokes)
    (packed,) = call(
        pack_kernel, "pack", [stack], prior_block_warmth.reshape(-1, spokes), substance_kind.reshape(-1, spokes)
    )
    (packed,) = call(gram_kernel, "gram", [stack], sheet, *around, packed)

    bricks = lax.all_to_all(packed.reshape(layers, BLOCK, 1, spokes), "slab", 0, 0)
    bins, *fields = call(
        functools.partial(deposit_kernel, layers),
        "deposit",
        [(SPAN, 16, spokes), rows, rows, rows],
        sheet,
        *around,
        scratch=[pltpu.VMEM((width // 128, 8 * SPAN, 128), f32)],
        cost=pl.CostEstimate(flops=10**8, bytes_accessed=2 * 10**6, transcendentals=0),
    )
    bricks, bins = lax.optimization_barrier((bricks.reshape(stack), bins))
    lines, early, late = call(
        functools.partial(share_kernel, layers),
        "share",
        [(magnets * layers, spokes)] + [(2 * HALO * layers, spokes)] * 2,
        bricks,
    )
    lines = lax.all_to_all(lines.reshape(magnets, layers, spokes), "magnet", 0, 0).reshape(count, spokes)

    padded = (SPAN, layers + 2 * EDGE, spokes)
    plain = (SPAN, layers, spokes)
    stage = call(
        functools.partial(first_kernel, layers),
        "first",
        [padded, plain, plain],
        bricks,
        lax.ppermute(early, BOTH, backward),
        lax.ppermute(late, BOTH, onward),
        scratch=[pltpu.VMEM(padded, f32), pltpu.VMEM(padded, f32)],
        cost=pl.CostEstimate(flops=0, bytes_accessed=0, transcendentals=0),
    )
    potential, heated = call(
        functools.partial(heat_kernel, layers),
        "heat",
        [rows, (layers * ROWS, spokes)],
        lines,
        *fields,
        bins,
        *stage,
        scratch=[pltpu.VMEM((2,) + padded, f32), pltpu.VMEM(padded, f32)],
    )
    heated = lax.all_to_all(heated.reshape(layers, ROWS, spokes), "slab", 0, 0)
    return potential, heated.reshape(prior_block_warmth.shape)


def solution(mesh):
    placed = (
        P(("magnet", "slab"), None),
        P(("magnet", "slab"), None),
        P(("magnet", "slab"), None),
        P("magnet", None),
        P("slab", "magnet", None),
        P("slab", "magnet", None),
    )
    return jax.shard_map(
        local,
        mesh=mesh,
        in_specs=placed,
        out_specs=(P(("magnet", "slab"), None), P("slab", "magnet", None)),
        check_vma=False,
    )
```

```python
import functools

import jax
import jax.numpy as jnp
from jax import lax
from jax.experimental import pallas as pl
from jax.experimental.pallas import tpu as pltpu
from jax.sharding import PartitionSpec as P

SUBSTEPS = 4
HALO = SUBSTEPS
ROWS = 8

leak_diag = 0.25
contact_gain = 4.0
copper_factor = 3.0
sheet_slope = 0.5
heat_factor = 1.5
time_step = 0.03
conduct_table = (0.3, 1.0, 2.0, 0.6)
capacity_table = (1.0, 1.5, 2.0, 1.2)
diffusivity_derivative = 0.4

SHIFT = 9.85
SCALE = 9.6
BOTH = ("magnet", "slab")
BLOCK = 2 * ROWS + 1


def place():
    size = lax.axis_size("slab")
    return lax.axis_index("magnet") * size + lax.axis_index("slab"), lax.axis_size("magnet") * size


def above(v):
    return pltpu.roll(v, 1, 0)


def below(v):
    return pltpu.roll(v, v.shape[0] - 1, 0)


def left(v):
    return pltpu.roll(v, 1, 1)


def right(v):
    return pltpu.roll(v, v.shape[1] - 1, 1)


def rows_inside(shape, margin):
    index, count = place()
    row = lax.broadcasted_iota(jnp.int32, shape, 0)
    low = jnp.where(index > 0, 0, margin)
    high = jnp.where(index < count - 1, shape[0], shape[0] - margin)
    return jnp.where((row >= low) & (row < high), 1.0, 0.0).astype(jnp.float32)


def sheet_kernel(warmth, voltage, pattern, cells, sheet, pattern_here, cells_here, sems):
    at = pl.multiple_of(lax.axis_index("slab") * ROWS, ROWS)
    copies = [
        pltpu.make_async_copy(pattern, pattern_here, sems.at[0]),
        pltpu.make_async_copy(cells.at[pl.ds(at, ROWS)], cells_here, sems.at[1]),
        pltpu.make_async_copy(warmth, sheet.at[0:ROWS], sems.at[2]),
        pltpu.make_async_copy(voltage, sheet.at[ROWS : 2 * ROWS], sems.at[3]),
    ]
    for copy in copies:
        copy.start()
    copies[0].wait()
    sheet[2 * ROWS : 3 * ROWS] = pattern_here[...].astype(jnp.float32)
    copies[1].wait()
    sheet[3 * ROWS : 4 * ROWS] = cells_here[...].astype(jnp.float32)
    copies[2].wait()
    copies[3].wait()


def pack_kernel(warmth, kind, packed):
    for slab in range(packed.shape[0] // BLOCK):
        part = slice(ROWS * slab, ROWS * (slab + 1))
        at = BLOCK * slab
        packed[at : at + ROWS] = warmth[part]
        packed[at + ROWS : at + 2 * ROWS] = kind[part].astype(jnp.float32)
        packed[at + 2 * ROWS : at + BLOCK] = jnp.zeros((1, packed.shape[1]), jnp.float32)


def sides(index, mate, cross):
    even = index % 2 == 0
    return jnp.where(even, cross, mate), jnp.where(even, mate, cross)


def window_of(own, mate, cross, i):
    part = slice(ROWS * i, ROWS * (i + 1))
    before, after = sides(place()[0], mate[part], cross[part])
    return jnp.concatenate([before, own[part], after], axis=0)


def basis(own, mate, cross):
    def window(i):
        return window_of(own, mate, cross, i)

    warmth, voltage, pattern = window(0), window(1), window(2)
    shape = warmth.shape
    inside = rows_inside(shape, ROWS)
    col = lax.broadcasted_iota(jnp.int32, shape, 1)
    last = col == shape[1] - 1
    sigma = inside * jnp.where(pattern == 1.0, copper_factor, 1.0) / (1.0 + sheet_slope * warmth)
    contact = jnp.where(pattern == 2.0, contact_gain, 0.0)
    c_down = 0.5 * (sigma + below(sigma))
    c_right = 0.5 * (sigma + jnp.where(last, 0.0, right(sigma)))
    c_left = jnp.where(col == 0, 0.5 * sigma, left(c_right))
    diagonal = leak_diag + contact + above(c_down) + c_down + c_left + c_right
    diagonal = (diagonal - SHIFT) * (1.0 / SCALE)
    o_down = c_down * inside * below(inside) * (1.0 / SCALE)
    o_up = above(o_down)
    o_right = jnp.where(last, 0.0, c_right) * (1.0 / SCALE)
    o_left = left(o_right)

    def apply(v):
        return diagonal * v - (o_up * above(v) + o_down * below(v)) - (o_left * left(v) + o_right * right(v))

    w0 = contact * voltage
    w1 = apply(w0)
    w2 = 2.0 * apply(w1) - w0
    return (w0, w1, w2), apply, inside, (c_down, c_right, c_left)


def gram_kernel(own, mate, cross, packed_in, packed):
    (w0, w1, w2), apply, _, _ = basis(own, mate, cross)
    w0, w1, w2, w3 = (w[ROWS : 2 * ROWS] for w in (w0, w1, w2, apply(w2)))
    lane = lax.broadcasted_iota(jnp.int32, (1, 128), 1)
    line = jnp.zeros((1, 128), jnp.float32)
    for i, (u, v) in enumerate(((w0, w0), (w0, w1), (w0, w2), (w1, w1), (w1, w2), (w2, w2), (w2, w3))):
        line = jnp.where(lane == i, jnp.sum(u * v, keepdims=True), line)
    for slab in range(packed.shape[0] // BLOCK):
        at = BLOCK * slab
        packed[at : at + 2 * ROWS] = packed_in[at : at + 2 * ROWS]
        packed[at + 2 * ROWS : at + BLOCK] = line


def solve_small(lines):
    total = jnp.sum(lines, axis=0, keepdims=True)
    total = total / total[:, 0:1]
    g00, g01, g02, g11, g12, g22, k22 = (total[:, i : i + 1] for i in range(7))
    gram = ((g00, g01, g02), (g01, g11, g12), (g02, g12, g22))
    k11, k12 = 0.5 * (g12 + g01), 0.5 * (g22 + g02)
    shifted = ((g01, g11, g12), (g11, k11, k12), (g12, k12, k22))
    energy = [[SCALE * shifted[i][j] + SHIFT * gram[i][j] for j in range(3)] for i in range(3)]

    def form(m, v):
        return sum(v[i] * (v[i] * m[i][i] + 2.0 * sum((v[j] * m[i][j] for j in range(i + 1, len(v))), 0.0)) for i in range(len(v)))

    def ratio(num, den, low, high):
        return jnp.clip(num / jnp.maximum(den, 1e-37), low, high)

    alpha0 = g00 / energy[0][0]
    r = [1.0 - alpha0 * SHIFT, -alpha0 * SCALE]
    rr1 = jnp.maximum(form(gram, r), 0.0)
    beta = ratio(rr1, g00, 0.0, 1e4)
    p = [r[0] + beta, r[1]]
    alpha1 = ratio(rr1, form(energy, p), 0.05, 4.1)
    half = 0.5 * SCALE * p[1]
    image = [half + SHIFT * p[0], SCALE * p[0] + SHIFT * p[1], half]
    x = [alpha0 + alpha1 * p[0], alpha1 * p[1]]
    r = [r[0] - alpha1 * image[0], r[1] - alpha1 * image[1], -alpha1 * image[2]]
    rr2 = jnp.maximum(form(gram, r), 0.0)
    beta = ratio(rr2, rr1, 0.0, 1e4)
    p = [r[0] + beta * p[0], r[1] + beta * p[1], r[2]]
    alpha2 = ratio(rr2, form(energy, p), 0.05, 4.1)
    return x[0] + alpha2 * p[0], x[1] + alpha2 * p[1], alpha2 * p[2]


PAIRS = ((0, 0), (0, 1), (0, 2), (1, 1), (1, 2), (2, 2))
SPAN = ROWS + 2 * HALO
EDGE = 8


def deposit_kernel(layers, own, mate, cross, bins, w0_out, w1_out, w2_out, heats):
    spokes = bins.shape[-1]
    fields, _, inside, (c_down, c_right, c_left) = basis(own, mate, cross)
    for out, w in zip((w0_out, w1_out, w2_out), fields):
        out[...] = w[ROWS : 2 * ROWS]
    shape = inside.shape
    col = lax.broadcasted_iota(jnp.int32, shape, 1)
    last, first = col == shape[1] - 1, col == 0
    fields = [w * inside for w in fields]
    falls = [w - below(w) for w in fields]
    steps = [w - jnp.where(last, 0.0, right(w)) for w in fields]
    wanted = slice(ROWS - HALO, ROWS - HALO + SPAN)
    for pair, (i, j) in enumerate(PAIRS):
        q_down = c_down * (falls[i] * falls[j])
        q_right = c_right * (steps[i] * steps[j])
        q_left = jnp.where(first, c_left * (fields[i] * fields[j]), left(q_right))
        joule = (q_down + above(q_down)) + (q_right + q_left)
        factor = heat_factor if i == j else 2.0 * heat_factor
        joule = factor * joule[wanted]
        for part in range(heats.shape[0]):
            heats[part, SPAN * pair : SPAN * (pair + 1)] = joule[:, 128 * part : 128 * (part + 1)]
    for part in range(heats.shape[0]):
        heats[part, SPAN * len(PAIRS) :] = jnp.zeros((SPAN * (8 - len(PAIRS)), 128), jnp.float32)
    cell = window_of(own, mate, cross, 3)[wanted].astype(jnp.int32)
    azimuth = cell & (spokes - 1)
    outermost = jnp.where(cell >= (layers - 1) * spokes, 1.0, 0.0)
    spoke = lax.broadcasted_iota(jnp.int32, (spokes, shape[1]), 0)
    for row in range(1, SPAN - 1):
        pick = jnp.where(azimuth[row : row + 1] == spoke, 1.0, 0.0).astype(jnp.bfloat16)
        joule = jnp.concatenate([heats[part, pl.ds(row, 8, stride=SPAN), :] for part in range(heats.shape[0])], axis=1)
        upper = joule * outermost[row : row + 1]
        pieces = []
        for part in (joule - upper, upper):
            for _ in range(3):
                piece = part.astype(jnp.bfloat16)
                part = part - piece.astype(jnp.float32)
                pieces.append(piece)
        total = lax.dot_general(
            jnp.concatenate(pieces, axis=0), pick, (((1,), (1,)), ((), ())), preferred_element_type=jnp.float32
        )
        bins[row, 0:8] = total[0:8] + (total[8:16] + total[16:24])
        bins[row, 8:16] = total[24:32] + (total[32:40] + total[40:48])


def substep_rows(rows, layers, warm, cond, base, done):
    body = slice(EDGE, EDGE + layers)
    inward, outward = slice(EDGE - 1, EDGE - 1 + layers), slice(EDGE + 1, EDGE + 1 + layers)

    def conductivity(row):
        t = warm[row, body]
        k = base[row] * (1.0 + diffusivity_derivative * t)
        cond[row, body] = k
        return t, k

    def between(t, k, t_other, k_other):
        return (k + k_other) * (t_other - t)

    below_row = conductivity(rows[0] - 1)
    here = conductivity(rows[0])
    inner = between(*below_row, *here)
    for row in rows:
        t, k = here
        here = conductivity(row + 1)
        outer = between(t, k, *here)
        flux = outer - inner
        inner = outer
        flux = flux + between(t, k, warm[row, inward], cond[row, inward])
        flux = flux + between(t, k, warm[row, outward], cond[row, outward])
        face = between(t, k, right(t), right(k))
        done(row, t, flux + (face - left(face)))


def clear_edges(layers, *fields):
    for field in fields:
        blank = jnp.zeros((EDGE, field.shape[-1]), jnp.float32)
        field[0:EDGE] = blank
        field[EDGE + layers : 2 * EDGE + layers] = blank


def share_kernel(layers, own, lines, for_cross):
    mine = own[pl.ds(2 * ROWS, layers, stride=BLOCK), :]
    for magnet in range(lines.shape[0] // layers):
        lines[layers * magnet : layers * (magnet + 1)] = mine
    even = place()[0] % 2 == 0
    for layer in range(layers):
        at = BLOCK * layer

        def rows_from(first):
            return jnp.concatenate([own[at + i + first : at + i + first + HALO] for i in (0, ROWS)], axis=0)

        early, late = rows_from(0), rows_from(ROWS - HALO)
        part = slice(2 * HALO * layer, 2 * HALO * (layer + 1))
        for_cross[part] = jnp.where(even, early, late)


def first_kernel(layers, own, cross, mate, fresh, base, store, warm, cond):
    block = own.shape[0] // layers
    index, count = place()
    body = slice(EDGE, EDGE + layers)
    for row in range(SPAN):

        def rows_of(array):
            if HALO <= row < HALO + ROWS:
                return own[pl.ds(ROWS * array + row - HALO, layers, stride=block), :]
            near = mate[pl.ds(ROWS * array + (row + ROWS - HALO) % ROWS, layers, stride=block), :]
            far = cross[pl.ds(HALO * array + row % HALO, layers, stride=2 * HALO), :]
            return sides(index, near, far)[int(row >= HALO)]

        there = 1.0
        if row < HALO:
            there = jnp.where(index > 0, 1.0, 0.0)
        elif row >= HALO + ROWS:
            there = jnp.where(index < count - 1, 1.0, 0.0)
        kind = rows_of(1)

        def table(values):
            return jnp.where(kind == 0.0, values[0], jnp.where(kind == 1.0, values[1], jnp.where(kind == 2.0, values[2], values[3])))

        base[row] = table(conduct_table) * there
        store[row] = table([0.5 * time_step / c for c in capacity_table]) * there
        warm[row, body] = rows_of(0)
        clear_edges(layers, warm.at[row], cond.at[row], fresh.at[row])

    def done(row, t, flux):
        fresh[row, body] = t + store[row] * flux

    substep_rows(range(1, SPAN - 1), layers, warm, cond, base, done)


def heat_kernel(layers, lines, w0, w1, w2, bins, fresh, base, store, potential, heated, warm, cond):
    spokes = heated.shape[-1]
    body = slice(EDGE, EDGE + layers)
    f = solve_small(lines[...])
    potential[...] = f[0] * w0[...] + f[1] * w1[...] + f[2] * w2[...]
    sublane = lax.broadcasted_iota(jnp.int32, (8, spokes), 0)
    weight = jnp.zeros((8, spokes), jnp.float32)
    for pair, (i, j) in enumerate(PAIRS):
        weight = jnp.where(sublane == pair, f[i] * f[j], weight)
    weight = 2.0 * weight
    heat = {}
    top = slice(layers - 8, layers)
    for row in range(1, SPAN - 1):
        inner = jnp.sum(weight * bins[row, 0:8], axis=0, keepdims=True)
        outer = jnp.sum(weight * bins[row, 8:16], axis=0, keepdims=True)
        heat[row] = jnp.where(sublane == 6, inner, jnp.where(sublane == 7, outer, 0.0))
        warm[1, row] = fresh[row]
        warm[1, row, EDGE + layers - 8 : EDGE + layers] = fresh[row, EDGE + layers - 8 : EDGE + layers] + store[row, top] * heat[row]
        clear_edges(layers, warm.at[0, row], cond.at[row])

    for substep in range(1, SUBSTEPS):

        def done(row, t, flux):
            flux = jnp.concatenate([flux[: layers - 8], flux[top] + heat[row]], axis=0)
            t = t + store[row] * flux
            if substep + 1 < SUBSTEPS:
                warm[1 - substep % 2, row, body] = t
            else:
                heated[pl.ds(row - HALO, layers, stride=ROWS), :] = t

        substep_rows(range(substep + 1, SPAN - 1 - substep), layers, warm.at[substep % 2], cond, base, done)


def local(foil_warmth, terminal_voltage_input, foil_segment_pattern, underlying_block_map, prior_block_warmth, substance_kind):
    f32 = jnp.float32
    magnets, layers = lax.axis_size("magnet"), lax.axis_size("slab")
    count = magnets * layers
    width, spokes = foil_warmth.shape[1], prior_block_warmth.shape[2]
    mates = [(i, i ^ 1) for i in range(count)]
    crossing = [(i, i + 1) for i in range(1, count - 1, 2)] + [(i + 1, i) for i in range(1, count - 1, 2)]

    def exchange(for_mate, for_cross):
        over = lax.ppermute(for_cross, BOTH, crossing)
        return lax.ppermute(for_mate, BOTH, mates), over

    def call(kernel, name, shapes, *operands, scratch=(), spaces=None, cost=None, room=8 << 20):
        return pl.pallas_call(
            kernel,
            out_shape=tuple(jax.ShapeDtypeStruct(dims, f32) for dims in shapes),
            in_specs=[pl.BlockSpec(memory_space=spaces or pltpu.VMEM)] * len(operands),
            out_specs=(pl.BlockSpec(memory_space=pltpu.VMEM),) * len(shapes),
            scratch_shapes=scratch,
            cost_estimate=cost,
            compiler_params=pltpu.CompilerParams(vmem_limit_bytes=room),
            name=name,
        )(*operands)

    rows = (ROWS, width)
    (sheet,) = call(
        sheet_kernel,
        "sheet",
        [(4 * ROWS, width)],
        foil_warmth,
        terminal_voltage_input,
        foil_segment_pattern,
        underlying_block_map,
        scratch=[pltpu.VMEM(rows, jnp.int32), pltpu.VMEM(rows, jnp.int32), pltpu.SemaphoreType.DMA((4,))],
        spaces=pltpu.HBM,
        room=66846720,
    )
    around = exchange(sheet, sheet)
    stack = (layers * BLOCK, spokes)
    (packed,) = call(
        pack_kernel, "pack", [stack], prior_block_warmth.reshape(-1, spokes), substance_kind.reshape(-1, spokes)
    )
    (packed,) = call(gram_kernel, "gram", [stack], sheet, *around, packed)

    bricks = lax.all_to_all(packed.reshape(layers, BLOCK, 1, spokes), "slab", 0, 0)
    bins, *fields = call(
        functools.partial(deposit_kernel, layers),
        "deposit",
        [(SPAN, 16, spokes), rows, rows, rows],
        sheet,
        *around,
        scratch=[pltpu.VMEM((width // 128, 8 * SPAN, 128), f32)],
        cost=pl.CostEstimate(flops=10**8, bytes_accessed=2 * 10**6, transcendentals=0),
    )
    bricks, bins = lax.optimization_barrier((bricks.reshape(stack), bins))
    lines, over = call(
        functools.partial(share_kernel, layers),
        "share",
        [(magnets * layers, spokes)] + [(2 * HALO * layers, spokes)],
        bricks,
    )
    lines = lax.all_to_all(lines.reshape(magnets, layers, spokes), "magnet", 0, 0).reshape(count, spokes)

    padded = (SPAN, layers + 2 * EDGE, spokes)
    plain = (SPAN, layers, spokes)
    stage = call(
        functools.partial(first_kernel, layers),
        "first",
        [padded, plain, plain],
        bricks,
        *exchange(bricks, over)[::-1],
        scratch=[pltpu.VMEM(padded, f32), pltpu.VMEM(padded, f32)],
        cost=pl.CostEstimate(flops=0, bytes_accessed=0, transcendentals=0),
    )
    potential, heated = call(
        functools.partial(heat_kernel, layers),
        "heat",
        [rows, (layers * ROWS, spokes)],
        lines,
        *fields,
        bins,
        *stage,
        scratch=[pltpu.VMEM((2,) + padded, f32), pltpu.VMEM(padded, f32)],
    )
    heated = lax.all_to_all(heated.reshape(layers, ROWS, spokes), "slab", 0, 0)
    return potential, heated.reshape(prior_block_warmth.shape)


def solution(mesh):
    placed = (
        P(("magnet", "slab"), None),
        P(("magnet", "slab"), None),
        P(("magnet", "slab"), None),
        P("magnet", None),
        P("slab", "magnet", None),
        P("slab", "magnet", None),
    )
    return jax.shard_map(
        local,
        mesh=mesh,
        in_specs=placed,
        out_specs=(P(("magnet", "slab"), None), P("slab", "magnet", None)),
        check_vma=False,
    )
```

```python
import functools

import jax
import jax.numpy as jnp
from jax import lax
from jax.experimental import pallas as pl
from jax.experimental.pallas import tpu as pltpu
from jax.sharding import PartitionSpec as P

SUBSTEPS = 4
HALO = SUBSTEPS
ROWS = 8

leak_diag = 0.25
contact_gain = 4.0
copper_factor = 3.0
sheet_slope = 0.5
heat_factor = 1.5
time_step = 0.03
conduct_table = (0.3, 1.0, 2.0, 0.6)
capacity_table = (1.0, 1.5, 2.0, 1.2)
diffusivity_derivative = 0.4

SHIFT = 9.85
SCALE = 9.6
BOTH = ("magnet", "slab")
BLOCK = 2 * ROWS + 1
COPIES = 24


def place():
    size = lax.axis_size("slab")
    return lax.axis_index("magnet") * size + lax.axis_index("slab"), lax.axis_size("magnet") * size


def above(v):
    return pltpu.roll(v, 1, 0)


def below(v):
    return pltpu.roll(v, v.shape[0] - 1, 0)


def left(v):
    return pltpu.roll(v, 1, 1)


def right(v):
    return pltpu.roll(v, v.shape[1] - 1, 1)


def rows_inside(shape, margin):
    index, count = place()
    row = lax.broadcasted_iota(jnp.int32, shape, 0)
    low = jnp.where(index > 0, 0, margin)
    high = jnp.where(index < count - 1, shape[0], shape[0] - margin)
    return jnp.where((row >= low) & (row < high), 1.0, 0.0).astype(jnp.float32)


def sheet_kernel(warmth, voltage, pattern, cells, sheet, pattern_here, cells_here, sems):
    at = pl.multiple_of(lax.axis_index("slab") * ROWS, ROWS)
    copies = [
        pltpu.make_async_copy(pattern, pattern_here, sems.at[0]),
        pltpu.make_async_copy(cells.at[pl.ds(at, ROWS)], cells_here, sems.at[1]),
        pltpu.make_async_copy(warmth, sheet.at[0:ROWS], sems.at[2]),
        pltpu.make_async_copy(voltage, sheet.at[ROWS : 2 * ROWS], sems.at[3]),
    ]
    for copy in copies:
        copy.start()
    copies[0].wait()
    sheet[2 * ROWS : 3 * ROWS] = pattern_here[...].astype(jnp.float32)
    copies[1].wait()
    sheet[3 * ROWS : 4 * ROWS] = cells_here[...].astype(jnp.float32)
    copies[2].wait()
    copies[3].wait()


def pack_kernel(warmth, kind, packed):
    for slab in range(packed.shape[0] // BLOCK):
        part = slice(ROWS * slab, ROWS * (slab + 1))
        at = BLOCK * slab
        packed[at : at + ROWS] = warmth[part]
        packed[at + ROWS : at + 2 * ROWS] = kind[part].astype(jnp.float32)
        packed[at + 2 * ROWS : at + BLOCK] = jnp.zeros((1, packed.shape[1]), jnp.float32)


def sides(index, mate, cross):
    even = index % 2 == 0
    return jnp.where(even, cross, mate), jnp.where(even, mate, cross)


def window_of(own, mate, cross, i):
    part = slice(ROWS * i, ROWS * (i + 1))
    before, after = sides(place()[0], mate[part], cross[part])
    return jnp.concatenate([before, own[part], after], axis=0)


def basis(own, mate, cross):
    def window(i):
        return window_of(own, mate, cross, i)

    warmth, voltage, pattern = window(0), window(1), window(2)
    shape = warmth.shape
    inside = rows_inside(shape, ROWS)
    col = lax.broadcasted_iota(jnp.int32, shape, 1)
    last = col == shape[1] - 1
    sigma = inside * jnp.where(pattern == 1.0, copper_factor, 1.0) / (1.0 + sheet_slope * warmth)
    contact = jnp.where(pattern == 2.0, contact_gain, 0.0)
    c_down = 0.5 * (sigma + below(sigma))
    c_right = 0.5 * (sigma + jnp.where(last, 0.0, right(sigma)))
    c_left = jnp.where(col == 0, 0.5 * sigma, left(c_right))
    diagonal = leak_diag + contact + above(c_down) + c_down + c_left + c_right
    diagonal = (diagonal - SHIFT) * (1.0 / SCALE)
    o_down = c_down * inside * below(inside) * (1.0 / SCALE)
    o_up = above(o_down)
    o_right = jnp.where(last, 0.0, c_right) * (1.0 / SCALE)
    o_left = left(o_right)

    def apply(v):
        return diagonal * v - (o_up * above(v) + o_down * below(v)) - (o_left * left(v) + o_right * right(v))

    w0 = contact * voltage
    w1 = apply(w0)
    w2 = 2.0 * apply(w1) - w0
    return (w0, w1, w2), apply, inside, (c_down, c_right, c_left)


def gram_kernel(own, cross, mate, packed_in, packed):
    (w0, w1, w2), apply, _, _ = basis(own, mate, cross)
    w0, w1, w2, w3 = (w[ROWS : 2 * ROWS] for w in (w0, w1, w2, apply(w2)))
    lane = lax.broadcasted_iota(jnp.int32, (1, 128), 1)
    line = jnp.zeros((1, 128), jnp.float32)
    for i, (u, v) in enumerate(((w0, w0), (w0, w1), (w0, w2), (w1, w1), (w1, w2), (w2, w2), (w2, w3))):
        line = jnp.where(lane == i, jnp.sum(u * v, keepdims=True), line)
    for slab in range(packed.shape[0] // BLOCK):
        at = BLOCK * slab
        packed[at : at + 2 * ROWS] = packed_in[at : at + 2 * ROWS]
        packed[at + 2 * ROWS : at + BLOCK] = line


def solve_small(lines):
    total = jnp.sum(lines, axis=0, keepdims=True)
    g00, g01, g02, g11, g12, g22, k22 = (total[:, i : i + 1] for i in range(7))
    gram = ((g00, g01, g02), (g01, g11, g12), (g02, g12, g22))
    k11, k12 = 0.5 * (g12 + g01), 0.5 * (g22 + g02)
    shifted = ((g01, g11, g12), (g11, k11, k12), (g12, k12, k22))
    energy = [[SCALE * shifted[i][j] + SHIFT * gram[i][j] for j in range(3)] for i in range(3)]

    def form(m, v):
        return sum(v[i] * (v[i] * m[i][i] + 2.0 * sum((v[j] * m[i][j] for j in range(i + 1, len(v))), 0.0)) for i in range(len(v)))

    def ratio(num, den, low, high):
        return jnp.clip(num / jnp.maximum(den, 1e-37), low, high)

    alpha0 = g00 / energy[0][0]
    r = [1.0 - alpha0 * SHIFT, -alpha0 * SCALE]
    rr1 = jnp.maximum(form(gram, r), 0.0)
    beta = ratio(rr1, g00, 0.0, 1e4)
    p = [r[0] + beta, r[1]]
    alpha1 = ratio(rr1, form(energy, p), 0.05, 4.1)
    half = 0.5 * SCALE * p[1]
    image = [half + SHIFT * p[0], SCALE * p[0] + SHIFT * p[1], half]
    x = [alpha0 + alpha1 * p[0], alpha1 * p[1]]
    r = [r[0] - alpha1 * image[0], r[1] - alpha1 * image[1], -alpha1 * image[2]]
    rr2 = jnp.maximum(form(gram, r), 0.0)
    beta = ratio(rr2, rr1, 0.0, 1e4)
    p = [r[0] + beta * p[0], r[1] + beta * p[1], r[2]]
    alpha2 = ratio(rr2, form(energy, p), 0.05, 4.1)
    return x[0] + alpha2 * p[0], x[1] + alpha2 * p[1], alpha2 * p[2]


PAIRS = ((0, 0), (0, 1), (0, 2), (1, 1), (1, 2), (2, 2))
SPAN = ROWS + 2 * HALO
EDGE = 8


def deposit_kernel(layers, own, mate, cross, bins, w0_out, w1_out, w2_out, heats):
    spokes = bins.shape[-1]
    fields, _, inside, (c_down, c_right, c_left) = basis(own, mate, cross)
    for out, w in zip((w0_out, w1_out, w2_out), fields):
        out[...] = w[ROWS : 2 * ROWS]
    shape = inside.shape
    col = lax.broadcasted_iota(jnp.int32, shape, 1)
    last, first = col == shape[1] - 1, col == 0
    fields = [w * inside for w in fields]
    falls = [w - below(w) for w in fields]
    steps = [w - jnp.where(last, 0.0, right(w)) for w in fields]
    wanted = slice(ROWS - HALO, ROWS - HALO + SPAN)
    for pair, (i, j) in enumerate(PAIRS):
        q_down = c_down * (falls[i] * falls[j])
        q_right = c_right * (steps[i] * steps[j])
        q_left = jnp.where(first, c_left * (fields[i] * fields[j]), left(q_right))
        joule = (q_down + above(q_down)) + (q_right + q_left)
        factor = heat_factor if i == j else 2.0 * heat_factor
        joule = factor * joule[wanted]
        for part in range(heats.shape[0]):
            heats[part, SPAN * pair : SPAN * (pair + 1)] = joule[:, 128 * part : 128 * (part + 1)]
    for part in range(heats.shape[0]):
        heats[part, SPAN * len(PAIRS) :] = jnp.zeros((SPAN * (8 - len(PAIRS)), 128), jnp.float32)
    cell = window_of(own, mate, cross, 3)[wanted].astype(jnp.int32)
    azimuth = cell & (spokes - 1)
    outermost = jnp.where(cell >= (layers - 1) * spokes, 1.0, 0.0)
    spoke = lax.broadcasted_iota(jnp.int32, (spokes, shape[1]), 0)
    for row in range(1, SPAN - 1):
        pick = jnp.where(azimuth[row : row + 1] == spoke, 1.0, 0.0).astype(jnp.bfloat16)
        joule = jnp.concatenate([heats[part, pl.ds(row, 8, stride=SPAN), :] for part in range(heats.shape[0])], axis=1)
        upper = joule * outermost[row : row + 1]
        pieces = []
        for part in (joule - upper, upper):
            for _ in range(3):
                piece = part.astype(jnp.bfloat16)
                part = part - piece.astype(jnp.float32)
                pieces.append(piece)
        total = lax.dot_general(
            jnp.concatenate(pieces, axis=0), pick, (((1,), (1,)), ((), ())), preferred_element_type=jnp.float32
        )
        bins[row, 0:8] = total[0:8] + (total[8:16] + total[16:24])
        bins[row, 8:16] = total[24:32] + (total[32:40] + total[40:48])


def substep_rows(rows, layers, warm, cond, base, done):
    body = slice(EDGE, EDGE + layers)
    inward, outward = slice(EDGE - 1, EDGE - 1 + layers), slice(EDGE + 1, EDGE + 1 + layers)

    def conductivity(row):
        t = warm[row, body]
        k = base[row] * (1.0 + diffusivity_derivative * t)
        cond[row, body] = k
        return t, k

    def between(t, k, t_other, k_other):
        return (k + k_other) * (t_other - t)

    below_row = conductivity(rows[0] - 1)
    here = conductivity(rows[0])
    inner = between(*below_row, *here)
    for row in rows:
        t, k = here
        here = conductivity(row + 1)
        outer = between(t, k, *here)
        flux = outer - inner
        inner = outer
        flux = flux + between(t, k, warm[row, inward], cond[row, inward])
        flux = flux + between(t, k, warm[row, outward], cond[row, outward])
        face = between(t, k, right(t), right(k))
        done(row, t, flux + (face - left(face)))


def clear_edges(layers, *fields):
    for field in fields:
        blank = jnp.zeros((EDGE, field.shape[-1]), jnp.float32)
        field[0:EDGE] = blank
        field[EDGE + layers : 2 * EDGE + layers] = blank


def share_kernel(layers, own, lines, for_cross, for_mate):
    mine = own[pl.ds(2 * ROWS, layers, stride=BLOCK), :]
    lines[...] = jnp.broadcast_to(jnp.sum(mine, axis=0, keepdims=True), lines.shape)
    even = place()[0] % 2 == 0
    for layer in range(layers):
        at = BLOCK * layer

        def rows_from(first):
            return jnp.concatenate([own[at + i + first : at + i + first + HALO] for i in (0, ROWS)], axis=0)

        early, late = rows_from(0), rows_from(ROWS - HALO)
        part = slice(2 * HALO * layer, 2 * HALO * (layer + 1))
        for_mate[part] = jnp.where(even, late, early)
        for_cross[part] = jnp.where(even, early, late)


def first_kernel(layers, own, cross, mate, fresh, base, store, warm, cond):
    block = own.shape[0] // layers
    index, count = place()
    body = slice(EDGE, EDGE + layers)
    for row in range(SPAN):

        def rows_of(array):
            if HALO <= row < HALO + ROWS:
                return own[pl.ds(ROWS * array + row - HALO, layers, stride=block), :]
            at = HALO * array + row % HALO
            return sides(index, *(ref[pl.ds(at, layers, stride=2 * HALO), :] for ref in (mate, cross)))[int(row >= HALO)]

        there = 1.0
        if row < HALO:
            there = jnp.where(index > 0, 1.0, 0.0)
        elif row >= HALO + ROWS:
            there = jnp.where(index < count - 1, 1.0, 0.0)
        kind = rows_of(1)

        def table(values):
            return jnp.where(kind == 0.0, values[0], jnp.where(kind == 1.0, values[1], jnp.where(kind == 2.0, values[2], values[3])))

        base[row] = table(conduct_table) * there
        store[row] = table([0.5 * time_step / c for c in capacity_table]) * there
        warm[row, body] = rows_of(0)
        clear_edges(layers, warm.at[row], cond.at[row], fresh.at[row])

    def done(row, t, flux):
        fresh[row, body] = t + store[row] * flux

    substep_rows(range(1, SPAN - 1), layers, warm, cond, base, done)


def heat_kernel(layers, lines, w0, w1, w2, bins, fresh, base, store, potential, heated, warm, cond):
    spokes = heated.shape[-1]
    body = slice(EDGE, EDGE + layers)
    f = solve_small(lines[pl.ds(0, lines.shape[0] // COPIES, stride=COPIES), :])
    potential[...] = f[0] * w0[...] + f[1] * w1[...] + f[2] * w2[...]
    sublane = lax.broadcasted_iota(jnp.int32, (8, spokes), 0)
    weight = jnp.zeros((8, spokes), jnp.float32)
    for pair, (i, j) in enumerate(PAIRS):
        weight = jnp.where(sublane == pair, f[i] * f[j], weight)
    weight = 2.0 * weight
    heat = {}
    top = slice(layers - 8, layers)
    for row in range(1, SPAN - 1):
        inner = jnp.sum(weight * bins[row, 0:8], axis=0, keepdims=True)
        outer = jnp.sum(weight * bins[row, 8:16], axis=0, keepdims=True)
        heat[row] = jnp.where(sublane == 6, inner, jnp.where(sublane == 7, outer, 0.0))
        warm[1, row] = fresh[row]
        warm[1, row, EDGE + layers - 8 : EDGE + layers] = fresh[row, EDGE + layers - 8 : EDGE + layers] + store[row, top] * heat[row]
        clear_edges(layers, warm.at[0, row], cond.at[row])

    for substep in range(1, SUBSTEPS):

        def done(row, t, flux):
            flux = jnp.concatenate([flux[: layers - 8], flux[top] + heat[row]], axis=0)
            t = t + store[row] * flux
            if substep + 1 < SUBSTEPS:
                warm[1 - substep % 2, row, body] = t
            else:
                heated[pl.ds(row - HALO, layers, stride=ROWS), :] = t

        substep_rows(range(substep + 1, SPAN - 1 - substep), layers, warm.at[substep % 2], cond, base, done)


def local(foil_warmth, terminal_voltage_input, foil_segment_pattern, underlying_block_map, prior_block_warmth, substance_kind):
    f32 = jnp.float32
    magnets, layers = lax.axis_size("magnet"), lax.axis_size("slab")
    count = magnets * layers
    width, spokes = foil_warmth.shape[1], prior_block_warmth.shape[2]
    mates = [(i, i ^ 1) for i in range(count)]
    crossing = [(i, i + 1) for i in range(1, count - 1, 2)] + [(i + 1, i) for i in range(1, count - 1, 2)]

    def exchange(for_mate, for_cross):
        over = lax.ppermute(for_cross, BOTH, crossing)
        return lax.ppermute(for_mate, BOTH, mates), over

    def call(kernel, name, shapes, *operands, scratch=(), spaces=None, cost=None, room=8 << 20):
        return pl.pallas_call(
            kernel,
            out_shape=tuple(jax.ShapeDtypeStruct(dims, f32) for dims in shapes),
            in_specs=[pl.BlockSpec(memory_space=spaces or pltpu.VMEM)] * len(operands),
            out_specs=(pl.BlockSpec(memory_space=pltpu.VMEM),) * len(shapes),
            scratch_shapes=scratch,
            cost_estimate=cost,
            compiler_params=pltpu.CompilerParams(vmem_limit_bytes=room),
            name=name,
        )(*operands)

    rows = (ROWS, width)
    (sheet,) = call(
        sheet_kernel,
        "sheet",
        [(4 * ROWS, width)],
        foil_warmth,
        terminal_voltage_input,
        foil_segment_pattern,
        underlying_block_map,
        scratch=[pltpu.VMEM(rows, jnp.int32), pltpu.VMEM(rows, jnp.int32), pltpu.SemaphoreType.DMA((4,))],
        spaces=pltpu.HBM,
        room=66846720,
    )
    around = exchange(sheet, sheet)
    stack = (layers * BLOCK, spokes)
    (packed,) = call(
        pack_kernel, "pack", [stack], prior_block_warmth.reshape(-1, spokes), substance_kind.reshape(-1, spokes)
    )
    (packed,) = call(gram_kernel, "gram", [stack], sheet, *around[::-1], packed)

    bricks = lax.all_to_all(packed.reshape(layers, BLOCK, 1, spokes), "slab", 0, 0)
    bins, *fields = call(
        functools.partial(deposit_kernel, layers),
        "deposit",
        [(SPAN, 16, spokes), rows, rows, rows],
        sheet,
        *around,
        scratch=[pltpu.VMEM((width // 128, 8 * SPAN, 128), f32)],
        cost=pl.CostEstimate(flops=10**8, bytes_accessed=2 * 10**6, transcendentals=0),
    )
    bricks, bins = lax.optimization_barrier((bricks.reshape(stack), bins))
    lines, over, beside = call(
        functools.partial(share_kernel, layers),
        "share",
        [(magnets * COPIES, spokes)] + [(2 * HALO * layers, spokes)] * 2,
        bricks,
    )
    lines = lax.all_to_all(lines.reshape(magnets, COPIES, spokes), "magnet", 0, 0).reshape(magnets * COPIES, spokes)

    padded = (SPAN, layers + 2 * EDGE, spokes)
    plain = (SPAN, layers, spokes)
    stage = call(
        functools.partial(first_kernel, layers),
        "first",
        [padded, plain, plain],
        bricks,
        *exchange(beside, over)[::-1],
        scratch=[pltpu.VMEM(padded, f32), pltpu.VMEM(padded, f32)],
        cost=pl.CostEstimate(flops=0, bytes_accessed=0, transcendentals=0),
    )
    potential, heated = call(
        functools.partial(heat_kernel, layers),
        "heat",
        [rows, (layers * ROWS, spokes)],
        lines,
        *fields,
        bins,
        *stage,
        scratch=[pltpu.VMEM((2,) + padded, f32), pltpu.VMEM(padded, f32)],
    )
    heated = lax.all_to_all(heated.reshape(layers, ROWS, spokes), "slab", 0, 0)
    return potential, heated.reshape(prior_block_warmth.shape)


def solution(mesh):
    placed = (
        P(("magnet", "slab"), None),
        P(("magnet", "slab"), None),
        P(("magnet", "slab"), None),
        P("magnet", None),
        P("slab", "magnet", None),
        P("slab", "magnet", None),
    )
    return jax.shard_map(
        local,
        mesh=mesh,
        in_specs=placed,
        out_specs=(P(("magnet", "slab"), None), P("slab", "magnet", None)),
        check_vma=False,
    )
```

```python
import functools

import jax
import jax.numpy as jnp
from jax import lax
from jax.experimental import pallas as pl
from jax.experimental.pallas import tpu as pltpu
from jax.sharding import PartitionSpec as P

SUBSTEPS = 4
HALO = SUBSTEPS
ROWS = 8

leak_diag = 0.25
contact_gain = 4.0
copper_factor = 3.0
sheet_slope = 0.5
heat_factor = 1.5
time_step = 0.03
conduct_table = (0.3, 1.0, 2.0, 0.6)
capacity_table = (1.0, 1.5, 2.0, 1.2)
diffusivity_derivative = 0.4

SHIFT = 9.85
SCALE = 9.6
BOTH = ("magnet", "slab")
BLOCK = 2 * ROWS + 1
COPIES = 24


def place():
    size = lax.axis_size("slab")
    return lax.axis_index("magnet") * size + lax.axis_index("slab"), lax.axis_size("magnet") * size


def above(v):
    return pltpu.roll(v, 1, 0)


def below(v):
    return pltpu.roll(v, v.shape[0] - 1, 0)


def left(v):
    return pltpu.roll(v, 1, 1)


def right(v):
    return pltpu.roll(v, v.shape[1] - 1, 1)


def rows_inside(shape, margin):
    index, count = place()
    row = lax.broadcasted_iota(jnp.int32, shape, 0)
    low = jnp.where(index > 0, 0, margin)
    high = jnp.where(index < count - 1, shape[0], shape[0] - margin)
    return jnp.where((row >= low) & (row < high), 1.0, 0.0).astype(jnp.float32)


def sheet_kernel(warmth, voltage, pattern, cells, sheet, pattern_here, cells_here, sems):
    at = pl.multiple_of(lax.axis_index("slab") * ROWS, ROWS)
    copies = [
        pltpu.make_async_copy(pattern, pattern_here, sems.at[0]),
        pltpu.make_async_copy(cells.at[pl.ds(at, ROWS)], cells_here, sems.at[1]),
        pltpu.make_async_copy(warmth, sheet.at[0:ROWS], sems.at[2]),
        pltpu.make_async_copy(voltage, sheet.at[ROWS : 2 * ROWS], sems.at[3]),
    ]
    for copy in copies:
        copy.start()
    copies[0].wait()
    sheet[2 * ROWS : 3 * ROWS] = pattern_here[...].astype(jnp.float32)
    copies[1].wait()
    sheet[3 * ROWS : 4 * ROWS] = cells_here[...].astype(jnp.float32)
    copies[2].wait()
    copies[3].wait()


def pack_kernel(warmth, kind, packed):
    for slab in range(packed.shape[0] // BLOCK):
        part = slice(ROWS * slab, ROWS * (slab + 1))
        at = BLOCK * slab
        packed[at : at + ROWS] = warmth[part]
        packed[at + ROWS : at + 2 * ROWS] = kind[part].astype(jnp.float32)
        packed[at + 2 * ROWS : at + BLOCK] = jnp.zeros((1, packed.shape[1]), jnp.float32)


def sides(index, mate, cross):
    even = index % 2 == 0
    return jnp.where(even, cross, mate), jnp.where(even, mate, cross)


def window_of(own, mate, cross, i):
    part = slice(ROWS * i, ROWS * (i + 1))
    before, after = sides(place()[0], mate[part], cross[part])
    return jnp.concatenate([before, own[part], after], axis=0)


def basis(own, mate, cross):
    def window(i):
        return window_of(own, mate, cross, i)

    warmth, voltage, pattern = window(0), window(1), window(2)
    shape = warmth.shape
    inside = rows_inside(shape, ROWS)
    col = lax.broadcasted_iota(jnp.int32, shape, 1)
    last = col == shape[1] - 1
    sigma = inside * jnp.where(pattern == 1.0, copper_factor, 1.0) / (1.0 + sheet_slope * warmth)
    contact = jnp.where(pattern == 2.0, contact_gain, 0.0)
    c_down = 0.5 * (sigma + below(sigma))
    c_right = 0.5 * (sigma + jnp.where(last, 0.0, right(sigma)))
    c_left = jnp.where(col == 0, 0.5 * sigma, left(c_right))
    diagonal = leak_diag + contact + above(c_down) + c_down + c_left + c_right
    diagonal = (diagonal - SHIFT) * (1.0 / SCALE)
    o_down = c_down * inside * below(inside) * (1.0 / SCALE)
    o_up = above(o_down)
    o_right = jnp.where(last, 0.0, c_right) * (1.0 / SCALE)
    o_left = left(o_right)

    def apply(v):
        return diagonal * v - (o_up * above(v) + o_down * below(v)) - (o_left * left(v) + o_right * right(v))

    w0 = contact * voltage
    w1 = apply(w0)
    w2 = 2.0 * apply(w1) - w0
    return (w0, w1, w2), apply, inside, (c_down, c_right, c_left)


def gram_kernel(own, mate, cross, packed_in, packed):
    (w0, w1, w2), apply, _, _ = basis(own, mate, cross)
    w0, w1, w2, w3 = (w[ROWS : 2 * ROWS] for w in (w0, w1, w2, apply(w2)))
    lane = lax.broadcasted_iota(jnp.int32, (1, 128), 1)
    line = jnp.zeros((1, 128), jnp.float32)
    for i, (u, v) in enumerate(((w0, w0), (w0, w1), (w0, w2), (w1, w1), (w1, w2), (w2, w2), (w2, w3))):
        line = jnp.where(lane == i, jnp.sum(u * v, keepdims=True), line)
    for slab in range(packed.shape[0] // BLOCK):
        at = BLOCK * slab
        packed[at : at + 2 * ROWS] = packed_in[at : at + 2 * ROWS]
        packed[at + 2 * ROWS : at + BLOCK] = line


def solve_small(lines):
    total = jnp.sum(lines, axis=0, keepdims=True)
    g00, g01, g02, g11, g12, g22, k22 = (total[:, i : i + 1] for i in range(7))
    gram = ((g00, g01, g02), (g01, g11, g12), (g02, g12, g22))
    k11, k12 = 0.5 * (g12 + g01), 0.5 * (g22 + g02)
    shifted = ((g01, g11, g12), (g11, k11, k12), (g12, k12, k22))
    energy = [[SCALE * shifted[i][j] + SHIFT * gram[i][j] for j in range(3)] for i in range(3)]

    def form(m, v):
        return sum(v[i] * (v[i] * m[i][i] + 2.0 * sum((v[j] * m[i][j] for j in range(i + 1, len(v))), 0.0)) for i in range(len(v)))

    def ratio(num, den, low, high):
        return jnp.clip(num / jnp.maximum(den, 1e-37), low, high)

    alpha0 = g00 / energy[0][0]
    r = [1.0 - alpha0 * SHIFT, -alpha0 * SCALE]
    rr1 = jnp.maximum(form(gram, r), 0.0)
    beta = ratio(rr1, g00, 0.0, 1e4)
    p = [r[0] + beta, r[1]]
    alpha1 = ratio(rr1, form(energy, p), 0.05, 4.1)
    half = 0.5 * SCALE * p[1]
    image = [half + SHIFT * p[0], SCALE * p[0] + SHIFT * p[1], half]
    x = [alpha0 + alpha1 * p[0], alpha1 * p[1]]
    r = [r[0] - alpha1 * image[0], r[1] - alpha1 * image[1], -alpha1 * image[2]]
    rr2 = jnp.maximum(form(gram, r), 0.0)
    beta = ratio(rr2, rr1, 0.0, 1e4)
    p = [r[0] + beta * p[0], r[1] + beta * p[1], r[2]]
    alpha2 = ratio(rr2, form(energy, p), 0.05, 4.1)
    return x[0] + alpha2 * p[0], x[1] + alpha2 * p[1], alpha2 * p[2]


PAIRS = ((0, 0), (0, 1), (0, 2), (1, 1), (1, 2), (2, 2))
SPAN = ROWS + 2 * HALO
EDGE = 8


def deposit_kernel(layers, own, mate, cross, bins, w0_out, w1_out, w2_out, heats):
    spokes = bins.shape[-1]
    fields, _, inside, (c_down, c_right, c_left) = basis(own, mate, cross)
    for out, w in zip((w0_out, w1_out, w2_out), fields):
        out[...] = w[ROWS : 2 * ROWS]
    shape = inside.shape
    col = lax.broadcasted_iota(jnp.int32, shape, 1)
    last, first = col == shape[1] - 1, col == 0
    fields = [w * inside for w in fields]
    falls = [w - below(w) for w in fields]
    steps = [w - jnp.where(last, 0.0, right(w)) for w in fields]
    wanted = slice(ROWS - HALO, ROWS - HALO + SPAN)
    for pair, (i, j) in enumerate(PAIRS):
        q_down = c_down * (falls[i] * falls[j])
        q_right = c_right * (steps[i] * steps[j])
        q_left = jnp.where(first, c_left * (fields[i] * fields[j]), left(q_right))
        joule = (q_down + above(q_down)) + (q_right + q_left)
        factor = heat_factor if i == j else 2.0 * heat_factor
        joule = factor * joule[wanted]
        for part in range(heats.shape[0]):
            heats[part, SPAN * pair : SPAN * (pair + 1)] = joule[:, 128 * part : 128 * (part + 1)]
    for part in range(heats.shape[0]):
        heats[part, SPAN * len(PAIRS) :] = jnp.zeros((SPAN * (8 - len(PAIRS)), 128), jnp.float32)
    cell = window_of(own, mate, cross, 3)[wanted].astype(jnp.int32)
    azimuth = cell & (spokes - 1)
    outermost = jnp.where(cell >= (layers - 1) * spokes, 1.0, 0.0)
    spoke = lax.broadcasted_iota(jnp.int32, (spokes, shape[1]), 0)
    for row in range(1, SPAN - 1):
        pick = jnp.where(azimuth[row : row + 1] == spoke, 1.0, 0.0).astype(jnp.bfloat16)
        joule = jnp.concatenate([heats[part, pl.ds(row, 8, stride=SPAN), :] for part in range(heats.shape[0])], axis=1)
        upper = joule * outermost[row : row + 1]
        pieces = []
        for part in (joule - upper, upper):
            for _ in range(3):
                piece = part.astype(jnp.bfloat16)
                part = part - piece.astype(jnp.float32)
                pieces.append(piece)
        total = lax.dot_general(
            jnp.concatenate(pieces, axis=0), pick, (((1,), (1,)), ((), ())), preferred_element_type=jnp.float32
        )
        bins[row, 0:8] = total[0:8] + (total[8:16] + total[16:24])
        bins[row, 8:16] = total[24:32] + (total[32:40] + total[40:48])


def substep_rows(rows, layers, warm, cond, base, done):
    body = slice(EDGE, EDGE + layers)
    inward, outward = slice(EDGE - 1, EDGE - 1 + layers), slice(EDGE + 1, EDGE + 1 + layers)

    def conductivity(row):
        t = warm[row, body]
        k = base[row] * (1.0 + diffusivity_derivative * t)
        cond[row, body] = k
        return t, k

    def between(t, k, t_other, k_other):
        return (k + k_other) * (t_other - t)

    below_row = conductivity(rows[0] - 1)
    here = conductivity(rows[0])
    inner = between(*below_row, *here)
    for row in rows:
        t, k = here
        here = conductivity(row + 1)
        outer = between(t, k, *here)
        flux = outer - inner
        inner = outer
        flux = flux + between(t, k, warm[row, inward], cond[row, inward])
        flux = flux + between(t, k, warm[row, outward], cond[row, outward])
        face = between(t, k, right(t), right(k))
        done(row, t, flux + (face - left(face)))


def clear_edges(layers, *fields):
    for field in fields:
        blank = jnp.zeros((EDGE, field.shape[-1]), jnp.float32)
        field[0:EDGE] = blank
        field[EDGE + layers : 2 * EDGE + layers] = blank


def share_kernel(layers, own, lines, for_cross, for_mate):
    mine = own[pl.ds(2 * ROWS, layers, stride=BLOCK), :]
    lines[...] = jnp.broadcast_to(jnp.sum(mine, axis=0, keepdims=True), lines.shape)
    even = place()[0] % 2 == 0
    for layer in range(layers):
        at = BLOCK * layer

        def rows_from(first):
            return jnp.concatenate([own[at + i + first : at + i + first + HALO] for i in (0, ROWS)], axis=0)

        early, late = rows_from(0), rows_from(ROWS - HALO)
        part = slice(2 * HALO * layer, 2 * HALO * (layer + 1))
        for_mate[part] = jnp.where(even, late, early)
        for_cross[part] = jnp.where(even, early, late)


def first_kernel(layers, own, edge, cross, mate, fresh, base, store, warm, cond):
    block = own.shape[0] // layers
    index, count = place()
    body = slice(EDGE, EDGE + layers)
    for row in range(SPAN):

        def rows_of(array):
            if HALO <= row < HALO + ROWS:
                return own[pl.ds(ROWS * array + row - HALO, layers, stride=block), :]
            at = HALO * array + row % HALO
            near = sides(index, *(ref[pl.ds(at, layers, stride=2 * HALO), :] for ref in (mate, cross)))[int(row >= HALO)]
            at = ROWS * array + (row + ROWS - HALO if row < HALO else row - HALO - ROWS)
            last = lax.axis_index("slab") == (0 if row < HALO else layers - 1)
            return jnp.where(last, edge[pl.ds(at, layers, stride=block), :], near)

        there = 1.0
        if row < HALO:
            there = jnp.where(index > 0, 1.0, 0.0)
        elif row >= HALO + ROWS:
            there = jnp.where(index < count - 1, 1.0, 0.0)
        kind = rows_of(1)

        def table(values):
            return jnp.where(kind == 0.0, values[0], jnp.where(kind == 1.0, values[1], jnp.where(kind == 2.0, values[2], values[3])))

        base[row] = table(conduct_table) * there
        store[row] = table([0.5 * time_step / c for c in capacity_table]) * there
        warm[row, body] = rows_of(0)
        clear_edges(layers, warm.at[row], cond.at[row], fresh.at[row])

    def done(row, t, flux):
        fresh[row, body] = t + store[row] * flux

    substep_rows(range(1, SPAN - 1), layers, warm, cond, base, done)


def heat_kernel(layers, lines, w0, w1, w2, bins, fresh, base, store, potential, heated, warm, cond):
    spokes = heated.shape[-1]
    body = slice(EDGE, EDGE + layers)
    f = solve_small(lines[pl.ds(0, lines.shape[0] // COPIES, stride=COPIES), :])
    potential[...] = f[0] * w0[...] + f[1] * w1[...] + f[2] * w2[...]
    sublane = lax.broadcasted_iota(jnp.int32, (8, spokes), 0)
    weight = jnp.zeros((8, spokes), jnp.float32)
    for pair, (i, j) in enumerate(PAIRS):
        weight = jnp.where(sublane == pair, f[i] * f[j], weight)
    weight = 2.0 * weight
    heat = {}
    top = slice(layers - 8, layers)
    for row in range(1, SPAN - 1):
        inner = jnp.sum(weight * bins[row, 0:8], axis=0, keepdims=True)
        outer = jnp.sum(weight * bins[row, 8:16], axis=0, keepdims=True)
        heat[row] = jnp.where(sublane == 6, inner, jnp.where(sublane == 7, outer, 0.0))
        warm[1, row] = fresh[row]
        warm[1, row, EDGE + layers - 8 : EDGE + layers] = fresh[row, EDGE + layers - 8 : EDGE + layers] + store[row, top] * heat[row]
        clear_edges(layers, warm.at[0, row], cond.at[row])

    for substep in range(1, SUBSTEPS):

        def done(row, t, flux):
            flux = jnp.concatenate([flux[: layers - 8], flux[top] + heat[row]], axis=0)
            t = t + store[row] * flux
            if substep + 1 < SUBSTEPS:
                warm[1 - substep % 2, row, body] = t
            else:
                heated[pl.ds(row - HALO, layers, stride=ROWS), :] = t

        substep_rows(range(substep + 1, SPAN - 1 - substep), layers, warm.at[substep % 2], cond, base, done)


def local(foil_warmth, terminal_voltage_input, foil_segment_pattern, underlying_block_map, prior_block_warmth, substance_kind):
    f32 = jnp.float32
    magnets, layers = lax.axis_size("magnet"), lax.axis_size("slab")
    count = magnets * layers
    width, spokes = foil_warmth.shape[1], prior_block_warmth.shape[2]
    mates = [(i, i + 1) for i in range(0, count, 2)]
    crossing = [(i, i + 1) for i in range(1, count - 1, 2)]
    ends = [pair for pair in crossing if pair[1] % layers == 0]
    inner = [pair for pair in crossing if pair[1] % layers]

    def swap(array, pairs):
        return lax.ppermute(array, BOTH, pairs + [(j, i) for i, j in pairs])

    def call(kernel, name, shapes, *operands, scratch=(), spaces=None, cost=None, room=8 << 20):
        return pl.pallas_call(
            kernel,
            out_shape=tuple(jax.ShapeDtypeStruct(dims, f32) for dims in shapes),
            in_specs=[pl.BlockSpec(memory_space=spaces or pltpu.VMEM)] * len(operands),
            out_specs=(pl.BlockSpec(memory_space=pltpu.VMEM),) * len(shapes),
            scratch_shapes=scratch,
            cost_estimate=cost,
            compiler_params=pltpu.CompilerParams(vmem_limit_bytes=room),
            name=name,
        )(*operands)

    rows = (ROWS, width)
    (sheet,) = call(
        sheet_kernel,
        "sheet",
        [(4 * ROWS, width)],
        foil_warmth,
        terminal_voltage_input,
        foil_segment_pattern,
        underlying_block_map,
        scratch=[pltpu.VMEM(rows, jnp.int32), pltpu.VMEM(rows, jnp.int32), pltpu.SemaphoreType.DMA((4,))],
        spaces=pltpu.HBM,
        room=66846720,
    )
    across = swap(sheet, crossing)
    around = (swap(sheet, mates), across)
    stack = (layers * BLOCK, spokes)
    (packed,) = call(
        pack_kernel, "pack", [stack], prior_block_warmth.reshape(-1, spokes), substance_kind.reshape(-1, spokes)
    )
    (packed,) = call(gram_kernel, "gram", [stack], sheet, *around, packed)

    bricks = lax.all_to_all(packed.reshape(layers, BLOCK, 1, spokes), "slab", 0, 0)
    bins, *fields = call(
        functools.partial(deposit_kernel, layers),
        "deposit",
        [(SPAN, 16, spokes), rows, rows, rows],
        sheet,
        *around,
        scratch=[pltpu.VMEM((width // 128, 8 * SPAN, 128), f32)],
        cost=pl.CostEstimate(flops=10**8, bytes_accessed=2 * 10**6, transcendentals=0),
    )
    bricks, bins = lax.optimization_barrier((bricks.reshape(stack), bins))
    lines, over, beside = call(
        functools.partial(share_kernel, layers),
        "share",
        [(magnets * COPIES, spokes)] + [(2 * HALO * layers, spokes)] * 2,
        bricks,
    )
    lines = lax.all_to_all(lines.reshape(magnets, COPIES, spokes), "magnet", 0, 0).reshape(magnets * COPIES, spokes)

    padded = (SPAN, layers + 2 * EDGE, spokes)
    plain = (SPAN, layers, spokes)
    stage = call(
        functools.partial(first_kernel, layers),
        "first",
        [padded, plain, plain],
        bricks,
        swap(bricks, ends),
        swap(over, inner),
        swap(beside, mates),
        scratch=[pltpu.VMEM(padded, f32), pltpu.VMEM(padded, f32)],
        cost=pl.CostEstimate(flops=0, bytes_accessed=0, transcendentals=0),
    )
    potential, heated = call(
        functools.partial(heat_kernel, layers),
        "heat",
        [rows, (layers * ROWS, spokes)],
        lines,
        *fields,
        bins,
        *stage,
        scratch=[pltpu.VMEM((2,) + padded, f32), pltpu.VMEM(padded, f32)],
    )
    heated = lax.all_to_all(heated.reshape(layers, ROWS, spokes), "slab", 0, 0)
    return potential, heated.reshape(prior_block_warmth.shape)


def solution(mesh):
    placed = (
        P(("magnet", "slab"), None),
        P(("magnet", "slab"), None),
        P(("magnet", "slab"), None),
        P("magnet", None),
        P("slab", "magnet", None),
        P("slab", "magnet", None),
    )
    return jax.shard_map(
        local,
        mesh=mesh,
        in_specs=placed,
        out_specs=(P(("magnet", "slab"), None), P("slab", "magnet", None)),
        check_vma=False,
    )
```

```python
import functools

import jax
import jax.numpy as jnp
from jax import lax
from jax.experimental import pallas as pl
from jax.experimental.pallas import tpu as pltpu
from jax.sharding import PartitionSpec as P

SUBSTEPS = 4
HALO = SUBSTEPS
ROWS = 8

leak_diag = 0.25
contact_gain = 4.0
copper_factor = 3.0
sheet_slope = 0.5
heat_factor = 1.5
time_step = 0.03
conduct_table = (0.3, 1.0, 2.0, 0.6)
capacity_table = (1.0, 1.5, 2.0, 1.2)
diffusivity_derivative = 0.4

SHIFT = 9.85
SCALE = 9.6
BOTH = ("magnet", "slab")
BLOCK = 2 * ROWS + 1
COPIES = 24


def place():
    size = lax.axis_size("slab")
    return lax.axis_index("magnet") * size + lax.axis_index("slab"), lax.axis_size("magnet") * size


def above(v):
    return pltpu.roll(v, 1, 0)


def below(v):
    return pltpu.roll(v, v.shape[0] - 1, 0)


def left(v):
    return pltpu.roll(v, 1, 1)


def right(v):
    return pltpu.roll(v, v.shape[1] - 1, 1)


def rows_inside(shape, margin):
    index, count = place()
    row = lax.broadcasted_iota(jnp.int32, shape, 0)
    low = jnp.where(index > 0, 0, margin)
    high = jnp.where(index < count - 1, shape[0], shape[0] - margin)
    return jnp.where((row >= low) & (row < high), 1.0, 0.0).astype(jnp.float32)


def sheet_kernel(warmth, voltage, pattern, cells, sheet, pattern_here, cells_here, sems):
    at = pl.multiple_of(lax.axis_index("slab") * ROWS, ROWS)
    copies = [
        pltpu.make_async_copy(pattern, pattern_here, sems.at[0]),
        pltpu.make_async_copy(cells.at[pl.ds(at, ROWS)], cells_here, sems.at[1]),
        pltpu.make_async_copy(warmth, sheet.at[0:ROWS], sems.at[2]),
        pltpu.make_async_copy(voltage, sheet.at[ROWS : 2 * ROWS], sems.at[3]),
    ]
    for copy in copies:
        copy.start()
    copies[0].wait()
    sheet[2 * ROWS : 3 * ROWS] = pattern_here[...].astype(jnp.float32)
    copies[1].wait()
    sheet[3 * ROWS : 4 * ROWS] = cells_here[...].astype(jnp.float32)
    copies[2].wait()
    copies[3].wait()


def pack_kernel(warmth, kind, packed):
    for slab in range(packed.shape[0] // BLOCK):
        part = slice(ROWS * slab, ROWS * (slab + 1))
        at = BLOCK * slab
        packed[at : at + ROWS] = warmth[part]
        packed[at + ROWS : at + 2 * ROWS] = kind[part].astype(jnp.float32)
        packed[at + 2 * ROWS : at + BLOCK] = jnp.zeros((1, packed.shape[1]), jnp.float32)


def sides(index, mate, cross):
    even = index % 2 == 0
    return jnp.where(even, cross, mate), jnp.where(even, mate, cross)


def window_of(own, mate, cross, i):
    part = slice(ROWS * i, ROWS * (i + 1))
    before, after = sides(place()[0], mate[part], cross[part])
    return jnp.concatenate([before, own[part], after], axis=0)


def basis(own, mate, cross):
    def window(i):
        return window_of(own, mate, cross, i)

    warmth, voltage, pattern = window(0), window(1), window(2)
    shape = warmth.shape
    inside = rows_inside(shape, ROWS)
    col = lax.broadcasted_iota(jnp.int32, shape, 1)
    last = col == shape[1] - 1
    sigma = inside * jnp.where(pattern == 1.0, copper_factor, 1.0) / (1.0 + sheet_slope * warmth)
    contact = jnp.where(pattern == 2.0, contact_gain, 0.0)
    c_down = 0.5 * (sigma + below(sigma))
    c_right = 0.5 * (sigma + jnp.where(last, 0.0, right(sigma)))
    c_left = jnp.where(col == 0, 0.5 * sigma, left(c_right))
    diagonal = leak_diag + contact + above(c_down) + c_down + c_left + c_right
    diagonal = (diagonal - SHIFT) * (1.0 / SCALE)
    o_down = c_down * inside * below(inside) * (1.0 / SCALE)
    o_up = above(o_down)
    o_right = jnp.where(last, 0.0, c_right) * (1.0 / SCALE)
    o_left = left(o_right)

    def apply(v):
        return diagonal * v - (o_up * above(v) + o_down * below(v)) - (o_left * left(v) + o_right * right(v))

    w0 = contact * voltage
    w1 = apply(w0)
    w2 = 2.0 * apply(w1) - w0
    return (w0, w1, w2), apply, inside, (c_down, c_right, c_left)


def gram_kernel(own, mate, cross, packed_in, packed):
    (w0, w1, w2), apply, _, _ = basis(own, mate, cross)
    w0, w1, w2, w3 = (w[ROWS : 2 * ROWS] for w in (w0, w1, w2, apply(w2)))
    lane = lax.broadcasted_iota(jnp.int32, (1, 128), 1)
    line = jnp.zeros((1, 128), jnp.float32)
    for i, (u, v) in enumerate(((w0, w0), (w0, w1), (w0, w2), (w1, w1), (w1, w2), (w2, w2), (w2, w3))):
        line = jnp.where(lane == i, jnp.sum(u * v, keepdims=True), line)
    for slab in range(packed.shape[0] // BLOCK):
        at = BLOCK * slab
        packed[at : at + 2 * ROWS] = packed_in[at : at + 2 * ROWS]
        packed[at + 2 * ROWS : at + BLOCK] = line


def solve_small(lines):
    total = jnp.sum(lines, axis=0, keepdims=True)
    g00, g01, g02, g11, g12, g22, k22 = (total[:, i : i + 1] for i in range(7))
    gram = ((g00, g01, g02), (g01, g11, g12), (g02, g12, g22))
    k11, k12 = 0.5 * (g12 + g01), 0.5 * (g22 + g02)
    shifted = ((g01, g11, g12), (g11, k11, k12), (g12, k12, k22))
    energy = [[SCALE * shifted[i][j] + SHIFT * gram[i][j] for j in range(3)] for i in range(3)]

    def form(m, v):
        return sum(v[i] * (v[i] * m[i][i] + 2.0 * sum((v[j] * m[i][j] for j in range(i + 1, len(v))), 0.0)) for i in range(len(v)))

    def ratio(num, den, low, high):
        return jnp.clip(num / jnp.maximum(den, 1e-37), low, high)

    alpha0 = g00 / energy[0][0]
    r = [1.0 - alpha0 * SHIFT, -alpha0 * SCALE]
    rr1 = jnp.maximum(form(gram, r), 0.0)
    beta = ratio(rr1, g00, 0.0, 1e4)
    p = [r[0] + beta, r[1]]
    alpha1 = ratio(rr1, form(energy, p), 0.05, 4.1)
    half = 0.5 * SCALE * p[1]
    image = [half + SHIFT * p[0], SCALE * p[0] + SHIFT * p[1], half]
    x = [alpha0 + alpha1 * p[0], alpha1 * p[1]]
    r = [r[0] - alpha1 * image[0], r[1] - alpha1 * image[1], -alpha1 * image[2]]
    rr2 = jnp.maximum(form(gram, r), 0.0)
    beta = ratio(rr2, rr1, 0.0, 1e4)
    p = [r[0] + beta * p[0], r[1] + beta * p[1], r[2]]
    alpha2 = ratio(rr2, form(energy, p), 0.05, 4.1)
    return x[0] + alpha2 * p[0], x[1] + alpha2 * p[1], alpha2 * p[2]


PAIRS = ((0, 0), (0, 1), (0, 2), (1, 1), (1, 2), (2, 2))
SPAN = ROWS + 2 * HALO
EDGE = 8


def deposit_kernel(layers, own, mate, cross, bins, w0_out, w1_out, w2_out, heats):
    spokes = bins.shape[-1]
    fields, _, inside, (c_down, c_right, c_left) = basis(own, mate, cross)
    for out, w in zip((w0_out, w1_out, w2_out), fields):
        out[...] = w[ROWS : 2 * ROWS]
    shape = inside.shape
    col = lax.broadcasted_iota(jnp.int32, shape, 1)
    last, first = col == shape[1] - 1, col == 0
    fields = [w * inside for w in fields]
    falls = [w - below(w) for w in fields]
    steps = [w - jnp.where(last, 0.0, right(w)) for w in fields]
    wanted = slice(ROWS - HALO, ROWS - HALO + SPAN)
    for pair, (i, j) in enumerate(PAIRS):
        q_down = c_down * (falls[i] * falls[j])
        q_right = c_right * (steps[i] * steps[j])
        q_left = jnp.where(first, c_left * (fields[i] * fields[j]), left(q_right))
        joule = (q_down + above(q_down)) + (q_right + q_left)
        factor = heat_factor if i == j else 2.0 * heat_factor
        joule = factor * joule[wanted]
        for part in range(heats.shape[0]):
            heats[part, SPAN * pair : SPAN * (pair + 1)] = joule[:, 128 * part : 128 * (part + 1)]
    for part in range(heats.shape[0]):
        heats[part, SPAN * len(PAIRS) :] = jnp.zeros((SPAN * (8 - len(PAIRS)), 128), jnp.float32)
    cell = window_of(own, mate, cross, 3)[wanted].astype(jnp.int32)
    azimuth = cell & (spokes - 1)
    outermost = jnp.where(cell >= (layers - 1) * spokes, 1.0, 0.0)
    spoke = lax.broadcasted_iota(jnp.int32, (spokes, shape[1]), 0)
    for row in range(1, SPAN - 1):
        pick = jnp.where(azimuth[row : row + 1] == spoke, 1.0, 0.0).astype(jnp.bfloat16)
        joule = jnp.concatenate([heats[part, pl.ds(row, 8, stride=SPAN), :] for part in range(heats.shape[0])], axis=1)
        upper = joule * outermost[row : row + 1]
        pieces = []
        for part in (joule - upper, upper):
            for _ in range(3):
                piece = part.astype(jnp.bfloat16)
                part = part - piece.astype(jnp.float32)
                pieces.append(piece)
        total = lax.dot_general(
            jnp.concatenate(pieces, axis=0), pick, (((1,), (1,)), ((), ())), preferred_element_type=jnp.float32
        )
        bins[row, 0:8] = total[0:8] + (total[8:16] + total[16:24])
        bins[row, 8:16] = total[24:32] + (total[32:40] + total[40:48])


def substep_rows(rows, layers, warm, cond, base, done):
    body = slice(EDGE, EDGE + layers)
    inward, outward = slice(EDGE - 1, EDGE - 1 + layers), slice(EDGE + 1, EDGE + 1 + layers)

    def conductivity(row):
        t = warm[row, body]
        k = base[row] * (1.0 + diffusivity_derivative * t)
        cond[row, body] = k
        return t, k

    def between(t, k, t_other, k_other):
        return (k + k_other) * (t_other - t)

    below_row = conductivity(rows[0] - 1)
    here = conductivity(rows[0])
    inner = between(*below_row, *here)
    for row in rows:
        t, k = here
        here = conductivity(row + 1)
        outer = between(t, k, *here)
        flux = outer - inner
        inner = outer
        flux = flux + between(t, k, warm[row, inward], cond[row, inward])
        flux = flux + between(t, k, warm[row, outward], cond[row, outward])
        face = between(t, k, right(t), right(k))
        done(row, t, flux + (face - left(face)))


def clear_edges(layers, *fields):
    for field in fields:
        blank = jnp.zeros((EDGE, field.shape[-1]), jnp.float32)
        field[0:EDGE] = blank
        field[EDGE + layers : 2 * EDGE + layers] = blank


def share_kernel(layers, own, lines, for_cross, for_mate):
    mine = own[pl.ds(2 * ROWS, layers, stride=BLOCK), :]
    lines[...] = jnp.broadcast_to(jnp.sum(mine, axis=0, keepdims=True), lines.shape)
    even = place()[0] % 2 == 0
    for layer in range(layers):
        at = BLOCK * layer

        def rows_from(first):
            return jnp.concatenate([own[at + i + first : at + i + first + HALO] for i in (0, ROWS)], axis=0)

        early, late = rows_from(0), rows_from(ROWS - HALO)
        part = slice(2 * HALO * layer, 2 * HALO * (layer + 1))
        for_mate[part] = jnp.where(even, late, early)
        for_cross[part] = jnp.where(even, early, late)


def first_kernel(layers, own, edge, cross, mate, fresh, base, store, warm, cond):
    block = own.shape[0] // layers
    index, count = place()
    body = slice(EDGE, EDGE + layers)
    for row in range(SPAN):

        def rows_of(array):
            if HALO <= row < HALO + ROWS:
                return own[pl.ds(ROWS * array + row - HALO, layers, stride=block), :]
            at = HALO * array + row % HALO
            near = sides(index, *(ref[pl.ds(at, layers, stride=2 * HALO), :] for ref in (mate, cross)))[int(row >= HALO)]
            at = ROWS * array + (row + ROWS - HALO if row < HALO else row - HALO - ROWS)
            last = lax.axis_index("slab") == (0 if row < HALO else layers - 1)
            return jnp.where(last, edge[pl.ds(at, layers, stride=block), :], near)

        there = 1.0
        if row < HALO:
            there = jnp.where(index > 0, 1.0, 0.0)
        elif row >= HALO + ROWS:
            there = jnp.where(index < count - 1, 1.0, 0.0)
        kind = rows_of(1)

        def table(values):
            return jnp.where(kind == 0.0, values[0], jnp.where(kind == 1.0, values[1], jnp.where(kind == 2.0, values[2], values[3])))

        base[row] = table(conduct_table) * there
        store[row] = table([0.5 * time_step / c for c in capacity_table]) * there
        warm[row, body] = rows_of(0)
        clear_edges(layers, warm.at[row], cond.at[row], fresh.at[row])

    def done(row, t, flux):
        fresh[row, body] = t + store[row] * flux

    substep_rows(range(1, SPAN - 1), layers, warm, cond, base, done)


def heat_kernel(layers, lines, w0, w1, w2, bins, fresh, base, store, potential_out, heated, warm, cond, potential, sem):
    spokes = heated.shape[-1]
    body = slice(EDGE, EDGE + layers)
    f = solve_small(lines[pl.ds(0, lines.shape[0] // COPIES, stride=COPIES), :])
    potential[...] = f[0] * w0[...] + f[1] * w1[...] + f[2] * w2[...]
    leaving = pltpu.make_async_copy(potential, potential_out, sem)
    leaving.start()
    sublane = lax.broadcasted_iota(jnp.int32, (8, spokes), 0)
    weight = jnp.zeros((8, spokes), jnp.float32)
    for pair, (i, j) in enumerate(PAIRS):
        weight = jnp.where(sublane == pair, f[i] * f[j], weight)
    weight = 2.0 * weight
    heat = {}
    top = slice(layers - 8, layers)
    for row in range(1, SPAN - 1):
        inner = jnp.sum(weight * bins[row, 0:8], axis=0, keepdims=True)
        outer = jnp.sum(weight * bins[row, 8:16], axis=0, keepdims=True)
        heat[row] = jnp.where(sublane == 6, inner, jnp.where(sublane == 7, outer, 0.0))
        warm[1, row] = fresh[row]
        warm[1, row, EDGE + layers - 8 : EDGE + layers] = fresh[row, EDGE + layers - 8 : EDGE + layers] + store[row, top] * heat[row]
        clear_edges(layers, warm.at[0, row], cond.at[row])

    for substep in range(1, SUBSTEPS):

        def done(row, t, flux):
            flux = jnp.concatenate([flux[: layers - 8], flux[top] + heat[row]], axis=0)
            t = t + store[row] * flux
            if substep + 1 < SUBSTEPS:
                warm[1 - substep % 2, row, body] = t
            else:
                heated[pl.ds(row - HALO, layers, stride=ROWS), :] = t

        substep_rows(range(substep + 1, SPAN - 1 - substep), layers, warm.at[substep % 2], cond, base, done)
    leaving.wait()


def local(foil_warmth, terminal_voltage_input, foil_segment_pattern, underlying_block_map, prior_block_warmth, substance_kind):
    f32 = jnp.float32
    magnets, layers = lax.axis_size("magnet"), lax.axis_size("slab")
    count = magnets * layers
    width, spokes = foil_warmth.shape[1], prior_block_warmth.shape[2]
    mates = [(i, i + 1) for i in range(0, count, 2)]
    crossing = [(i, i + 1) for i in range(1, count - 1, 2)]
    ends = [pair for pair in crossing if pair[1] % layers == 0]
    inner = [pair for pair in crossing if pair[1] % layers]

    def swap(array, pairs):
        return lax.ppermute(array, BOTH, pairs + [(j, i) for i, j in pairs])

    def call(kernel, name, shapes, *operands, scratch=(), spaces=None, outs=None, cost=None, room=8 << 20):
        return pl.pallas_call(
            kernel,
            out_shape=tuple(jax.ShapeDtypeStruct(dims, f32) for dims in shapes),
            in_specs=[pl.BlockSpec(memory_space=spaces or pltpu.VMEM)] * len(operands),
            out_specs=tuple(pl.BlockSpec(memory_space=space) for space in outs or (pltpu.VMEM,) * len(shapes)),
            scratch_shapes=scratch,
            cost_estimate=cost,
            compiler_params=pltpu.CompilerParams(vmem_limit_bytes=room),
            name=name,
        )(*operands)

    rows = (ROWS, width)
    (sheet,) = call(
        sheet_kernel,
        "sheet",
        [(4 * ROWS, width)],
        foil_warmth,
        terminal_voltage_input,
        foil_segment_pattern,
        underlying_block_map,
        scratch=[pltpu.VMEM(rows, jnp.int32), pltpu.VMEM(rows, jnp.int32), pltpu.SemaphoreType.DMA((4,))],
        spaces=pltpu.HBM,
        room=66846720,
    )
    across = swap(sheet, crossing)
    around = (swap(sheet, mates), across)
    stack = (layers * BLOCK, spokes)
    (packed,) = call(
        pack_kernel, "pack", [stack], prior_block_warmth.reshape(-1, spokes), substance_kind.reshape(-1, spokes)
    )
    (packed,) = call(gram_kernel, "gram", [stack], sheet, *around, packed)

    bricks = lax.all_to_all(packed.reshape(layers, BLOCK, 1, spokes), "slab", 0, 0)
    bins, *fields = call(
        functools.partial(deposit_kernel, layers),
        "deposit",
        [(SPAN, 16, spokes), rows, rows, rows],
        sheet,
        *around,
        scratch=[pltpu.VMEM((width // 128, 8 * SPAN, 128), f32)],
        cost=pl.CostEstimate(flops=10**8, bytes_accessed=2 * 10**6, transcendentals=0),
    )
    bricks, bins = lax.optimization_barrier((bricks.reshape(stack), bins))
    lines, over, beside = call(
        functools.partial(share_kernel, layers),
        "share",
        [(magnets * COPIES, spokes)] + [(2 * HALO * layers, spokes)] * 2,
        bricks,
    )
    lines = lax.all_to_all(lines.reshape(magnets, COPIES, spokes), "magnet", 0, 0).reshape(magnets * COPIES, spokes)

    padded = (SPAN, layers + 2 * EDGE, spokes)
    plain = (SPAN, layers, spokes)
    stage = call(
        functools.partial(first_kernel, layers),
        "first",
        [padded, plain, plain],
        bricks,
        swap(bricks, ends),
        swap(over, inner),
        swap(beside, mates),
        scratch=[pltpu.VMEM(padded, f32), pltpu.VMEM(padded, f32)],
        cost=pl.CostEstimate(flops=0, bytes_accessed=0, transcendentals=0),
    )
    potential, heated = call(
        functools.partial(heat_kernel, layers),
        "heat",
        [rows, (layers * ROWS, spokes)],
        lines,
        *fields,
        bins,
        *stage,
        outs=(pltpu.HBM, pltpu.VMEM),
        scratch=[
            pltpu.VMEM((2,) + padded, f32),
            pltpu.VMEM(padded, f32),
            pltpu.VMEM(rows, f32),
            pltpu.SemaphoreType.DMA(()),
        ],
    )
    heated = lax.all_to_all(heated.reshape(layers, ROWS, spokes), "slab", 0, 0)
    return potential, heated.reshape(prior_block_warmth.shape)


def solution(mesh):
    placed = (
        P(("magnet", "slab"), None),
        P(("magnet", "slab"), None),
        P(("magnet", "slab"), None),
        P("magnet", None),
        P("slab", "magnet", None),
        P("slab", "magnet", None),
    )
    return jax.shard_map(
        local,
        mesh=mesh,
        in_specs=placed,
        out_specs=(P(("magnet", "slab"), None), P("slab", "magnet", None)),
        check_vma=False,
    )
```

```python
import functools

import jax
import jax.numpy as jnp
from jax import lax
from jax.experimental import pallas as pl
from jax.experimental.pallas import tpu as pltpu
from jax.sharding import PartitionSpec as P

SUBSTEPS = 4
HALO = SUBSTEPS
ROWS = 8

leak_diag = 0.25
contact_gain = 4.0
copper_factor = 3.0
sheet_slope = 0.5
heat_factor = 1.5
time_step = 0.03
conduct_table = (0.3, 1.0, 2.0, 0.6)
capacity_table = (1.0, 1.5, 2.0, 1.2)
diffusivity_derivative = 0.4

SHIFT = 9.85
SCALE = 9.6
BOTH = ("magnet", "slab")
BLOCK = 2 * ROWS + 1
COPIES = 24


def place():
    size = lax.axis_size("slab")
    return lax.axis_index("magnet") * size + lax.axis_index("slab"), lax.axis_size("magnet") * size


def above(v):
    return pltpu.roll(v, 1, 0)


def below(v):
    return pltpu.roll(v, v.shape[0] - 1, 0)


def left(v):
    return pltpu.roll(v, 1, 1)


def right(v):
    return pltpu.roll(v, v.shape[1] - 1, 1)


def rows_inside(shape, margin):
    index, count = place()
    row = lax.broadcasted_iota(jnp.int32, shape, 0)
    low = jnp.where(index > 0, 0, margin)
    high = jnp.where(index < count - 1, shape[0], shape[0] - margin)
    return jnp.where((row >= low) & (row < high), 1.0, 0.0).astype(jnp.float32)


def sheet_kernel(warmth, voltage, pattern, cells, sheet, pattern_here, cells_here, sems):
    at = pl.multiple_of(lax.axis_index("slab") * ROWS, ROWS)
    copies = [
        pltpu.make_async_copy(pattern, pattern_here, sems.at[0]),
        pltpu.make_async_copy(cells.at[pl.ds(at, ROWS)], cells_here, sems.at[1]),
        pltpu.make_async_copy(warmth, sheet.at[0:ROWS], sems.at[2]),
        pltpu.make_async_copy(voltage, sheet.at[ROWS : 2 * ROWS], sems.at[3]),
    ]
    for copy in copies:
        copy.start()
    copies[0].wait()
    sheet[2 * ROWS : 3 * ROWS] = pattern_here[...].astype(jnp.float32)
    copies[1].wait()
    sheet[3 * ROWS : 4 * ROWS] = cells_here[...].astype(jnp.float32)
    copies[2].wait()
    copies[3].wait()


def pack_kernel(warmth, kind, packed):
    for slab in range(packed.shape[0] // BLOCK):
        part = slice(ROWS * slab, ROWS * (slab + 1))
        at = BLOCK * slab
        packed[at : at + ROWS] = warmth[part]
        packed[at + ROWS : at + 2 * ROWS] = kind[part].astype(jnp.float32)
        packed[at + 2 * ROWS : at + BLOCK] = jnp.zeros((1, packed.shape[1]), jnp.float32)


def sides(index, mate, cross):
    even = index % 2 == 0
    return jnp.where(even, cross, mate), jnp.where(even, mate, cross)


def window_of(own, mate, cross, i):
    part = slice(ROWS * i, ROWS * (i + 1))
    before, after = sides(place()[0], mate[part], cross[part])
    return jnp.concatenate([before, own[part], after], axis=0)


def basis(own, mate, cross):
    def window(i):
        return window_of(own, mate, cross, i)

    warmth, voltage, pattern = window(0), window(1), window(2)
    shape = warmth.shape
    inside = rows_inside(shape, ROWS)
    col = lax.broadcasted_iota(jnp.int32, shape, 1)
    last = col == shape[1] - 1
    sigma = inside * jnp.where(pattern == 1.0, copper_factor, 1.0) / (1.0 + sheet_slope * warmth)
    contact = jnp.where(pattern == 2.0, contact_gain, 0.0)
    c_down = 0.5 * (sigma + below(sigma))
    c_right = 0.5 * (sigma + jnp.where(last, 0.0, right(sigma)))
    c_left = jnp.where(col == 0, 0.5 * sigma, left(c_right))
    diagonal = leak_diag + contact + above(c_down) + c_down + c_left + c_right
    diagonal = (diagonal - SHIFT) * (1.0 / SCALE)
    o_down = c_down * inside * below(inside) * (1.0 / SCALE)
    o_up = above(o_down)
    o_right = jnp.where(last, 0.0, c_right) * (1.0 / SCALE)
    o_left = left(o_right)

    def apply(v):
        return diagonal * v - (o_up * above(v) + o_down * below(v)) - (o_left * left(v) + o_right * right(v))

    w0 = contact * voltage
    w1 = apply(w0)
    w2 = 2.0 * apply(w1) - w0
    return (w0, w1, w2), apply, inside, (c_down, c_right, c_left)


def gram_kernel(own, mate, cross, packed_in, packed):
    (w0, w1, w2), apply, _, _ = basis(own, mate, cross)
    w0, w1, w2, w3 = (w[ROWS : 2 * ROWS] for w in (w0, w1, w2, apply(w2)))
    lane = lax.broadcasted_iota(jnp.int32, (1, 128), 1)
    line = jnp.zeros((1, 128), jnp.float32)
    for i, (u, v) in enumerate(((w0, w0), (w0, w1), (w0, w2), (w1, w1), (w1, w2), (w2, w2), (w2, w3))):
        line = jnp.where(lane == i, jnp.sum(u * v, keepdims=True), line)
    for slab in range(packed.shape[0] // BLOCK):
        at = BLOCK * slab
        packed[at : at + 2 * ROWS] = packed_in[at : at + 2 * ROWS]
        packed[at + 2 * ROWS : at + BLOCK] = line


def solve_small(lines):
    total = jnp.sum(lines, axis=0, keepdims=True)
    g00, g01, g02, g11, g12, g22, k22 = (total[:, i : i + 1] for i in range(7))
    gram = ((g00, g01, g02), (g01, g11, g12), (g02, g12, g22))
    k11, k12 = 0.5 * (g12 + g01), 0.5 * (g22 + g02)
    shifted = ((g01, g11, g12), (g11, k11, k12), (g12, k12, k22))
    energy = [[SCALE * shifted[i][j] + SHIFT * gram[i][j] for j in range(3)] for i in range(3)]

    gram, energy = ([[m[i][j] * (1.0 if i == j else 2.0) for j in range(3)] for i in range(3)] for m in (gram, energy))

    def form(m, v):
        return sum(v[i] * sum(v[j] * m[i][j] for j in range(i, len(v))) for i in range(len(v)))

    def ratio(num, den, low, high):
        return jnp.clip(num / jnp.maximum(den, 1e-37), low, high)

    alpha0 = g00 / energy[0][0]
    r = [1.0 - alpha0 * SHIFT, -alpha0 * SCALE]
    rr1 = jnp.maximum(form(gram, r), 0.0)
    beta = ratio(rr1, g00, 0.0, 1e4)
    p = [r[0] + beta, r[1]]
    alpha1 = ratio(rr1, form(energy, p), 0.05, 4.1)
    half = 0.5 * SCALE * p[1]
    image = [half + SHIFT * p[0], SCALE * p[0] + SHIFT * p[1], half]
    x = [alpha0 + alpha1 * p[0], alpha1 * p[1]]
    r = [r[0] - alpha1 * image[0], r[1] - alpha1 * image[1], -alpha1 * image[2]]
    rr2 = jnp.maximum(form(gram, r), 0.0)
    beta = ratio(rr2, rr1, 0.0, 1e4)
    p = [r[0] + beta * p[0], r[1] + beta * p[1], r[2]]
    alpha2 = ratio(rr2, form(energy, p), 0.05, 4.1)
    return x[0] + alpha2 * p[0], x[1] + alpha2 * p[1], alpha2 * p[2]


PAIRS = ((0, 0), (0, 1), (0, 2), (1, 1), (1, 2), (2, 2))
SPAN = ROWS + 2 * HALO
EDGE = 8


def deposit_kernel(layers, own, mate, cross, bins, w0_out, w1_out, w2_out, heats):
    spokes = bins.shape[-1]
    fields, _, inside, (c_down, c_right, c_left) = basis(own, mate, cross)
    for out, w in zip((w0_out, w1_out, w2_out), fields):
        out[...] = w[ROWS : 2 * ROWS]
    shape = inside.shape
    col = lax.broadcasted_iota(jnp.int32, shape, 1)
    last, first = col == shape[1] - 1, col == 0
    fields = [w * inside for w in fields]
    falls = [w - below(w) for w in fields]
    steps = [w - jnp.where(last, 0.0, right(w)) for w in fields]
    wanted = slice(ROWS - HALO, ROWS - HALO + SPAN)
    for pair, (i, j) in enumerate(PAIRS):
        q_down = c_down * (falls[i] * falls[j])
        q_right = c_right * (steps[i] * steps[j])
        q_left = jnp.where(first, c_left * (fields[i] * fields[j]), left(q_right))
        joule = (q_down + above(q_down)) + (q_right + q_left)
        factor = heat_factor if i == j else 2.0 * heat_factor
        joule = factor * joule[wanted]
        for part in range(heats.shape[0]):
            heats[part, SPAN * pair : SPAN * (pair + 1)] = joule[:, 128 * part : 128 * (part + 1)]
    for part in range(heats.shape[0]):
        heats[part, SPAN * len(PAIRS) :] = jnp.zeros((SPAN * (8 - len(PAIRS)), 128), jnp.float32)
    cell = window_of(own, mate, cross, 3)[wanted].astype(jnp.int32)
    azimuth = cell & (spokes - 1)
    outermost = jnp.where(cell >= (layers - 1) * spokes, 1.0, 0.0)
    spoke = lax.broadcasted_iota(jnp.int32, (spokes, shape[1]), 0)
    for row in range(1, SPAN - 1):
        pick = jnp.where(azimuth[row : row + 1] == spoke, 1.0, 0.0).astype(jnp.bfloat16)
        joule = jnp.concatenate([heats[part, pl.ds(row, 8, stride=SPAN), :] for part in range(heats.shape[0])], axis=1)
        upper = joule * outermost[row : row + 1]
        pieces = []
        for part in (joule - upper, upper):
            for _ in range(3):
                piece = part.astype(jnp.bfloat16)
                part = part - piece.astype(jnp.float32)
                pieces.append(piece)
        total = lax.dot_general(
            jnp.concatenate(pieces, axis=0), pick, (((1,), (1,)), ((), ())), preferred_element_type=jnp.float32
        )
        bins[row, 0:8] = total[0:8] + (total[8:16] + total[16:24])
        bins[row, 8:16] = total[24:32] + (total[32:40] + total[40:48])


def substep_rows(rows, layers, warm, cond, base, done):
    body = slice(EDGE, EDGE + layers)
    inward, outward = slice(EDGE - 1, EDGE - 1 + layers), slice(EDGE + 1, EDGE + 1 + layers)

    def conductivity(row):
        t = warm[row, body]
        k = base[row] * (1.0 + diffusivity_derivative * t)
        cond[row, body] = k
        return t, k

    def between(t, k, t_other, k_other):
        return (k + k_other) * (t_other - t)

    below_row = conductivity(rows[0] - 1)
    here = conductivity(rows[0])
    inner = between(*below_row, *here)
    for row in rows:
        t, k = here
        here = conductivity(row + 1)
        outer = between(t, k, *here)
        flux = outer - inner
        inner = outer
        flux = flux + between(t, k, warm[row, inward], cond[row, inward])
        flux = flux + between(t, k, warm[row, outward], cond[row, outward])
        face = between(t, k, right(t), right(k))
        done(row, t, flux + (face - left(face)))


def clear_edges(layers, *fields):
    for field in fields:
        blank = jnp.zeros((EDGE, field.shape[-1]), jnp.float32)
        field[0:EDGE] = blank
        field[EDGE + layers : 2 * EDGE + layers] = blank


def share_kernel(layers, own, lines, for_cross, for_mate):
    mine = own[pl.ds(2 * ROWS, layers, stride=BLOCK), :]
    lines[...] = jnp.broadcast_to(jnp.sum(mine, axis=0, keepdims=True), lines.shape)
    even = place()[0] % 2 == 0
    for layer in range(layers):
        at = BLOCK * layer

        def rows_from(first):
            return jnp.concatenate([own[at + i + first : at + i + first + HALO] for i in (0, ROWS)], axis=0)

        early, late = rows_from(0), rows_from(ROWS - HALO)
        part = slice(2 * HALO * layer, 2 * HALO * (layer + 1))
        for_mate[part] = jnp.where(even, late, early)
        for_cross[part] = jnp.where(even, early, late)


def first_kernel(layers, own, edge, cross, mate, fresh, base, store, warm, cond):
    block = own.shape[0] // layers
    index, count = place()
    body = slice(EDGE, EDGE + layers)
    for row in range(SPAN):

        def rows_of(array):
            if HALO <= row < HALO + ROWS:
                return own[pl.ds(ROWS * array + row - HALO, layers, stride=block), :]
            at = HALO * array + row % HALO
            near = sides(index, *(ref[pl.ds(at, layers, stride=2 * HALO), :] for ref in (mate, cross)))[int(row >= HALO)]
            at = ROWS * array + (row + ROWS - HALO if row < HALO else row - HALO - ROWS)
            last = lax.axis_index("slab") == (0 if row < HALO else layers - 1)
            return jnp.where(last, edge[pl.ds(at, layers, stride=block), :], near)

        there = 1.0
        if row < HALO:
            there = jnp.where(index > 0, 1.0, 0.0)
        elif row >= HALO + ROWS:
            there = jnp.where(index < count - 1, 1.0, 0.0)
        kind = rows_of(1)

        def table(values):
            return jnp.where(kind == 0.0, values[0], jnp.where(kind == 1.0, values[1], jnp.where(kind == 2.0, values[2], values[3])))

        base[row] = table(conduct_table) * there
        store[row] = table([0.5 * time_step / c for c in capacity_table]) * there
        warm[row, body] = rows_of(0)
        clear_edges(layers, warm.at[row], cond.at[row], fresh.at[row])

    def done(row, t, flux):
        fresh[row, body] = t + store[row] * flux

    substep_rows(range(1, SPAN - 1), layers, warm, cond, base, done)


def heat_kernel(layers, lines, w0, w1, w2, bins, fresh, base, store, potential_out, heated, warm, cond, potential, sem):
    spokes = heated.shape[-1]
    body = slice(EDGE, EDGE + layers)
    f = solve_small(lines[pl.ds(0, lines.shape[0] // COPIES, stride=COPIES), :])
    potential[...] = f[0] * w0[...] + f[1] * w1[...] + f[2] * w2[...]
    leaving = pltpu.make_async_copy(potential, potential_out, sem)
    leaving.start()
    sublane = lax.broadcasted_iota(jnp.int32, (8, spokes), 0)
    weight = jnp.zeros((8, spokes), jnp.float32)
    for pair, (i, j) in enumerate(PAIRS):
        weight = jnp.where(sublane == pair, f[i] * f[j], weight)
    weight = 2.0 * weight
    heat = {}
    top = slice(layers - 8, layers)
    for row in range(1, SPAN - 1):
        inner = jnp.sum(weight * bins[row, 0:8], axis=0, keepdims=True)
        outer = jnp.sum(weight * bins[row, 8:16], axis=0, keepdims=True)
        heat[row] = jnp.where(sublane == 6, inner, jnp.where(sublane == 7, outer, 0.0))
        warm[1, row] = fresh[row]
        warm[1, row, EDGE + layers - 8 : EDGE + layers] = fresh[row, EDGE + layers - 8 : EDGE + layers] + store[row, top] * heat[row]
        clear_edges(layers, warm.at[0, row], cond.at[row])

    for substep in range(1, SUBSTEPS):

        def done(row, t, flux):
            flux = jnp.concatenate([flux[: layers - 8], flux[top] + heat[row]], axis=0)
            t = t + store[row] * flux
            if substep + 1 < SUBSTEPS:
                warm[1 - substep % 2, row, body] = t
            else:
                heated[pl.ds(row - HALO, layers, stride=ROWS), :] = t

        substep_rows(range(substep + 1, SPAN - 1 - substep), layers, warm.at[substep % 2], cond, base, done)
    leaving.wait()


def local(foil_warmth, terminal_voltage_input, foil_segment_pattern, underlying_block_map, prior_block_warmth, substance_kind):
    f32 = jnp.float32
    magnets, layers = lax.axis_size("magnet"), lax.axis_size("slab")
    count = magnets * layers
    width, spokes = foil_warmth.shape[1], prior_block_warmth.shape[2]
    mates = [(i, i + 1) for i in range(0, count, 2)]
    crossing = [(i, i + 1) for i in range(1, count - 1, 2)]
    ends = [pair for pair in crossing if pair[1] % layers == 0]
    inner = [pair for pair in crossing if pair[1] % layers]

    def swap(array, pairs):
        return lax.ppermute(array, BOTH, pairs + [(j, i) for i, j in pairs])

    def call(kernel, name, shapes, *operands, scratch=(), spaces=None, outs=None, cost=None, room=8 << 20):
        return pl.pallas_call(
            kernel,
            out_shape=tuple(jax.ShapeDtypeStruct(dims, f32) for dims in shapes),
            in_specs=[pl.BlockSpec(memory_space=spaces or pltpu.VMEM)] * len(operands),
            out_specs=tuple(pl.BlockSpec(memory_space=space) for space in outs or (pltpu.VMEM,) * len(shapes)),
            scratch_shapes=scratch,
            cost_estimate=cost,
            compiler_params=pltpu.CompilerParams(vmem_limit_bytes=room),
            name=name,
        )(*operands)

    rows = (ROWS, width)
    (sheet,) = call(
        sheet_kernel,
        "sheet",
        [(4 * ROWS, width)],
        foil_warmth,
        terminal_voltage_input,
        foil_segment_pattern,
        underlying_block_map,
        scratch=[pltpu.VMEM(rows, jnp.int32), pltpu.VMEM(rows, jnp.int32), pltpu.SemaphoreType.DMA((4,))],
        spaces=pltpu.HBM,
        room=66846720,
    )
    across = swap(sheet, crossing)
    around = (swap(sheet, mates), across)
    stack = (layers * BLOCK, spokes)
    (packed,) = call(
        pack_kernel, "pack", [stack], prior_block_warmth.reshape(-1, spokes), substance_kind.reshape(-1, spokes)
    )
    (packed,) = call(gram_kernel, "gram", [stack], sheet, *around, packed)

    bricks = lax.all_to_all(packed.reshape(layers, BLOCK, 1, spokes), "slab", 0, 0)
    bins, *fields = call(
        functools.partial(deposit_kernel, layers),
        "deposit",
        [(SPAN, 16, spokes), rows, rows, rows],
        sheet,
        *around,
        scratch=[pltpu.VMEM((width // 128, 8 * SPAN, 128), f32)],
        cost=pl.CostEstimate(flops=10**8, bytes_accessed=2 * 10**6, transcendentals=0),
    )
    bricks, bins = lax.optimization_barrier((bricks.reshape(stack), bins))
    lines, over, beside = call(
        functools.partial(share_kernel, layers),
        "share",
        [(magnets * COPIES, spokes)] + [(2 * HALO * layers, spokes)] * 2,
        bricks,
    )
    lines = lax.all_to_all(lines.reshape(magnets, COPIES, spokes), "magnet", 0, 0).reshape(magnets * COPIES, spokes)

    padded = (SPAN, layers + 2 * EDGE, spokes)
    plain = (SPAN, layers, spokes)
    stage = call(
        functools.partial(first_kernel, layers),
        "first",
        [padded, plain, plain],
        bricks,
        swap(bricks, ends),
        swap(over, inner),
        swap(beside, mates),
        scratch=[pltpu.VMEM(padded, f32), pltpu.VMEM(padded, f32)],
        cost=pl.CostEstimate(flops=0, bytes_accessed=0, transcendentals=0),
    )
    potential, heated = call(
        functools.partial(heat_kernel, layers),
        "heat",
        [rows, (layers * ROWS, spokes)],
        lines,
        *fields,
        bins,
        *stage,
        outs=(pltpu.HBM, pltpu.VMEM),
        scratch=[
            pltpu.VMEM((2,) + padded, f32),
            pltpu.VMEM(padded, f32),
            pltpu.VMEM(rows, f32),
            pltpu.SemaphoreType.DMA(()),
        ],
    )
    heated = lax.all_to_all(heated.reshape(layers, ROWS, spokes), "slab", 0, 0)
    return potential, heated.reshape(prior_block_warmth.shape)


def solution(mesh):
    placed = (
        P(("magnet", "slab"), None),
        P(("magnet", "slab"), None),
        P(("magnet", "slab"), None),
        P("magnet", None),
        P("slab", "magnet", None),
        P("slab", "magnet", None),
    )
    return jax.shard_map(
        local,
        mesh=mesh,
        in_specs=placed,
        out_specs=(P(("magnet", "slab"), None), P("slab", "magnet", None)),
        check_vma=False,
    )
```
